256 devices in a mesh: section: 2 (over z_hi), dp: 16 (over z_lo, y), tensor: 8 (over x, core).
Axes of the slice: x: 4, y: 4, z: 8 (z_hi: 2, z_lo: 4; z = z_hi * 4 + z_lo), core: 2. Of those that a mesh axis runs over, the one named last changes fastest.
Arguments:
- section_input: bfloat16 [2, 1024, 8192], P('section', 'tensor', 'dp'), may hold values from -40 to 40
- norm_gain_attn: bfloat16 [2, 8192], P('section', 'dp'), may hold values from 0.099609375 to 1.8984375
- w_query: bfloat16 [2, 8192, 4096], P('section', 'dp', 'tensor'), may hold values from -0.0625 to 0.0625
- key_value_weight: bfloat16 [2, 2, 8192, 512], P('section', None, 'dp'), may hold values from -0.0625 to 0.0625
- w_output: bfloat16 [2, 4096, 8192], P('section', 'tensor', 'dp'), may hold values from -0.09375 to 0.09375
- norm_gain_ffn: bfloat16 [2, 8192], P('section', 'dp'), may hold values from 0.099609375 to 1.8984375
- w_gate_up: bfloat16 [2, 2, 8192, 14336], P('section', None, 'dp', 'tensor'), may hold values from -0.0625 to 0.0625
- w_down: bfloat16 [2, 14336, 8192], P('section', 'tensor', 'dp'), may hold values from -0.046875 to 0.046875
Outputs:
- section_output: bfloat16 [2, 1024, 8192], P('section', 'tensor', 'dp')
The draws below stay inside these ranges and needn't reach their ends.
All inputs are finite; a program needn't handle non-finite values.
Results may differ from the reference program's by a relative error of at most 0.019.
Values may be sent and summed in bfloat16 or wider, within the bound.
A program may use at most 64 MiB of HBM per device.

```python
import math
import jax
import jax.numpy as jnp
from jax import lax

MODEL_WIDTH = 8192
HEAD_SIZE = 128
QUERY_HEADS = 32
KEY_VALUE_HEADS = 4
FF = 14336
TOKENS_PER_BATCH = 1024
QUERY_PER_KEY = 8
N_DP = 16
N_TENSOR = 8


def draw_section_input(key, part):
    noise_key = jax.random.fold_in(key, 11)
    rough_key = jax.random.fold_in(key, 12)
    shape = (2, TOKENS_PER_BATCH, MODEL_WIDTH)
    column = jnp.arange(MODEL_WIDTH, dtype=jnp.float32) / MODEL_WIDTH
    rough = jax.random.uniform(rough_key, (MODEL_WIDTH,), jnp.float32, 0.7, 1.4)
    noise = jnp.clip(jax.random.normal(noise_key, shape, jnp.float32), -6.0, 6.0)
    scale = 0.5 * jnp.exp(column * jnp.log(8.0)) * rough
    values = noise * scale[None, None, :]
    return jnp.clip(values, -40.0, 40.0).astype(jnp.bfloat16)


def block_levels(own_key, extent, split, least, largest):
    factor_of = 1.0
    for dim, shards_of in split:
        heights = jax.random.uniform(jax.random.fold_in(jax.random.fold_in(own_key, 6), dim), (shards_of,), jnp.float32, least / len(split), largest / len(split))
        factor_of = factor_of * jnp.repeat(jnp.exp(heights), extent[dim] // shards_of).reshape((-1,) + (1,) * (len(extent) - 1 - dim))
    return factor_of


def centred(stream_key, dims, deviation, reach, shards=(), kind=jnp.bfloat16):
    factor_of = block_levels(stream_key, dims, shards, -0.22, 0.18) if shards else 1.0
    result = jax.random.normal(stream_key, dims, jnp.float32) * deviation * factor_of
    return jnp.minimum(jnp.maximum(result, -reach), reach).astype(kind)


def setup_inputs(seed: int = 0) -> dict:
    seeds = jax.random.split(jax.random.key(seed), 9)
    section_input = draw_section_input(jax.random.fold_in(seeds[8], 71), 0)
    norm_gain_attn = jnp.clip(1.0 + 0.18 * jax.random.normal(seeds[1], (2, MODEL_WIDTH), jnp.float32), 0.099609375, 1.8984375).astype(jnp.bfloat16)
    w_query = centred(seeds[2], (2, MODEL_WIDTH, QUERY_HEADS * HEAD_SIZE), MODEL_WIDTH ** -0.5, 0.0625, ((0, 2), (1, 16), (2, 8)))
    key_value_weight = centred(seeds[3], (2, 2, MODEL_WIDTH, KEY_VALUE_HEADS * HEAD_SIZE), MODEL_WIDTH ** -0.5, 0.0625, ((0, 2), (2, 16)))
    w_output = centred(seeds[4], (2, QUERY_HEADS * HEAD_SIZE, MODEL_WIDTH), (QUERY_HEADS * HEAD_SIZE) ** -0.5, 0.09375, ((0, 2), (1, 8), (2, 16)))
    norm_gain_ffn = jnp.clip(1.0 + 0.18 * jax.random.normal(seeds[5], (2, MODEL_WIDTH), jnp.float32), 0.099609375, 1.8984375).astype(jnp.bfloat16)
    w_gate_up = centred(seeds[6], (2, 2, MODEL_WIDTH, FF), MODEL_WIDTH ** -0.5, 0.0625, ((0, 2), (2, 16), (3, 8)))
    w_down = centred(seeds[7], (2, FF, MODEL_WIDTH), FF ** -0.5, 0.046875, ((0, 2), (1, 8), (2, 16)))
    return dict(section_input=section_input, norm_gain_attn=norm_gain_attn, w_query=w_query, key_value_weight=key_value_weight, w_output=w_output, norm_gain_ffn=norm_gain_ffn, w_gate_up=w_gate_up, w_down=w_down)


EPS = 1e-05
THETA = 500000.0

def apply_rotary(value_states, token_positions):
    width = value_states.shape[-1]
    half = width // 2
    freqs = jnp.exp(-(2.0 * jnp.arange(half, dtype=jnp.float32) / width) * math.log(THETA))
    angles = token_positions.astype(jnp.float32)[:, None] * freqs[None, :]
    cosine = jnp.cos(angles)[:, None, :]
    sine = jnp.sin(angles)[:, None, :]
    first = value_states[..., :half]
    second = value_states[..., half:]
    return jnp.concatenate([first * cosine - second * sine, second * cosine + first * sine], axis=-1)

def rms_norm(rows, gain):
    wide = rows.astype(jnp.float32)
    meansq = lax.optimization_barrier(jnp.mean(wide * wide, axis=-1, keepdims=True))
    return (wide * lax.rsqrt(meansq + EPS) * gain.astype(jnp.float32)[None, :]).astype(jnp.bfloat16)

def divided_product(left, right, blocks):
    inner = left.shape[1] // blocks

    def add_block(total, index):
        start = (index * inner).astype(jnp.int32)
        piece_left = lax.dynamic_slice_in_dim(left, start, inner, 1)
        piece_right = lax.dynamic_slice_in_dim(right, start, inner, 0)
        partial_value = jnp.dot(piece_left, piece_right, preferred_element_type=jnp.float32)
        rounded = lax.optimization_barrier(partial_value.astype(jnp.bfloat16))
        return (total + rounded.astype(jnp.float32), None)
    start_total = jnp.zeros((left.shape[0], right.shape[1]), jnp.float32)
    total, unused = lax.scan(add_block, start_total, jnp.arange(blocks, dtype=jnp.int32))
    return total

def layer(tokens, gain_attn, w_query, key_value_weight, w_output, gain_ffn, w_gate_up, w_down):
    token_positions = jnp.arange(TOKENS_PER_BATCH, dtype=jnp.int32)
    normed_input = rms_norm(tokens, gain_attn)
    query_unrotated = divided_product(normed_input, w_query, N_DP).reshape(TOKENS_PER_BATCH, QUERY_HEADS, HEAD_SIZE)
    key_unrotated = divided_product(normed_input, key_value_weight[0], N_DP).reshape(TOKENS_PER_BATCH, KEY_VALUE_HEADS, HEAD_SIZE)
    value_states = divided_product(normed_input, key_value_weight[1], N_DP).astype(jnp.bfloat16).reshape(TOKENS_PER_BATCH, KEY_VALUE_HEADS, HEAD_SIZE)
    query_states = apply_rotary(query_unrotated, token_positions).astype(jnp.bfloat16).reshape(TOKENS_PER_BATCH, KEY_VALUE_HEADS, QUERY_PER_KEY, HEAD_SIZE)
    keys = apply_rotary(key_unrotated, token_positions).astype(jnp.bfloat16)
    scores = jnp.einsum('qkgd,skd->kgqs', query_states.astype(jnp.float32), keys.astype(jnp.float32)) * HEAD_SIZE ** (-0.5)
    visible = token_positions[None, :] <= token_positions[:, None]
    weights_exp = jnp.where(visible, jnp.exp(scores), 0.0)
    probs = (weights_exp / lax.optimization_barrier(jnp.sum(weights_exp, axis=-1, keepdims=True))).astype(jnp.bfloat16)
    mixed = jnp.einsum('kgqs,skd->qkgd', probs.astype(jnp.float32), value_states.astype(jnp.float32)).astype(jnp.bfloat16).reshape(TOKENS_PER_BATCH, QUERY_HEADS * HEAD_SIZE)
    attn = divided_product(mixed, w_output, N_TENSOR)
    resid = (tokens.astype(jnp.float32) + attn).astype(jnp.bfloat16)
    normed_ffn = rms_norm(resid, gain_ffn)
    gate = divided_product(normed_ffn, w_gate_up[0], N_DP)
    upper = divided_product(normed_ffn, w_gate_up[1], N_DP)
    hidden = (jax.nn.silu(gate) * upper).astype(jnp.bfloat16)
    ffn = divided_product(hidden, w_down, N_TENSOR)
    return (resid.astype(jnp.float32) + ffn).astype(jnp.bfloat16)

def reference(section_input, norm_gain_attn, w_query, key_value_weight, w_output, norm_gain_ffn, w_gate_up, w_down):
    results = []
    for section in range(2):
        results.append(layer(section_input[1 - section], norm_gain_attn[section], w_query[section], key_value_weight[section], w_output[section], norm_gain_ffn[section], w_gate_up[section], w_down[section]))
    return jnp.stack(results, axis=0)
```

```python
import functools
import math

import jax
import jax.numpy as jnp
import numpy as np
from jax import lax
from jax.experimental import pallas as pl
from jax.experimental.pallas import tpu as pltpu
from jax.sharding import PartitionSpec as P

HEAD = 128
EPS = 1e-05
THETA = 500000.0
RING = 4
ROWS = 64
GROUP = RING * ROWS
WIDTH = 8192
CHUNK = 256

MESH_ID = pl.DeviceIdType.MESH
BF = jnp.bfloat16
F32 = jnp.float32


class Place:
    def __init__(self):
        self.section = lax.axis_index("section")
        dp = lax.axis_index("dp")
        tensor = lax.axis_index("tensor")
        self.dp = dp
        self.z, self.y = lax.div(dp, RING), lax.rem(dp, RING)
        self.x, self.core = lax.div(tensor, 2), lax.rem(tensor, 2)

    def yi(self, k):
        return lax.rem(self.y + k, RING)

    def zi(self, k):
        return lax.rem(self.z + k, RING)

    def xi(self, k):
        return lax.rem(self.x + k, RING)

    def ydev(self, k):
        return {"dp": self.z * RING + self.yi(k)}

    def zdev(self, k):
        return {"dp": self.zi(k) * RING + self.y}

    def xdev(self, k):
        return {"tensor": self.xi(k) * 2 + self.core}

    def sibling(self):
        return {"tensor": self.x * 2 + 1 - self.core}

    def across(self):
        return {"section": 1 - self.section}


def enter(devices):
    barrier = pltpu.get_barrier_semaphore()
    for device in devices:
        pl.semaphore_signal(barrier, inc=1, device_id=device, device_id_type=MESH_ID)
    pl.semaphore_wait(barrier, len(devices))


def send(src, dst, sems, index, device):
    return pltpu.make_async_remote_copy(
        src_ref=src,
        dst_ref=dst,
        send_sem=sems[0].at[index],
        recv_sem=sems[1].at[index],
        device_id=device,
        device_id_type=MESH_ID,
    )


def gather_x(at, tokens, sems):
    def block(xx):
        return tokens.at[pl.ds(2 * at.core, 2), pl.ds(xx * ROWS, ROWS)]

    def half(xx, h):
        return tokens.at[2 * at.core + h, pl.ds(xx * ROWS, ROWS)]

    right, left, far = at.xi(1), at.xi(3), at.xi(2)
    go_right = send(block(at.x), block(at.x), sems, 0, at.xdev(1))
    go_left = send(block(at.x), block(at.x), sems, 1, at.xdev(3))
    share = send(block(at.x), block(at.x), sems, 2, at.sibling())
    go_right.start()
    go_left.start()
    share.start()
    go_right.wait_recv()
    pass_right = send(half(left, 0), half(left, 0), sems, 3, at.xdev(1))
    share_left = send(block(left), block(left), sems, 4, at.sibling())
    pass_right.start()
    share_left.start()
    go_left.wait_recv()
    pass_left = send(half(right, 1), half(right, 1), sems, 5, at.xdev(3))
    share_right = send(block(right), block(right), sems, 6, at.sibling())
    pass_left.start()
    share_right.start()
    pass_right.wait_recv()
    pass_left.wait_recv()
    share_far = send(block(far), block(far), sems, 7, at.sibling())
    share_far.start()
    share.wait_recv()
    share_left.wait_recv()
    share_right.wait_recv()
    share_far.wait_recv()
    return [go_right, go_left, share, pass_right, share_left, pass_left, share_right, share_far]


def scatter_x(at, part, pair, total, first, second, sems):
    mine, other = 2 * at.core, 2 * (1 - at.core)
    right, left, far = at.xi(1), at.xi(3), at.xi(2)

    def rows(xx):
        return pl.ds(xx * ROWS, ROWS)

    shares = []
    for i, xx in enumerate((far, right, left, at.x)):
        shares.append(
            send(part.at[pl.ds(other, 2), rows(xx)], pair.at[:, rows(xx)], sems, i, at.sibling())
        )
        shares[-1].start()

    def summed(i, xx):
        shares[i].wait_recv()
        return part[pl.ds(mine, 2), rows(xx)].astype(F32) + pair[:, rows(xx)].astype(F32)

    total[:, rows(far)] = summed(0, far).astype(BF)
    one_right = send(total.at[0, rows(far)], first.at[0], sems, 4, at.xdev(1))
    one_left = send(total.at[1, rows(far)], first.at[1], sems, 5, at.xdev(3))
    one_right.start()
    one_left.start()
    to_right = summed(1, right)
    one_right.wait_recv()
    total[0, rows(right)] = (to_right[0] + first[0].astype(F32)).astype(BF)
    total[1, rows(right)] = to_right[1].astype(BF)
    two_right = send(total.at[:, rows(right)], second.at[0], sems, 6, at.xdev(1))
    two_right.start()
    to_left = summed(2, left)
    one_left.wait_recv()
    total[0, rows(left)] = to_left[0].astype(BF)
    total[1, rows(left)] = (to_left[1] + first[1].astype(F32)).astype(BF)
    two_left = send(total.at[:, rows(left)], second.at[1], sems, 7, at.xdev(3))
    two_left.start()
    own = summed(3, at.x)
    two_right.wait_recv()
    two_left.wait_recv()
    tile = own + second[0].astype(F32) + second[1].astype(F32)
    return tile, shares + [one_right, one_left, two_right, two_left]


class Reduce:
    def __init__(self, at, part, first, second, third, sems_one, sems_two, sems_three):
        self.at = at
        self.part, self.first, self.second, self.third = part, first, second, third
        self.sems_one, self.sems_two, self.sems_three = sems_one, sems_two, sems_three

    def ones(self, c):
        far = self.at.yi(2)
        low, high = pl.ds(0, GROUP // 2), pl.ds(GROUP // 2, GROUP // 2)
        return (
            send(self.part.at[c, far, low], self.first.at[c, 0], self.sems_one, (c, 0), self.at.ydev(1)),
            send(self.part.at[c, far, high], self.first.at[c, 1], self.sems_one, (c, 1), self.at.ydev(3)),
        )

    def twos(self, c):
        return (
            send(self.part.at[c, self.at.yi(1)], self.second.at[c, 0], self.sems_two, (c, 0), self.at.ydev(1)),
            send(self.part.at[c, self.at.yi(3)], self.second.at[c, 1], self.sems_two, (c, 1), self.at.ydev(3)),
        )

    def threes(self, c):
        return [
            send(
                self.part.at[c, self.at.y, pl.ds(self.at.zi(k) * ROWS, ROWS)],
                self.third.at[c, k - 1],
                self.sems_three,
                (c, k - 1),
                self.at.zdev(k),
            )
            for k in (2, 1, 3)
        ]

    def far(self, c, product):
        self.part[c, self.at.yi(2)] = product(c, self.at.yi(2)).astype(BF)
        for copy in self.ones(c):
            copy.start()

    def near(self, c, product):
        half = GROUP // 2
        one, two = self.ones(c), self.twos(c)
        right, left = self.at.yi(1), self.at.yi(3)
        value = product(c, right)
        one[0].wait_recv()
        self.part[c, right, 0:half] = (value[:half] + self.first[c, 0].astype(F32)).astype(BF)
        self.part[c, right, half:GROUP] = value[half:].astype(BF)
        two[0].start()
        value = product(c, left)
        one[1].wait_recv()
        self.part[c, left, 0:half] = value[:half].astype(BF)
        self.part[c, left, half:GROUP] = (value[half:] + self.first[c, 1].astype(F32)).astype(BF)
        two[1].start()

    def own(self, c, product):
        value = product(c, self.at.y)
        two = self.twos(c)
        two[0].wait_recv()
        two[1].wait_recv()
        self.part[c, self.at.y] = (
            value + self.second[c, 0].astype(F32) + self.second[c, 1].astype(F32)
        ).astype(BF)
        for copy in self.threes(c):
            copy.start()

    def result(self, c):
        for copy in self.threes(c):
            copy.wait_recv()
        total = self.part[c, self.at.y, pl.ds(self.at.z * ROWS, ROWS)].astype(F32)
        for k in range(3):
            total = total + self.third[c, k].astype(F32)
        return total

    def drain(self, c):
        for copy in (*self.ones(c), *self.twos(c), *self.threes(c)):
            copy.wait_send()


class Gather:
    def __init__(self, at, whole, sems_line, sems_ring, sems_pass):
        self.at, self.whole = at, whole
        self.sems_line, self.sems_ring, self.sems_pass = sems_line, sems_ring, sems_pass

    def mine(self, c):
        return self.whole.at[c, self.at.y, pl.ds(self.at.z * ROWS, ROWS)]

    def lines(self, c):
        return [
            send(self.mine(c), self.mine(c), self.sems_line, (c, k - 1), self.at.zdev(k))
            for k in (2, 1, 3)
        ]

    def rings(self, c):
        block = self.whole.at[c, self.at.y]
        return [
            send(block, block, self.sems_ring, (c, 0), self.at.ydev(1)),
            send(block, block, self.sems_ring, (c, 1), self.at.ydev(3)),
        ]

    def passes(self, c):
        low = self.whole.at[c, self.at.yi(3), pl.ds(0, GROUP // 2)]
        high = self.whole.at[c, self.at.yi(1), pl.ds(GROUP // 2, GROUP // 2)]
        return [
            send(low, low, self.sems_pass, (c, 0), self.at.ydev(1)),
            send(high, high, self.sems_pass, (c, 1), self.at.ydev(3)),
        ]

    def line(self, c):
        for copy in self.lines(c):
            copy.start()

    def ring(self, c):
        for copy in self.lines(c):
            copy.wait_recv()
        for copy in self.rings(c):
            copy.start()

    def hand_on(self, c):
        for ring, onward in zip(self.rings(c), self.passes(c)):
            ring.wait_recv()
            onward.start()

    def finish(self, c):
        for copy in self.passes(c):
            copy.wait_recv()

    def drain(self, c):
        for copy in (*self.lines(c), *self.rings(c), *self.passes(c)):
            copy.wait_send()


class Squares:
    def __init__(self, at, part, near, mid, far, sems_y, sems_z):
        self.at, self.part, self.near, self.mid, self.far = at, part, near, mid, far
        self.sems_y, self.sems_z = sems_y, sems_z

    def fill(self, yy, wide):
        squared = (wide * wide).astype(BF)
        self.part[yy] = lax.dot_general(
            jnp.ones((8, wide.shape[1]), BF),
            squared,
            (((1,), (1,)), ((), ())),
            preferred_element_type=F32,
        )

    def ys(self):
        return [
            send(self.part.at[self.at.yi(k)], self.near.at[k - 1], self.sems_y, k - 1, self.at.ydev(k))
            for k in (1, 2, 3)
        ]

    def zs(self):
        return [
            send(self.mid, self.far.at[k - 1], self.sems_z, k - 1, self.at.zdev(k)) for k in (1, 2, 3)
        ]

    def start(self):
        for copy in self.ys():
            copy.start()

    def middle(self):
        for copy in self.ys():
            copy.wait_recv()
        self.mid[...] = self.part[self.at.y] + self.near[0] + self.near[1] + self.near[2]
        for copy in self.zs():
            copy.start()

    def scale(self):
        for copy in self.zs():
            copy.wait_recv()
        total = self.mid[...] + self.far[0] + self.far[1] + self.far[2]
        line = lax.rsqrt(total / WIDTH + EPS)[0:1]
        row = lax.broadcasted_iota(jnp.int32, (ROWS, GROUP), 0)
        lane = lax.broadcasted_iota(jnp.int32, (ROWS, GROUP), 1)
        picked = jnp.where(lane == row + self.at.z * ROWS, jnp.broadcast_to(line, (ROWS, GROUP)), 0.0)
        return jnp.sum(picked, axis=1, keepdims=True)

    def drain(self):
        for copy in (*self.ys(), *self.zs()):
            copy.wait_send()


def scaled(tokens, gain, out, squares, yy):
    wide = tokens[yy].astype(F32)
    squares.fill(yy, wide)
    out[yy] = (wide * gain).astype(BF)


def attend(
    src, gain_ref, wq_hbm, wkv_hbm, wo_hbm, table, out,
    tokens, normed, wq, wkv, wo,
    q_part, q_one, q_two, q_three, k_part, k_one, k_two, k_three,
    ss_part, ss_near, ss_mid, ss_far,
    keys, mixed, scores, part, pair, total, first, second,
    local, swap_s, swap_r, gx_s, gx_r, sx_s, sx_r, y_s, y_r, z_s, z_r,
    q1_s, q1_r, q2_s, q2_r, q3_s, q3_r, k1_s, k1_r, k2_s, k2_r, k3_s, k3_r,
    kl_s, kl_r, kr_s, kr_r, kp_s, kp_r, kc_s, kc_r, ml_s, ml_r, mr_s, mr_r, mp_s, mp_r,
):
    at = Place()
    loads = [
        pltpu.make_async_copy(wq_hbm, wq, local.at[0]),
        pltpu.make_async_copy(wkv_hbm.at[at.core, :, pl.ds(at.x * HEAD, HEAD)], wkv, local.at[1]),
        pltpu.make_async_copy(wo_hbm, wo, local.at[2]),
    ]
    for load in loads:
        load.start()
    enter(
        [at.ydev(k) for k in (1, 2, 3)]
        + [at.zdev(k) for k in (1, 2, 3)]
        + [at.xdev(1), at.xdev(3), at.sibling(), at.across()]
    )
    own_tile = tokens.at[pl.ds(2 * at.core, 2), pl.ds(at.x * ROWS, ROWS)]
    swap = send(src, own_tile, (swap_s, swap_r), 0, at.across())
    swap.start()
    gain = gain_ref[...].astype(F32)
    half = HEAD // 2
    lane = lax.broadcasted_iota(jnp.int32, (1, HEAD), 1)
    base = (table[0, pl.ds(ROWS + at.dp, 1), :], table[1, pl.ds(ROWS + at.dp, 1), :])
    step = (table[0, 0:ROWS, :], table[1, 0:ROWS, :])
    cosine = base[0] * step[0] - base[1] * step[1]
    sine = (base[1] * step[0] + base[0] * step[1]) * jnp.where(lane < half, -1.0, 1.0)
    for load in loads:
        load.wait()
    swap.wait_recv()
    pending = [swap] + gather_x(at, tokens, (gx_s, gx_r))

    squares = Squares(at, ss_part, ss_near, ss_mid, ss_far, (y_s, y_r), (z_s, z_r))
    qs = Reduce(at, q_part, q_one, q_two, q_three, (q1_s, q1_r), (q2_s, q2_r), (q3_s, q3_r))
    ks = Reduce(at, k_part, k_one, k_two, k_three, (k1_s, k1_r), (k2_s, k2_r), (k3_s, k3_r))

    def product_q(c, yy):
        return jnp.dot(normed[yy], wq[...], preferred_element_type=F32)

    def product_k(c, yy):
        return jnp.dot(normed[yy], wkv[...], preferred_element_type=F32)

    scaled(tokens, gain, normed, squares, at.yi(2))
    ks.far(0, product_k)
    qs.far(0, product_q)
    scaled(tokens, gain, normed, squares, at.yi(1))
    scaled(tokens, gain, normed, squares, at.yi(3))
    squares.start()
    ks.near(0, product_k)
    scaled(tokens, gain, normed, squares, at.y)
    qs.near(0, product_q)
    squares.middle()
    ks.own(0, product_k)
    scale = squares.scale()

    def rotated(value, cos, sin):
        return value * cos + pltpu.roll(value, half, 1) * sin

    is_key = at.core == 0
    whole = Gather(at, keys, (kl_s, kl_r), (kr_s, kr_r), (kp_s, kp_r))
    core = at.core
    value = ks.result(0) * scale
    keys[core, at.y, pl.ds(at.z * ROWS, ROWS)] = rotated(
        value, jnp.where(is_key, cosine, 1.0), jnp.where(is_key, sine, 0.0)
    ).astype(BF)
    key_sems = ((kl_s, kl_r), (kr_s, kr_r), (kc_s, kc_r))
    mine = keys.at[core, at.y, pl.ds(at.z * ROWS, ROWS)]
    lines = [send(mine, mine, key_sems[0], k - 1, at.zdev(k)) for k in (2, 1, 3)]
    for copy in lines:
        copy.start()
    qs.own(0, product_q)
    for copy in lines:
        copy.wait_recv()
    block = keys.at[core, at.y]
    rings = [send(block, block, key_sems[1], k - 1, at.ydev(k)) for k in (2, 1, 3)]
    shares = [send(block, block, key_sems[2], 0, at.sibling())]
    for copy in rings + shares:
        copy.start()
    for k, ring in zip((2, 1, 3), rings):
        ring.wait_recv()
        came = keys.at[core, at.yi(RING - k)]
        shares.append(send(came, came, key_sems[2], k, at.sibling()))
        shares[-1].start()
    pending += lines + rings + shares

    queries = qs.result(0) * scale
    stacked = jnp.concatenate(
        [rotated(queries[:, h * HEAD : (h + 1) * HEAD], cosine, sine) for h in range(4)], axis=0
    ).astype(BF)
    for copy in shares:
        copy.wait_recv()
    row = lax.broadcasted_iota(jnp.int32, (RING * ROWS, GROUP), 0)
    col = lax.broadcasted_iota(jnp.int32, (RING * ROWS, GROUP), 1)
    query_at = lax.rem(row, ROWS) + at.dp * ROWS
    key_at = lax.div(col, ROWS) * GROUP + lax.rem(col, ROWS)
    weight = jnp.zeros((RING * ROWS, 1), F32)
    for yy in range(RING):
        raw = lax.dot_general(
            stacked, keys[0, yy], (((1,), (1,)), ((), ())), preferred_element_type=F32
        ) * HEAD ** (-0.5)
        kept = jnp.where(key_at + yy * ROWS <= query_at, jnp.exp(raw), 0.0)
        scores[yy] = kept
        weight = weight + jnp.sum(kept, axis=1, keepdims=True)
    mix = jnp.zeros((RING * ROWS, HEAD), F32)
    for yy in range(RING):
        mix = mix + jnp.dot(
            (scores[yy] / weight).astype(BF), keys[1, yy], preferred_element_type=F32
        )
    for h in range(4):
        mixed[0, at.y, pl.ds(at.z * ROWS, ROWS), h * HEAD : (h + 1) * HEAD] = mix[
            h * ROWS : (h + 1) * ROWS
        ].astype(BF)

    heads = Gather(at, mixed, (ml_s, ml_r), (mr_s, mr_r), (mp_s, mp_r))
    heads.line(0)
    heads.ring(0)
    heads.hand_on(0)

    def project(yy):
        part[yy] = jnp.dot(mixed[0, yy], wo[...], preferred_element_type=F32).astype(BF)

    project(at.y)
    project(at.yi(1))
    project(at.yi(3))
    heads.finish(0)
    project(at.yi(2))
    tile, more = scatter_x(at, part, pair, total, first, second, (sx_s, sx_r))
    out[...] = (
        tokens[pl.ds(2 * at.core, 2), pl.ds(at.x * ROWS, ROWS)].astype(F32) + tile
    ).astype(BF)
    for copy in pending + more:
        copy.wait_send()
    squares.drain()
    qs.drain(0)
    ks.drain(0)
    heads.drain(0)


def feed(
    src, gain_ref, wgu_hbm, wd_hbm, out,
    tokens, normed, wgu, wd, h_part, h_one, h_two, h_three,
    ss_part, ss_near, ss_mid, ss_far, hidden, acc, part, pair, total, first, second,
    local, load_s, gx_s, gx_r, sx_s, sx_r, y_s, y_r, z_s, z_r,
    h1_s, h1_r, h2_s, h2_r, h3_s, h3_r, hl_s, hl_r, hr_s, hr_r, hp_s, hp_r,
):
    at = Place()
    chunks = wgu.shape[0]
    own_tile = tokens.at[pl.ds(2 * at.core, 2), pl.ds(at.x * ROWS, ROWS)]
    tile_in = pltpu.make_async_copy(src, own_tile, local.at[0])
    tile_in.start()
    down_in = pltpu.make_async_copy(wd_hbm, wd, local.at[1])
    loads = [
        pltpu.make_async_copy(
            wgu_hbm.at[g, :, pl.ds(c * CHUNK, CHUNK)], wgu.at[c, g], load_s.at[c, g]
        )
        for c in range(chunks)
        for g in range(2)
    ]
    for load in loads:
        load.start()
    down_in.start()
    enter(
        [at.ydev(k) for k in (1, 2, 3)]
        + [at.zdev(k) for k in (1, 2, 3)]
        + [at.xdev(1), at.xdev(3), at.sibling()]
    )
    tile_in.wait()
    gain = gain_ref[...].astype(F32)
    pending = gather_x(at, tokens, (gx_s, gx_r))
    for load in loads:
        load.wait()
    down_in.wait()
    squares = Squares(at, ss_part, ss_near, ss_mid, ss_far, (y_s, y_r), (z_s, z_r))
    hs = Reduce(at, h_part, h_one, h_two, h_three, (h1_s, h1_r), (h2_s, h2_r), (h3_s, h3_r))
    hg = Gather(at, hidden, (hl_s, hl_r), (hr_s, hr_r), (hp_s, hp_r))

    def product(c, yy):
        return jnp.concatenate(
            [jnp.dot(normed[yy], wgu[c, g], preferred_element_type=F32) for g in range(2)], axis=1
        )

    def each(body):
        lax.fori_loop(0, chunks, lambda c, carry: (body(c), carry)[1], 0)

    scaled(tokens, gain, normed, squares, at.yi(2))
    each(lambda c: hs.far(c, product))
    scaled(tokens, gain, normed, squares, at.yi(1))
    scaled(tokens, gain, normed, squares, at.yi(3))
    squares.start()
    scaled(tokens, gain, normed, squares, at.y)
    each(lambda c: hs.near(c, product))
    squares.middle()
    scale = squares.scale()
    each(lambda c: hs.own(c, product))

    def activate(c):
        both = hs.result(c) * scale
        gate, up = both[:, :CHUNK], both[:, CHUNK:]
        hidden[c, at.y, pl.ds(at.z * ROWS, ROWS)] = (gate / (1.0 + jnp.exp(-gate)) * up).astype(BF)
        hg.line(c)

    each(activate)
    each(hg.ring)
    each(hg.hand_on)

    def project(yy):
        acc[...] = jnp.zeros_like(acc)

        def body(c):
            acc[...] += jnp.dot(hidden[c, yy], wd[c], preferred_element_type=F32)

        each(body)
        part[yy] = acc[...].astype(BF)

    project(at.y)
    project(at.yi(1))
    project(at.yi(3))
    each(hg.finish)
    project(at.yi(2))
    tile, more = scatter_x(at, part, pair, total, first, second, (sx_s, sx_r))
    out[...] = (
        tokens[pl.ds(2 * at.core, 2), pl.ds(at.x * ROWS, ROWS)].astype(F32) + tile
    ).astype(BF)
    for copy in pending + more:
        copy.wait_send()
    squares.drain()
    each(hs.drain)
    each(hg.drain)


def pairs(*shapes):
    return [pltpu.SemaphoreType.DMA(shape) for shape in shapes for _ in range(2)]


def reduce_scratch(chunks, columns):
    return [
        pltpu.VMEM((chunks, RING, GROUP, columns), BF),
        pltpu.VMEM((chunks, 2, GROUP // 2, columns), BF),
        pltpu.VMEM((chunks, 2, GROUP, columns), BF),
        pltpu.VMEM((chunks, 3, ROWS, columns), BF),
    ]


def square_scratch():
    return [
        pltpu.VMEM((RING, 8, GROUP), F32),
        pltpu.VMEM((3, 8, GROUP), F32),
        pltpu.VMEM((8, GROUP), F32),
        pltpu.VMEM((3, 8, GROUP), F32),
    ]


def scatter_scratch(columns):
    return [
        pltpu.VMEM((RING, GROUP, columns), BF),
        pltpu.VMEM((2, GROUP, columns), BF),
        pltpu.VMEM((2, GROUP, columns), BF),
        pltpu.VMEM((2, ROWS, columns), BF),
        pltpu.VMEM((2, 2, ROWS, columns), BF),
    ]


def rotary_table(count):
    freq = np.exp(-(2.0 * np.arange(HEAD // 2) / HEAD) * math.log(THETA))
    position = np.concatenate([np.arange(ROWS), np.arange(count) * ROWS]).astype(np.float64)
    angle = position[:, None] * np.concatenate([freq, freq])[None, :]
    return np.stack([np.cos(angle), np.sin(angle)]).astype(np.float32)


def local_layer(
    section_input, gain_attn, w_query, key_value_weight, w_output, gain_ffn, w_gate_up, w_down
):
    cols = section_input.shape[2]
    heads = w_query.shape[2]
    ff = w_gate_up.shape[3]
    chunks = ff // CHUNK
    anywhere = pl.BlockSpec(memory_space=pl.ANY)
    vmem = pl.BlockSpec(memory_space=pltpu.VMEM)
    tile = jax.ShapeDtypeStruct((2, ROWS, cols), BF)
    limit = 60 * 1024 * 1024
    resid = pl.pallas_call(
        attend,
        name="attention_half",
        out_shape=tile,
        in_specs=[anywhere, vmem, anywhere, anywhere, anywhere, vmem],
        out_specs=vmem,
        scratch_shapes=[
            pltpu.VMEM((RING, GROUP, cols), BF),
            pltpu.VMEM((RING, GROUP, cols), BF),
            pltpu.VMEM((cols, heads), BF),
            pltpu.VMEM((cols, HEAD), BF),
            pltpu.VMEM((heads, cols), BF),
            *reduce_scratch(1, heads),
            *reduce_scratch(1, HEAD),
            *square_scratch(),
            pltpu.VMEM((2, RING, GROUP, HEAD), BF),
            pltpu.VMEM((1, RING, GROUP, heads), BF),
            pltpu.VMEM((RING, RING * ROWS, GROUP), F32),
            *scatter_scratch(cols),
            pltpu.SemaphoreType.DMA((3,)),
            *pairs((1,), (8,), (8,), (3,), (3,)),
            *pairs((1, 2), (1, 2), (1, 3), (1, 2), (1, 2), (1, 3)),
            *pairs((3,), (3,), (1,), (4,), (1, 3), (1, 2), (1, 2)),
        ],
        compiler_params=pltpu.CompilerParams(
            collective_id=0, has_side_effects=True, vmem_limit_bytes=limit
        ),
    )(
        section_input.reshape(2, ROWS, cols),
        gain_attn,
        w_query[0],
        key_value_weight[0],
        w_output[0],
        jnp.asarray(rotary_table(RING * RING)),
    )
    result = pl.pallas_call(
        feed,
        name="feed_forward_half",
        out_shape=tile,
        in_specs=[anywhere, vmem, anywhere, anywhere],
        out_specs=vmem,
        scratch_shapes=[
            pltpu.VMEM((RING, GROUP, cols), BF),
            pltpu.VMEM((RING, GROUP, cols), BF),
            pltpu.VMEM((chunks, 2, cols, CHUNK), BF),
            pltpu.VMEM((chunks, CHUNK, cols), BF),
            *reduce_scratch(chunks, 2 * CHUNK),
            *square_scratch(),
            pltpu.VMEM((chunks, RING, GROUP, CHUNK), BF),
            pltpu.VMEM((GROUP, cols), F32),
            *scatter_scratch(cols),
            pltpu.SemaphoreType.DMA((2,)),
            pltpu.SemaphoreType.DMA((chunks, 2)),
            *pairs((8,), (8,), (3,), (3,)),
            *pairs((chunks, 2), (chunks, 2), (chunks, 3)),
            *pairs((chunks, 3), (chunks, 2), (chunks, 2)),
        ],
        compiler_params=pltpu.CompilerParams(
            collective_id=1, has_side_effects=True, vmem_limit_bytes=limit
        ),
    )(resid, gain_ffn, w_gate_up[0], w_down[0].reshape(chunks, CHUNK, cols))
    return result.reshape(1, 2 * ROWS, cols)


def solution(mesh):
    placed = (
        P("section", "tensor", "dp"),
        P("section", "dp"),
        P("section", "dp", "tensor"),
        P("section", None, "dp", None),
        P("section", "tensor", "dp"),
        P("section", "dp"),
        P("section", None, "dp", "tensor"),
        P("section", "tensor", "dp"),
    )
    return jax.shard_map(
        local_layer, mesh=mesh, in_specs=placed, out_specs=P("section", "tensor", "dp"), check_vma=False
    )
```

```python
import functools
import math
import types

import jax
import jax.numpy as jnp
import numpy as np
from jax import lax
from jax.experimental import pallas as pl
from jax.experimental.pallas import tpu as pltpu
from jax.sharding import PartitionSpec as P

HEAD = 128
EPS = 1e-05
THETA = 500000.0
RING = 4
ROWS = 64
GROUP = RING * ROWS
WIDTH = 8192

MESH_ID = pl.DeviceIdType.MESH
BF = jnp.bfloat16
F32 = jnp.float32


class Place:
    def __init__(self):
        self.section = lax.axis_index("section")
        dp = lax.axis_index("dp")
        tensor = lax.axis_index("tensor")
        self.dp = dp
        self.z, self.y = lax.div(dp, RING), lax.rem(dp, RING)
        self.x, self.core = lax.div(tensor, 2), lax.rem(tensor, 2)

    def yi(self, k):
        return lax.rem(self.y + k, RING)

    def zi(self, k):
        return lax.rem(self.z + k, RING)

    def xi(self, k):
        return lax.rem(self.x + k, RING)

    def ydev(self, k):
        return {"dp": self.z * RING + self.yi(k)}

    def zdev(self, k):
        return {"dp": self.zi(k) * RING + self.y}

    def xdev(self, k):
        return {"tensor": self.xi(k) * 2 + self.core}

    def sibling(self):
        return {"tensor": self.x * 2 + 1 - self.core}

    def across(self):
        return {"section": 1 - self.section}


def enter(devices):
    barrier = pltpu.get_barrier_semaphore()
    for device in devices:
        pl.semaphore_signal(barrier, inc=1, device_id=device, device_id_type=MESH_ID)
    pl.semaphore_wait(barrier, len(devices))


def send(src, dst, sems, index, device):
    return pltpu.make_async_remote_copy(
        src_ref=src,
        dst_ref=dst,
        send_sem=sems[0].at[index],
        recv_sem=sems[1].at[index],
        device_id=device,
        device_id_type=MESH_ID,
    )


class Spread:
    def __init__(self, at, tokens, sems):
        self.at = at
        self.right, self.left, self.far = at.xi(1), at.xi(3), at.xi(2)

        def block(xx):
            return tokens.at[pl.ds(2 * at.core, 2), pl.ds(xx * ROWS, ROWS)]

        def half(xx, h):
            return tokens.at[2 * at.core + h, pl.ds(xx * ROWS, ROWS)]

        def same(ref, index, device):
            return send(ref, ref, sems, index, device)

        self.out = [
            same(block(at.x), 0, at.xdev(1)),
            same(block(at.x), 1, at.xdev(3)),
            same(block(at.x), 2, at.sibling()),
        ]
        self.after_left = [
            same(half(self.left, 0), 3, at.xdev(1)),
            same(block(self.left), 4, at.sibling()),
        ]
        self.after_right = [
            same(half(self.right, 1), 5, at.xdev(3)),
            same(block(self.right), 6, at.sibling()),
        ]
        self.last = [same(block(self.far), 7, at.sibling())]

    def start(self):
        for copy in self.out:
            copy.start()

    def onward(self):
        self.out[0].wait_recv()
        for copy in self.after_left:
            copy.start()
        self.out[1].wait_recv()
        for copy in self.after_right:
            copy.start()

    def end(self):
        self.after_left[0].wait_recv()
        self.after_right[0].wait_recv()
        self.last[0].start()

    def finish(self):
        for copy in (self.out[2], self.after_left[1], self.after_right[1], self.last[0]):
            copy.wait_recv()

    def copies(self):
        return [*self.out, *self.after_left, *self.after_right, *self.last]


def scatter_x(at, part, pair, total, first, second, sems):
    mine, other = 2 * at.core, 2 * (1 - at.core)
    right, left, far = at.xi(1), at.xi(3), at.xi(2)

    def rows(xx):
        return pl.ds(xx * ROWS, ROWS)

    shares = []
    for i, xx in enumerate((far, right, left, at.x)):
        shares.append(
            send(part.at[pl.ds(other, 2), rows(xx)], pair.at[:, rows(xx)], sems, i, at.sibling())
        )
        shares[-1].start()

    def summed(i, xx):
        shares[i].wait_recv()
        return part[pl.ds(mine, 2), rows(xx)].astype(F32) + pair[:, rows(xx)].astype(F32)

    total[:, rows(far)] = summed(0, far).astype(BF)
    one_right = send(total.at[0, rows(far)], first.at[0], sems, 4, at.xdev(1))
    one_left = send(total.at[1, rows(far)], first.at[1], sems, 5, at.xdev(3))
    one_right.start()
    one_left.start()
    to_right = summed(1, right)
    one_right.wait_recv()
    total[0, rows(right)] = (to_right[0] + first[0].astype(F32)).astype(BF)
    total[1, rows(right)] = to_right[1].astype(BF)
    two_right = send(total.at[:, rows(right)], second.at[0], sems, 6, at.xdev(1))
    two_right.start()
    to_left = summed(2, left)
    one_left.wait_recv()
    total[0, rows(left)] = to_left[0].astype(BF)
    total[1, rows(left)] = (to_left[1] + first[1].astype(F32)).astype(BF)
    two_left = send(total.at[:, rows(left)], second.at[1], sems, 7, at.xdev(3))
    two_left.start()
    own = summed(3, at.x)
    two_right.wait_recv()
    two_left.wait_recv()
    tile = own + second[0].astype(F32) + second[1].astype(F32)
    return tile, shares + [one_right, one_left, two_right, two_left]


class Reduce:
    def __init__(self, at, part, first, second, third, sems, hand):
        self.at = at
        self.part, self.first, self.second, self.third = part, first, second, third
        self.sems_one, self.sems_two, self.sems_three = sems
        self.hand = hand

    def ones(self, c):
        far = self.at.yi(2)
        low, high = pl.ds(0, GROUP // 2), pl.ds(GROUP // 2, GROUP // 2)
        return (
            send(self.part.at[c, far, low], self.first.at[c, 0], self.sems_one, (c, 0), self.at.ydev(1)),
            send(self.part.at[c, far, high], self.first.at[c, 1], self.sems_one, (c, 1), self.at.ydev(3)),
        )

    def twos(self, c):
        return (
            send(self.part.at[c, self.at.yi(1)], self.second.at[c, 0], self.sems_two, (c, 0), self.at.ydev(1)),
            send(self.part.at[c, self.at.yi(3)], self.second.at[c, 1], self.sems_two, (c, 1), self.at.ydev(3)),
        )

    def threes(self, c):
        return [
            send(
                self.part.at[c, self.at.y, rows], self.third.at[c, slot], self.sems_three, (c, slot), device
            )
            for slot, rows, device in self.hand
        ]

    def far(self, c, product):
        self.part[c, self.at.yi(2)] = product(c, self.at.yi(2)).astype(BF)
        for copy in self.ones(c):
            copy.start()

    def near(self, c, product):
        half = GROUP // 2
        one, two = self.ones(c), self.twos(c)
        right, left = self.at.yi(1), self.at.yi(3)
        value = product(c, right)
        one[0].wait_recv()
        self.part[c, right, 0:half] = (value[:half] + self.first[c, 0].astype(F32)).astype(BF)
        self.part[c, right, half:GROUP] = value[half:].astype(BF)
        two[0].start()
        value = product(c, left)
        one[1].wait_recv()
        self.part[c, left, 0:half] = value[:half].astype(BF)
        self.part[c, left, half:GROUP] = (value[half:] + self.first[c, 1].astype(F32)).astype(BF)
        two[1].start()

    def own(self, c, product):
        value = product(c, self.at.y)
        for copy in self.twos(c):
            copy.wait_recv()
        self.part[c, self.at.y] = (
            value + self.second[c, 0].astype(F32) + self.second[c, 1].astype(F32)
        ).astype(BF)
        for copy in self.threes(c):
            copy.start()

    def result(self, c, rows):
        for copy in self.threes(c):
            copy.wait_recv()
        total = self.part[c, self.at.y, rows].astype(F32)
        for slot, _, _ in self.hand:
            total = total + self.third[c, slot].astype(F32)
        return total

    def drain(self, c):
        for copy in (*self.ones(c), *self.twos(c), *self.threes(c)):
            copy.wait_send()


class Gather:
    def __init__(self, at, mine, block, sems):
        self.at, self.mine, self.block = at, mine, block
        self.sems_line, self.sems_ring, self.sems_pass = sems

    def lines(self, c):
        return [
            send(self.mine(c), self.mine(c), self.sems_line, (c, k - 1), self.at.zdev(k))
            for k in (2, 1, 3)
        ]

    def rings(self, c):
        block = self.block(c, self.at.y, pl.ds(0, GROUP))
        return [
            send(block, block, self.sems_ring, (c, 0), self.at.ydev(1)),
            send(block, block, self.sems_ring, (c, 1), self.at.ydev(3)),
        ]

    def passes(self, c):
        low = self.block(c, self.at.yi(3), pl.ds(0, GROUP // 2))
        high = self.block(c, self.at.yi(1), pl.ds(GROUP // 2, GROUP // 2))
        return [
            send(low, low, self.sems_pass, (c, 0), self.at.ydev(1)),
            send(high, high, self.sems_pass, (c, 1), self.at.ydev(3)),
        ]

    def line(self, c):
        for copy in self.lines(c):
            copy.start()

    def arrived(self, c):
        for copy in self.lines(c):
            copy.wait_recv()

    def ring(self, c):
        for copy in self.rings(c):
            copy.start()

    def hand_on(self, c):
        for ring, onward in zip(self.rings(c), self.passes(c)):
            ring.wait_recv()
            onward.start()

    def finish(self, c):
        for copy in self.passes(c):
            copy.wait_recv()

    def drain(self, c):
        for copy in (*self.lines(c), *self.rings(c), *self.passes(c)):
            copy.wait_send()


class Squares:
    def __init__(self, at, part, near, mid, far, sems_y, sems_z):
        self.at, self.part, self.near, self.mid, self.far = at, part, near, mid, far
        self.sems_y, self.sems_z = sems_y, sems_z

    def fill(self, yy, wide):
        squared = (wide * wide).astype(BF)
        self.part[yy] = lax.dot_general(
            jnp.ones((8, wide.shape[1]), BF),
            squared,
            (((1,), (1,)), ((), ())),
            preferred_element_type=F32,
        )

    def ys(self):
        return [
            send(self.part.at[self.at.yi(k)], self.near.at[k - 1], self.sems_y, k - 1, self.at.ydev(k))
            for k in (1, 2, 3)
        ]

    def zs(self):
        return [
            send(self.mid, self.far.at[k - 1], self.sems_z, k - 1, self.at.zdev(k)) for k in (1, 2, 3)
        ]

    def start(self):
        for copy in self.ys():
            copy.start()

    def middle(self):
        for copy in self.ys():
            copy.wait_recv()
        self.mid[...] = self.part[self.at.y] + self.near[0] + self.near[1] + self.near[2]
        for copy in self.zs():
            copy.start()

    def scale(self, count, start):
        for copy in self.zs():
            copy.wait_recv()
        total = self.mid[...] + self.far[0] + self.far[1] + self.far[2]
        line = lax.rsqrt(total / WIDTH + EPS)[0:1]
        row = lax.broadcasted_iota(jnp.int32, (count, GROUP), 0)
        lane = lax.broadcasted_iota(jnp.int32, (count, GROUP), 1)
        picked = jnp.where(lane == row + start, jnp.broadcast_to(line, (count, GROUP)), 0.0)
        return jnp.sum(picked, axis=1, keepdims=True)

    def drain(self):
        for copy in (*self.ys(), *self.zs()):
            copy.wait_send()


def scaled(tokens, gain, out, squares, yy):
    wide = tokens[yy].astype(F32)
    squares.fill(yy, wide)
    out[yy] = (wide * gain).astype(BF)


def attention(at, m, gain, spread_weights):
    half = HEAD // 2
    lane = lax.broadcasted_iota(jnp.int32, (1, HEAD), 1)
    base = [m.table[i, pl.ds(ROWS + at.dp, 1), :] for i in range(2)]
    step = [m.table[i, 0:ROWS, :] for i in range(2)]
    cosine = base[0] * step[0] - base[1] * step[1]
    sine = (base[1] * step[0] + base[0] * step[1]) * jnp.where(lane < half, -1.0, 1.0)
    spread = Spread(at, m.tokens, m.gx)
    spread.start()
    spread.onward()
    spread.end()
    spread.finish()
    pending = spread.copies()

    squares = Squares(at, m.ss_part, m.ss_near, m.ss_mid, m.ss_far, m.ssy, m.ssz)
    along = [(k - 1, pl.ds(at.zi(k) * ROWS, ROWS), at.zdev(k)) for k in (2, 1, 3)]
    own_rows = pl.ds(at.z * ROWS, ROWS)
    qs = Reduce(at, m.q_part, m.q_one, m.q_two, m.q_three, (m.q1, m.q2, m.q3), along)
    q_chunks = m.q_part.shape[0]
    q_cols = m.q_part.shape[3]

    def product_q(c, yy):
        columns = m.wq[:, c * q_cols : (c + 1) * q_cols]
        return jnp.dot(m.normed[yy], columns, preferred_element_type=F32)

    def product_k(yy):
        return jnp.dot(m.normed[yy], m.wkv[...], preferred_element_type=F32)

    key_y = [
        send(m.k_part.at[at.yi(k)], m.k_near.at[k - 1], m.k1, k - 1, at.ydev(k)) for k in (2, 1, 3)
    ]
    for k, copy in zip((2, 1, 3), key_y):
        scaled(m.tokens, gain, m.normed, squares, at.yi(k))
        m.k_part[at.yi(k)] = product_k(at.yi(k)).astype(BF)
        copy.start()
    squares.start()
    for c in range(q_chunks):
        qs.far(c, product_q)
    scaled(m.tokens, gain, m.normed, squares, at.y)
    total = product_k(at.y)
    for k, copy in zip((2, 1, 3), key_y):
        copy.wait_recv()
        total = total + m.k_near[k - 1].astype(F32)
    m.k_part[at.y] = total.astype(BF)
    key_z = [
        send(m.k_part.at[at.y, rows], m.k_far.at[slot], m.k2, slot, device)
        for slot, rows, device in along
    ]
    for copy in key_z:
        copy.start()
    squares.middle()
    for c in range(q_chunks):
        qs.near(c, product_q)
    scale = squares.scale(ROWS, at.z * ROWS)

    def rotated(value, cos, sin):
        return value * cos + pltpu.roll(value, half, 1) * sin

    is_key = at.core == 0
    core = at.core
    value = m.k_part[at.y, own_rows].astype(F32)
    for slot, copy in zip((1, 0, 2), key_z):
        copy.wait_recv()
        value = value + m.k_far[slot].astype(F32)
    m.keys[core, at.y, own_rows] = rotated(
        value * scale, jnp.where(is_key, cosine, 1.0), jnp.where(is_key, sine, 0.0)
    ).astype(BF)
    mine = m.keys.at[core, at.y, own_rows]
    lines = [send(mine, mine, m.kl, k - 1, at.zdev(k)) for k in (2, 1, 3)]
    for copy in lines:
        copy.start()
    qs.own(0, product_q)
    for copy in lines:
        copy.wait_recv()
    block = m.keys.at[core, at.y]
    rings = [send(block, block, m.kr, k - 1, at.ydev(k)) for k in (2, 1, 3)]
    shares = [send(block, block, m.kc, 0, at.sibling())]
    for copy in rings + shares:
        copy.start()
    for c in range(1, q_chunks):
        qs.own(c, product_q)
    for k, ring in zip((2, 1, 3), rings):
        ring.wait_recv()
        came = m.keys.at[core, at.yi(RING - k)]
        shares.append(send(came, came, m.kc, k, at.sibling()))
        shares[-1].start()
    pending += key_y + key_z + lines + rings + shares

    per = q_cols // HEAD
    pieces = []
    for c in range(q_chunks):
        queries = qs.result(c, own_rows) * scale
        pieces += [rotated(queries[:, h * HEAD : (h + 1) * HEAD], cosine, sine) for h in range(per)]
    stacked = jnp.concatenate(pieces, axis=0).astype(BF)
    spread_weights(1)
    for copy in shares:
        copy.wait_recv()
    row = lax.broadcasted_iota(jnp.int32, (RING * ROWS, GROUP), 0)
    col = lax.broadcasted_iota(jnp.int32, (RING * ROWS, GROUP), 1)
    query_at = lax.rem(row, ROWS) + at.dp * ROWS
    key_at = lax.div(col, ROWS) * GROUP + lax.rem(col, ROWS)
    weight = jnp.zeros((RING * ROWS, 1), F32)
    for yy in range(RING):
        raw = lax.dot_general(
            stacked, m.keys[0, yy], (((1,), (1,)), ((), ())), preferred_element_type=F32
        ) * HEAD ** (-0.5)
        kept = jnp.where(key_at + yy * ROWS <= query_at, jnp.exp(raw), 0.0)
        m.scores[yy] = kept
        weight = weight + jnp.sum(kept, axis=1, keepdims=True)
    mix = jnp.zeros((RING * ROWS, HEAD), F32)
    for yy in range(RING):
        mix = mix + jnp.dot(
            (m.scores[yy] / weight).astype(BF), m.keys[1, yy], preferred_element_type=F32
        )

    def head_of(c):
        return pl.ds(c * HEAD, HEAD)

    heads = Gather(
        at,
        lambda c: m.mixed.at[at.y, own_rows, head_of(c)],
        lambda c, yy, rows: m.mixed.at[yy, rows, head_of(c)],
        (m.ml, m.mr, m.mp),
    )
    for h in range(RING):
        m.mixed[at.y, own_rows, h * HEAD : (h + 1) * HEAD] = mix[h * ROWS : (h + 1) * ROWS].astype(BF)
        heads.line(h)
    for h in range(RING):
        heads.arrived(h)
        heads.ring(h)
    spread_weights(2)
    for h in range(RING):
        heads.hand_on(h)

    def project(yy):
        m.a_part[yy] = jnp.dot(m.mixed[yy], m.wo[...], preferred_element_type=F32).astype(BF)

    project(at.y)
    project(at.yi(1))
    project(at.yi(3))
    for h in range(RING):
        heads.finish(h)
    project(at.yi(2))
    tile, more = scatter_x(at, m.a_part, m.a_pair, m.a_total, m.a_first, m.a_second, m.ax)

    def drain():
        for copy in pending + more:
            copy.wait_send()
        squares.drain()
        for c in range(q_chunks):
            qs.drain(c)
        for h in range(RING):
            heads.drain(h)

    return tile, drain


def kernel(names, *refs):
    m = types.SimpleNamespace()
    for name, ref in zip(names, refs):
        if name.endswith("_s"):
            setattr(m, name[:-2], [ref])
        elif name.endswith("_r"):
            getattr(m, name[:-2]).append(ref)
        else:
            setattr(m, name, ref)
    at = Place()
    chunks = m.wgu.shape[0]
    side, team = lax.rem(at.z, 2), lax.div(at.z, 2)
    partner = {"dp": (at.z + 1 - 2 * side) * RING + at.y}
    span = chunks * HEAD

    loads = [
        pltpu.make_async_copy(m.wq_hbm, m.wq, m.local.at[0]),
        pltpu.make_async_copy(
            m.wkv_hbm.at[at.core, :, pl.ds(at.x * HEAD, HEAD)], m.wkv, m.local.at[1]
        ),
        pltpu.make_async_copy(m.wo_hbm, m.wo, m.local.at[2]),
    ]

    def columns(n, c):
        return pl.ds(pl.multiple_of(n * span + c * HEAD, HEAD), HEAD)

    def kept(c, g):
        return pltpu.make_async_copy(
            m.wgu_hbm.at[g, :, columns(side, c)],
            m.wgu.at[c, side, :, pl.ds(g * HEAD, HEAD)],
            m.keep.at[c, g],
        )

    def given(c, g):
        return send(
            m.wgu_hbm.at[g, :, columns(1 - side, c)],
            m.wgu.at[c, side, :, pl.ds(g * HEAD, HEAD)],
            m.give,
            (c, g),
            partner,
        )

    def down(c, n):
        return pltpu.make_async_copy(
            m.wd_hbm.at[pl.ds(n * span + c * HEAD, HEAD)],
            m.wd.at[c, pl.ds(n * HEAD, HEAD)],
            m.down.at[c, n],
        )

    every = [(c, g) for c in range(chunks) for g in range(2)]
    shares = (every[:6], every[6:8], every[8:])

    def spread_weights(stage):
        for c, g in shares[stage]:
            given(c, g).start()

    for load in loads:
        load.start()
    enter(
        [at.ydev(k) for k in (1, 2, 3)]
        + [at.zdev(k) for k in (1, 2, 3)]
        + [at.xdev(1), at.xdev(3), at.sibling(), at.across()]
    )
    own = (pl.ds(2 * at.core, 2), pl.ds(at.x * ROWS, ROWS))
    swap = send(m.src, m.tokens.at[own], m.swap, 0, at.across())
    swap.start()
    for c, g in every:
        kept(c, g).start()
        down(c, g).start()
    for load in loads:
        load.wait()
    swap.wait_recv()
    spread_weights(0)
    tile, drain = attention(at, m, m.gain_attn[...].astype(F32), spread_weights)
    resid = (m.tokens[own].astype(F32) + tile).astype(BF)

    gain = m.gain_ffn[...].astype(F32)
    m.f_gained[...] = (resid.astype(F32) * gain[None]).astype(BF)
    trade = send(m.f_gained, m.f_tokens.at[(1, *own)], m.trade, 0, partner)
    trade.start()
    m.f_tokens[(0, *own)] = resid
    near, away = (Spread(at, m.f_tokens.at[i], sems) for i, sems in enumerate((m.fx, m.gz)))
    near.start()
    trade.wait_recv()
    away.start()
    near.onward()
    near.end()
    away.onward()
    away.end()
    near.finish()
    squares = Squares(at, m.fs_part, m.fs_near, m.fs_mid, m.fs_far, m.fsy, m.fsz)
    for k in (2, 1, 3):
        scaled(m.f_tokens.at[0], gain, m.f_normed, squares, at.yi(k))
    squares.start()
    scaled(m.f_tokens.at[0], gain, m.f_normed, squares, at.y)
    away.finish()

    fellow = [(0, pl.ds((1 - team) * 2 * ROWS, 2 * ROWS), at.zdev(2))]
    own_rows = pl.ds(team * 2 * ROWS, 2 * ROWS)
    own_lanes = pl.ds(pl.multiple_of(side * HEAD, HEAD), HEAD)
    hs = Reduce(at, m.h_part, m.h_one, m.h_two, m.h_three, (m.h1, m.h2, m.h3), fellow)
    hg = Gather(
        at,
        lambda c: m.hidden.at[c, at.y, own_rows, own_lanes],
        lambda c, yy, rows: m.hidden.at[c, yy, rows],
        (m.hl, m.hr, m.hp),
    )

    def product(c, yy):
        return jnp.dot(m.f_normed[yy], m.wgu[c, side], preferred_element_type=F32) + jnp.dot(
            m.f_tokens[1, yy], m.wgu[c, 1 - side], preferred_element_type=F32
        )

    def first(c):
        for g in range(2):
            kept(c, g).wait()
            given(c, g).wait_recv()
        hs.far(c, product)

    def activate(c):
        both = hs.result(c, own_rows) * m.scale[...]
        gate, up = both[:, :HEAD], both[:, HEAD:]
        m.hidden[c, at.y, own_rows, own_lanes] = (gate / (1.0 + jnp.exp(-gate)) * up).astype(BF)
        hg.line(c)

    def ring(c):
        hg.arrived(c)
        hg.ring(c)

    def add_down(c, k):
        yy = at.yi(k)
        m.acc[k] += jnp.dot(m.hidden[c, yy], m.wd[c], preferred_element_type=F32)

    def down_near(c):
        for n in range(2):
            down(c, n).wait()
        for k in (0, 1, 3):
            add_down(c, k)

    def down_far(c):
        hg.finish(c)
        add_down(c, 2)

    m.acc[...] = jnp.zeros_like(m.acc)
    squares.middle()
    m.scale[...] = jnp.broadcast_to(squares.scale(2 * ROWS, team * 2 * ROWS), m.scale.shape)
    stages = (
        (first, 0),
        (lambda c: hs.near(c, product), 2),
        (lambda c: hs.own(c, product), 4),
        (activate, 5),
        (ring, 6),
        (hg.hand_on, 7),
        (down_near, 8),
        (down_far, 9),
    )

    def turn(i, carry):
        for stage, lag in stages:
            c = i - lag

            @pl.when((c >= 0) & (c < chunks))
            def _():
                stage(c)

        return carry

    lax.fori_loop(0, chunks + stages[-1][1], turn, 0)
    for k in range(RING):
        m.f_part[at.yi(k)] = m.acc[k].astype(BF)
    tile, more = scatter_x(at, m.f_part, m.f_pair, m.f_total, m.f_first, m.f_second, m.bx)
    m.out[...] = (m.f_tokens[(0, *own)].astype(F32) + tile).astype(BF)

    def each(body):
        lax.fori_loop(0, chunks, lambda c, carry: (body(c), carry)[1], 0)

    drain()
    for copy in [swap, trade] + near.copies() + away.copies() + more:
        copy.wait_send()
    squares.drain()
    each(hs.drain)
    each(hg.drain)

    def drain_given(c):
        for g in range(2):
            given(c, g).wait_send()

    each(drain_given)


def reduce_scratch(name, chunks, columns, slots, rows):
    return {
        name + "_part": pltpu.VMEM((chunks, RING, GROUP, columns), BF),
        name + "_one": pltpu.VMEM((chunks, 2, GROUP // 2, columns), BF),
        name + "_two": pltpu.VMEM((chunks, 2, GROUP, columns), BF),
        name + "_three": pltpu.VMEM((chunks, slots, rows, columns), BF),
    }


def square_scratch(name):
    return {
        name + "_part": pltpu.VMEM((RING, 8, GROUP), F32),
        name + "_near": pltpu.VMEM((3, 8, GROUP), F32),
        name + "_mid": pltpu.VMEM((8, GROUP), F32),
        name + "_far": pltpu.VMEM((3, 8, GROUP), F32),
    }


def scatter_scratch(name, columns):
    return {
        name + "_part": pltpu.VMEM((RING, GROUP, columns), BF),
        name + "_pair": pltpu.VMEM((2, GROUP, columns), BF),
        name + "_total": pltpu.VMEM((2, GROUP, columns), BF),
        name + "_first": pltpu.VMEM((2, ROWS, columns), BF),
        name + "_second": pltpu.VMEM((2, 2, ROWS, columns), BF),
    }


def scratch(cols, heads, chunks, q_chunks):
    wide = 2 * HEAD
    buffers = {
        "tokens": pltpu.VMEM((RING, GROUP, cols), BF),
        "normed": pltpu.VMEM((RING, GROUP, cols), BF),
        "wq": pltpu.VMEM((cols, heads), BF),
        "wkv": pltpu.VMEM((cols, HEAD), BF),
        "wo": pltpu.VMEM((heads, cols), BF),
        **reduce_scratch("q", q_chunks, heads // q_chunks, 3, ROWS),
        "k_part": pltpu.VMEM((RING, GROUP, HEAD), BF),
        "k_near": pltpu.VMEM((3, GROUP, HEAD), BF),
        "k_far": pltpu.VMEM((3, ROWS, HEAD), BF),
        **square_scratch("ss"),
        "keys": pltpu.VMEM((2, RING, GROUP, HEAD), BF),
        "mixed": pltpu.VMEM((RING, GROUP, heads), BF),
        "scores": pltpu.VMEM((RING, RING * ROWS, GROUP), F32),
        **scatter_scratch("a", cols),
        "f_gained": pltpu.VMEM((2, ROWS, cols), BF),
        "f_tokens": pltpu.VMEM((2, RING, GROUP, cols), BF),
        "f_normed": pltpu.VMEM((RING, GROUP, cols), BF),
        "wgu": pltpu.VMEM((chunks, 2, cols, wide), BF),
        "wd": pltpu.VMEM((chunks, wide, cols), BF),
        **reduce_scratch("h", chunks, wide, 1, 2 * ROWS),
        **square_scratch("fs"),
        "scale": pltpu.VMEM((2 * ROWS, wide), F32),
        "hidden": pltpu.VMEM((chunks, RING, GROUP, wide), BF),
        "acc": pltpu.VMEM((RING, GROUP, cols), F32),
        **scatter_scratch("f", cols),
    }
    single = {"local": (3,), "keep": (chunks, 2), "down": (chunks, 2)}
    double = {
        "give": (chunks, 2), "swap": (1,), "trade": (1,),
        "gx": (8,), "fx": (8,), "gz": (8,), "ax": (8,), "bx": (8,),
        "ssy": (3,), "ssz": (3,), "fsy": (3,), "fsz": (3,),
        "q1": (q_chunks, 2), "q2": (q_chunks, 2), "q3": (q_chunks, 3),
        "k1": (3,), "k2": (3,), "kl": (3,), "kr": (3,), "kc": (4,),
        "ml": (RING, 3), "mr": (RING, 2), "mp": (RING, 2),
        "h1": (chunks, 2), "h2": (chunks, 2), "h3": (chunks, 1),
        "hl": (chunks, 3), "hr": (chunks, 2), "hp": (chunks, 2),
    }
    for name, shape in single.items():
        buffers[name] = pltpu.SemaphoreType.DMA(shape)
    for name, shape in double.items():
        buffers[name + "_s"] = pltpu.SemaphoreType.DMA(shape)
        buffers[name + "_r"] = pltpu.SemaphoreType.DMA(shape)
    return buffers


def rotary_table(count):
    freq = np.exp(-(2.0 * np.arange(HEAD // 2) / HEAD) * math.log(THETA))
    position = np.concatenate([np.arange(ROWS), np.arange(count) * ROWS]).astype(np.float64)
    angle = position[:, None] * np.concatenate([freq, freq])[None, :]
    return np.stack([np.cos(angle), np.sin(angle)]).astype(np.float32)


def local_layer(
    section_input, gain_attn, w_query, key_value_weight, w_output, gain_ffn, w_gate_up, w_down
):
    cols = section_input.shape[2]
    heads = w_query.shape[2]
    chunks = w_gate_up.shape[3] // (2 * HEAD)
    anywhere = pl.BlockSpec(memory_space=pl.ANY)
    vmem = pl.BlockSpec(memory_space=pltpu.VMEM)
    inputs = {
        "src": (section_input.reshape(2, ROWS, cols), anywhere),
        "gain_attn": (gain_attn, vmem),
        "wq_hbm": (w_query[0], anywhere),
        "wkv_hbm": (key_value_weight[0], anywhere),
        "wo_hbm": (w_output[0], anywhere),
        "gain_ffn": (gain_ffn, vmem),
        "wgu_hbm": (w_gate_up[0], anywhere),
        "wd_hbm": (w_down[0], anywhere),
        "table": (jnp.asarray(rotary_table(RING * RING)), vmem),
    }
    buffers = scratch(cols, heads, chunks, 2)
    result = pl.pallas_call(
        functools.partial(kernel, (*inputs, "out", *buffers)),
        name="layer",
        out_shape=jax.ShapeDtypeStruct((2, ROWS, cols), BF),
        in_specs=[spec for _, spec in inputs.values()],
        out_specs=vmem,
        scratch_shapes=list(buffers.values()),
        compiler_params=pltpu.CompilerParams(
            collective_id=0, has_side_effects=True, vmem_limit_bytes=60 * 1024 * 1024
        ),
    )(*[array for array, _ in inputs.values()])
    return result.reshape(1, 2 * ROWS, cols)


def solution(mesh):
    placed = (
        P("section", "tensor", "dp"),
        P("section", "dp"),
        P("section", "dp", "tensor"),
        P("section", None, "dp", None),
        P("section", "tensor", "dp"),
        P("section", "dp"),
        P("section", None, "dp", "tensor"),
        P("section", "tensor", "dp"),
    )
    return jax.shard_map(
        local_layer, mesh=mesh, in_specs=placed, out_specs=P("section", "tensor", "dp"), check_vma=False
    )
```

```python
import functools
import math
import types

import jax
import jax.numpy as jnp
import numpy as np
from jax import lax
from jax.experimental import pallas as pl
from jax.experimental.pallas import tpu as pltpu
from jax.sharding import PartitionSpec as P

HEAD = 128
EPS = 1e-05
THETA = 500000.0
RING = 4
ROWS = 64
GROUP = RING * ROWS
WIDTH = 8192
SPLIT = (5, 11)

MESH_ID = pl.DeviceIdType.MESH
BF = jnp.bfloat16
F32 = jnp.float32


class Place:
    def __init__(self):
        self.section = lax.axis_index("section")
        dp = lax.axis_index("dp")
        tensor = lax.axis_index("tensor")
        self.dp = dp
        self.z, self.y = lax.div(dp, RING), lax.rem(dp, RING)
        self.x, self.core = lax.div(tensor, 2), lax.rem(tensor, 2)

    def yi(self, k):
        return lax.rem(self.y + k, RING)

    def zi(self, k):
        return lax.rem(self.z + k, RING)

    def xi(self, k):
        return lax.rem(self.x + k, RING)

    def ydev(self, k):
        return {"dp": self.z * RING + self.yi(k)}

    def zdev(self, k):
        return {"dp": self.zi(k) * RING + self.y}

    def xdev(self, k):
        return {"tensor": self.xi(k) * 2 + self.core}

    def sibling(self):
        return {"tensor": self.x * 2 + 1 - self.core}

    def across(self):
        return {"section": 1 - self.section}


def enter(devices):
    barrier = pltpu.get_barrier_semaphore()
    for device in devices:
        pl.semaphore_signal(barrier, inc=1, device_id=device, device_id_type=MESH_ID)
    pl.semaphore_wait(barrier, len(devices))


def send(src, dst, sems, index, device):
    return pltpu.make_async_remote_copy(
        src_ref=src,
        dst_ref=dst,
        send_sem=sems[0].at[index],
        recv_sem=sems[1].at[index],
        device_id=device,
        device_id_type=MESH_ID,
    )


class Spread:
    def __init__(self, at, tokens, h, sems):
        self.right, self.left, self.far = at.xi(1), at.xi(3), at.xi(2)

        def rows(xx, start, count):
            return tokens.at[2 * at.core + h, pl.ds(xx * ROWS + start, count)]

        def block(xx):
            return rows(xx, 0, ROWS)

        def same(ref, index, device):
            return send(ref, ref, sems, (h, index), device)

        half = ROWS // 2
        self.out = [
            same(block(at.x), 0, at.xdev(1)),
            same(block(at.x), 1, at.xdev(3)),
            same(block(at.x), 2, at.sibling()),
        ]
        self.after_left = [
            same(rows(self.left, 0, half), 3, at.xdev(1)),
            same(block(self.left), 4, at.sibling()),
        ]
        self.after_right = [
            same(rows(self.right, half, half), 5, at.xdev(3)),
            same(block(self.right), 6, at.sibling()),
        ]
        self.last = [same(block(self.far), 7, at.sibling())]

    def start(self):
        for copy in self.out:
            copy.start()

    def onward(self):
        self.out[0].wait_recv()
        for copy in self.after_left:
            copy.start()
        self.out[1].wait_recv()
        for copy in self.after_right:
            copy.start()

    def end(self):
        self.after_left[0].wait_recv()
        self.after_right[0].wait_recv()
        self.last[0].start()

    def finish(self):
        for copy in (self.out[2], self.after_left[1], self.after_right[1], self.last[0]):
            copy.wait_recv()

    def copies(self):
        return [*self.out, *self.after_left, *self.after_right, *self.last]


class Scatter:
    def __init__(self, at, part, pair, total, first, second, h, sems):
        self.at, self.part, self.pair, self.h = at, part, pair, h
        self.total, self.first, self.second = total, first, second
        self.mine, other = 2 * at.core + h, 2 * (1 - at.core) + h
        self.right, self.left, self.far = at.xi(1), at.xi(3), at.xi(2)
        self.half = ROWS // 2

        def to(src, dst, index, device):
            return send(src, dst, sems, (h, index), device)

        self.shares = [
            to(part.at[other, self.rows(xx)], pair.at[h, self.rows(xx)], i, at.sibling())
            for i, xx in enumerate((self.far, self.right, self.left, at.x))
        ]
        self.ones = [
            to(total.at[h, pl.ds(self.far * ROWS, self.half)], first.at[h, 0], 4, at.xdev(1)),
            to(total.at[h, pl.ds(self.far * ROWS + self.half, self.half)], first.at[h, 1], 5, at.xdev(3)),
        ]
        self.twos = [
            to(total.at[h, self.rows(self.right)], second.at[h, 0], 6, at.xdev(1)),
            to(total.at[h, self.rows(self.left)], second.at[h, 1], 7, at.xdev(3)),
        ]

    def rows(self, xx):
        return pl.ds(xx * ROWS, ROWS)

    def summed(self, i, xx):
        self.shares[i].wait_recv()
        return self.part[self.mine, self.rows(xx)].astype(F32) + self.pair[self.h, self.rows(xx)].astype(F32)

    def start(self):
        for copy in self.shares:
            copy.start()

    def step_one(self):
        self.total[self.h, self.rows(self.far)] = self.summed(0, self.far).astype(BF)
        for copy in self.ones:
            copy.start()

    def step_two(self):
        half = self.half
        value = self.summed(1, self.right)
        self.ones[0].wait_recv()
        added = value[:half] + self.first[self.h, 0].astype(F32)
        self.total[self.h, self.rows(self.right)] = jnp.concatenate([added, value[half:]], axis=0).astype(BF)
        self.twos[0].start()
        value = self.summed(2, self.left)
        self.ones[1].wait_recv()
        added = value[half:] + self.first[self.h, 1].astype(F32)
        self.total[self.h, self.rows(self.left)] = jnp.concatenate([value[:half], added], axis=0).astype(BF)
        self.twos[1].start()

    def result(self):
        own = self.summed(3, self.at.x)
        for copy in self.twos:
            copy.wait_recv()
        return own + self.second[self.h, 0].astype(F32) + self.second[self.h, 1].astype(F32)

    def copies(self):
        return [*self.shares, *self.ones, *self.twos]


class Reduce:
    def __init__(self, at, part, first, second, third, sems, hand):
        self.at = at
        self.part, self.first, self.second, self.third = part, first, second, third
        self.sems_one, self.sems_two, self.sems_three = sems
        self.hand = hand

    def ones(self, c):
        far = self.at.yi(2)
        low, high = pl.ds(0, GROUP // 2), pl.ds(GROUP // 2, GROUP // 2)
        return (
            send(self.part.at[c, far, low], self.first.at[c, 0], self.sems_one, (c, 0), self.at.ydev(1)),
            send(self.part.at[c, far, high], self.first.at[c, 1], self.sems_one, (c, 1), self.at.ydev(3)),
        )

    def twos(self, c):
        return (
            send(self.part.at[c, self.at.yi(1)], self.second.at[c, 0], self.sems_two, (c, 0), self.at.ydev(1)),
            send(self.part.at[c, self.at.yi(3)], self.second.at[c, 1], self.sems_two, (c, 1), self.at.ydev(3)),
        )

    def threes(self, c):
        return [
            send(
                self.part.at[c, self.at.y, rows], self.third.at[c, slot], self.sems_three, (c, slot), device
            )
            for slot, rows, device in self.hand
        ]

    def far(self, c, product):
        self.part[c, self.at.yi(2)] = product(c, self.at.yi(2)).astype(BF)
        for copy in self.ones(c):
            copy.start()

    def near(self, c, product):
        half = GROUP // 2
        one, two = self.ones(c), self.twos(c)
        right, left = self.at.yi(1), self.at.yi(3)
        value = product(c, right)
        one[0].wait_recv()
        self.part[c, right, 0:half] = (value[:half] + self.first[c, 0].astype(F32)).astype(BF)
        self.part[c, right, half:GROUP] = value[half:].astype(BF)
        two[0].start()
        value = product(c, left)
        one[1].wait_recv()
        self.part[c, left, 0:half] = value[:half].astype(BF)
        self.part[c, left, half:GROUP] = (value[half:] + self.first[c, 1].astype(F32)).astype(BF)
        two[1].start()

    def own(self, c, product):
        value = product(c, self.at.y)
        for copy in self.twos(c):
            copy.wait_recv()
        self.part[c, self.at.y] = (
            value + self.second[c, 0].astype(F32) + self.second[c, 1].astype(F32)
        ).astype(BF)
        for copy in self.threes(c):
            copy.start()

    def result(self, c, rows):
        for copy in self.threes(c):
            copy.wait_recv()
        total = self.part[c, self.at.y, rows].astype(F32)
        for slot, _, _ in self.hand:
            total = total + self.third[c, slot].astype(F32)
        return total

    def drain(self, c):
        for copy in (*self.ones(c), *self.twos(c), *self.threes(c)):
            copy.wait_send()


class Gather:
    def __init__(self, at, mine, block, sems):
        self.at, self.mine, self.block = at, mine, block
        self.sems_line, self.sems_ring, self.sems_pass = sems

    def lines(self, c):
        return [
            send(self.mine(c), self.mine(c), self.sems_line, (c, k - 1), self.at.zdev(k))
            for k in (2, 1, 3)
        ]

    def rings(self, c):
        block = self.block(c, self.at.y, pl.ds(0, GROUP))
        return [
            send(block, block, self.sems_ring, (c, 0), self.at.ydev(1)),
            send(block, block, self.sems_ring, (c, 1), self.at.ydev(3)),
        ]

    def passes(self, c):
        low = self.block(c, self.at.yi(3), pl.ds(0, GROUP // 2))
        high = self.block(c, self.at.yi(1), pl.ds(GROUP // 2, GROUP // 2))
        return [
            send(low, low, self.sems_pass, (c, 0), self.at.ydev(1)),
            send(high, high, self.sems_pass, (c, 1), self.at.ydev(3)),
        ]

    def line(self, c):
        for copy in self.lines(c):
            copy.start()

    def arrived(self, c):
        for copy in self.lines(c):
            copy.wait_recv()

    def ring(self, c):
        for copy in self.rings(c):
            copy.start()

    def hand_on(self, c):
        for ring, onward in zip(self.rings(c), self.passes(c)):
            ring.wait_recv()
            onward.start()

    def finish(self, c):
        for copy in self.passes(c):
            copy.wait_recv()

    def drain(self, c):
        for copy in (*self.lines(c), *self.rings(c), *self.passes(c)):
            copy.wait_send()


class Squares:
    def __init__(self, at, part, near, mid, far, sems_y, sems_z):
        self.at, self.part, self.near, self.mid, self.far = at, part, near, mid, far
        self.sems_y, self.sems_z = sems_y, sems_z

    def fill(self, yy, wide):
        squared = (wide * wide).astype(BF)
        self.part[yy] = lax.dot_general(
            jnp.ones((8, wide.shape[1]), BF),
            squared,
            (((1,), (1,)), ((), ())),
            preferred_element_type=F32,
        )

    def ys(self):
        return [
            send(self.part.at[self.at.yi(k)], self.near.at[k - 1], self.sems_y, k - 1, self.at.ydev(k))
            for k in (1, 2, 3)
        ]

    def zs(self):
        return [
            send(self.mid, self.far.at[k - 1], self.sems_z, k - 1, self.at.zdev(k)) for k in (1, 2, 3)
        ]

    def start(self):
        for copy in self.ys():
            copy.start()

    def middle(self):
        for copy in self.ys():
            copy.wait_recv()
        self.mid[...] = self.part[self.at.y] + self.near[0] + self.near[1] + self.near[2]
        for copy in self.zs():
            copy.start()

    def scale(self, count, start):
        for copy in self.zs():
            copy.wait_recv()
        total = self.mid[...] + self.far[0] + self.far[1] + self.far[2]
        line = lax.rsqrt(total / WIDTH + EPS)[0:1]
        row = lax.broadcasted_iota(jnp.int32, (count, GROUP), 0)
        lane = lax.broadcasted_iota(jnp.int32, (count, GROUP), 1)
        picked = jnp.where(lane == row + start, jnp.broadcast_to(line, (count, GROUP)), 0.0)
        return jnp.sum(picked, axis=1, keepdims=True)

    def drain(self):
        for copy in (*self.ys(), *self.zs()):
            copy.wait_send()


def scaled(tokens, gain, out, squares, yy):
    wide = tokens[yy].astype(F32)
    squares.fill(yy, wide)
    out[yy] = (wide * gain).astype(BF)


def attention(at, m, spread, gain, spread_weights):
    half = HEAD // 2
    lane = lax.broadcasted_iota(jnp.int32, (1, HEAD), 1)
    base = [m.table[i, pl.ds(ROWS + at.dp, 1), :] for i in range(2)]
    step = [m.table[i, 0:ROWS, :] for i in range(2)]
    cosine = base[0] * step[0] - base[1] * step[1]
    sine = (base[1] * step[0] + base[0] * step[1]) * jnp.where(lane < half, -1.0, 1.0)
    for piece in spread:
        piece.onward()
    for piece in spread:
        piece.end()
    for piece in spread:
        piece.finish()
    pending = [copy for piece in spread for copy in piece.copies()]

    squares = Squares(at, m.ss_part, m.ss_near, m.ss_mid, m.ss_far, m.ssy, m.ssz)
    along = [(k - 1, pl.ds(at.zi(k) * ROWS, ROWS), at.zdev(k)) for k in (2, 1, 3)]
    own_rows = pl.ds(at.z * ROWS, ROWS)
    qs = Reduce(at, m.q_part, m.q_one, m.q_two, m.q_three, (m.q1, m.q2, m.q3), along)
    q_chunks = m.q_part.shape[0]
    q_cols = m.q_part.shape[3]

    def product_q(c, yy):
        columns = m.wq[:, c * q_cols : (c + 1) * q_cols]
        return jnp.dot(m.normed[yy], columns, preferred_element_type=F32)

    def product_k(yy):
        return jnp.dot(m.normed[yy], m.wkv[...], preferred_element_type=F32)

    key_y = [
        send(m.k_part.at[at.yi(k)], m.k_near.at[k - 1], m.k1, k - 1, at.ydev(k)) for k in (2, 1, 3)
    ]
    for k, copy in zip((2, 1, 3), key_y):
        scaled(m.tokens, gain, m.normed, squares, at.yi(k))
        m.k_part[at.yi(k)] = product_k(at.yi(k)).astype(BF)
        copy.start()
    squares.start()
    for c in range(q_chunks):
        qs.far(c, product_q)
    scaled(m.tokens, gain, m.normed, squares, at.y)
    total = product_k(at.y)
    for k, copy in zip((2, 1, 3), key_y):
        copy.wait_recv()
        total = total + m.k_near[k - 1].astype(F32)
    m.k_part[at.y] = total.astype(BF)
    key_z = [
        send(m.k_part.at[at.y, rows], m.k_far.at[slot], m.k2, slot, device)
        for slot, rows, device in along
    ]
    for copy in key_z:
        copy.start()
    squares.middle()
    for c in range(q_chunks):
        qs.near(c, product_q)
    scale = squares.scale(ROWS, at.z * ROWS)

    def rotated(value, cos, sin):
        return value * cos + pltpu.roll(value, half, 1) * sin

    is_key = at.core == 0
    core = at.core
    value = m.k_part[at.y, own_rows].astype(F32)
    for slot, copy in zip((1, 0, 2), key_z):
        copy.wait_recv()
        value = value + m.k_far[slot].astype(F32)
    m.keys[core, at.y, own_rows] = rotated(
        value * scale, jnp.where(is_key, cosine, 1.0), jnp.where(is_key, sine, 0.0)
    ).astype(BF)
    mine = m.keys.at[core, at.y, own_rows]
    lines = [send(mine, mine, m.kl, k - 1, at.zdev(k)) for k in (2, 1, 3)]
    for copy in lines:
        copy.start()
    qs.own(0, product_q)
    for copy in lines:
        copy.wait_recv()
    block = m.keys.at[core, at.y]
    rings = [send(block, block, m.kr, k - 1, at.ydev(k)) for k in (2, 1, 3)]
    shares = [send(block, block, m.kc, 0, at.sibling())]
    for copy in rings + shares:
        copy.start()
    for c in range(1, q_chunks):
        qs.own(c, product_q)
    for k, ring in zip((2, 1, 3), rings):
        ring.wait_recv()
        came = m.keys.at[core, at.yi(RING - k)]
        shares.append(send(came, came, m.kc, k, at.sibling()))
        shares[-1].start()
    pending += key_y + key_z + lines + rings + shares

    per = q_cols // HEAD
    pieces = []
    for c in range(q_chunks):
        queries = qs.result(c, own_rows) * scale
        pieces += [rotated(queries[:, h * HEAD : (h + 1) * HEAD], cosine, sine) for h in range(per)]
    stacked = jnp.concatenate(pieces, axis=0).astype(BF)
    for copy in shares:
        copy.wait_recv()
    row = lax.broadcasted_iota(jnp.int32, (RING * ROWS, GROUP), 0)
    col = lax.broadcasted_iota(jnp.int32, (RING * ROWS, GROUP), 1)
    query_at = lax.rem(row, ROWS) + at.dp * ROWS
    key_at = lax.div(col, ROWS) * GROUP + lax.rem(col, ROWS)
    weight = jnp.zeros((RING * ROWS, 1), F32)
    for yy in range(RING):
        raw = lax.dot_general(
            stacked, m.keys[0, yy], (((1,), (1,)), ((), ())), preferred_element_type=F32
        ) * HEAD ** (-0.5)
        kept = jnp.where(key_at + yy * ROWS <= query_at, jnp.exp(raw), 0.0)
        m.scores[yy] = kept
        weight = weight + jnp.sum(kept, axis=1, keepdims=True)
    mix = jnp.zeros((RING * ROWS, HEAD), F32)
    for yy in range(RING):
        mix = mix + jnp.dot(
            (m.scores[yy] / weight).astype(BF), m.keys[1, yy], preferred_element_type=F32
        )

    def head_of(c):
        return pl.ds(c * HEAD, HEAD)

    heads = Gather(
        at,
        lambda c: m.mixed.at[at.y, own_rows, head_of(c)],
        lambda c, yy, rows: m.mixed.at[yy, rows, head_of(c)],
        (m.ml, m.mr, m.mp),
    )
    for h in range(RING):
        m.mixed[at.y, own_rows, h * HEAD : (h + 1) * HEAD] = mix[h * ROWS : (h + 1) * ROWS].astype(BF)
        heads.line(h)
    for h in range(RING):
        heads.arrived(h)
        heads.ring(h)
    spread_weights(1)
    for h in range(RING):
        heads.hand_on(h)

    def project(yy):
        m.a_part[yy] = jnp.dot(m.mixed[yy], m.wo[...], preferred_element_type=F32).astype(BF)

    project(at.y)
    project(at.yi(1))
    project(at.yi(3))
    for h in range(RING):
        heads.finish(h)
    project(at.yi(2))

    def drain():
        for copy in pending:
            copy.wait_send()
        squares.drain()
        for c in range(q_chunks):
            qs.drain(c)
        for h in range(RING):
            heads.drain(h)

    return drain


def kernel(names, *refs):
    m = types.SimpleNamespace()
    for name, ref in zip(names, refs):
        if name.endswith("_s"):
            setattr(m, name[:-2], [ref])
        elif name.endswith("_r"):
            getattr(m, name[:-2]).append(ref)
        else:
            setattr(m, name, ref)
    at = Place()
    chunks = m.wgu.shape[0]
    side, team = lax.rem(at.z, 2), lax.div(at.z, 2)
    partner = {"dp": (at.z + 1 - 2 * side) * RING + at.y}
    span = chunks * HEAD

    enter(
        [at.ydev(k) for k in (1, 2, 3)]
        + [at.zdev(k) for k in (1, 2, 3)]
        + [at.xdev(1), at.xdev(3), at.sibling(), at.across()]
    )
    own = [(2 * at.core + h, pl.ds(at.x * ROWS, ROWS)) for h in range(2)]
    swaps = [send(m.src.at[h], m.tokens.at[own[h]], m.swap, h, at.across()) for h in range(2)]
    for swap in swaps:
        swap.start()
    loads = [
        pltpu.make_async_copy(*pair, m.local.at[i])
        for i, pair in enumerate(
            (
                (m.gain_attn_hbm, m.gain_attn),
                (m.wkv_hbm.at[at.core, :, pl.ds(at.x * HEAD, HEAD)], m.wkv),
                (m.wq_hbm, m.wq),
                (m.table_hbm, m.table),
                (m.wo_hbm, m.wo),
                (m.gain_ffn_hbm, m.gain_ffn),
            )
        )
    ]
    for load in loads:
        load.start()

    def columns(n, c):
        return pl.ds(pl.multiple_of(n * span + c * HEAD, HEAD), HEAD)

    def kept(c, g):
        return pltpu.make_async_copy(
            m.wgu_hbm.at[g, :, columns(side, c)],
            m.wgu.at[c, side, :, pl.ds(g * HEAD, HEAD)],
            m.keep.at[c, g],
        )

    def given(c, g):
        return send(
            m.wgu_hbm.at[g, :, columns(1 - side, c)],
            m.wgu.at[c, side, :, pl.ds(g * HEAD, HEAD)],
            m.give,
            (c, g),
            partner,
        )

    def down(c, n):
        return pltpu.make_async_copy(
            m.wd_hbm.at[pl.ds(n * span + c * HEAD, HEAD)],
            m.wd.at[c, pl.ds(n * HEAD, HEAD)],
            m.down.at[c, n],
        )

    every = [(c, g) for c in range(chunks) for g in range(2)]
    shares = (every[:SPLIT[0]], every[SPLIT[0]:SPLIT[1]], every[SPLIT[1]:])

    def spread_weights(stage):
        for c, g in shares[stage]:
            given(c, g).start()

    for c, g in every:
        kept(c, g).start()
        down(c, g).start()
    for load in loads:
        load.wait()
    spread = [Spread(at, m.tokens, h, m.gx) for h in range(2)]
    for swap, piece in zip(swaps, spread):
        swap.wait_recv()
        piece.start()
    spread_weights(0)
    drain = attention(at, m, spread, m.gain_attn[...].astype(F32), spread_weights)

    def scatters(part, pair, total, first, second, sems):
        pieces = [Scatter(at, part, pair, total, first, second, h, sems) for h in range(2)]
        for piece in pieces:
            piece.start()
        for piece in pieces:
            piece.step_one()
        for piece in pieces:
            piece.step_two()
        return pieces

    gain = m.gain_ffn[...].astype(F32)
    scatter_a = scatters(m.a_part, m.a_pair, m.a_total, m.a_first, m.a_second, m.ax)
    trades = [
        send(m.f_gained.at[h], m.f_tokens.at[(1, *own[h])], m.trade, h, partner) for h in range(2)
    ]
    near, away = (
        [Spread(at, m.f_tokens.at[i], h, sems) for h in range(2)] for i, sems in enumerate((m.fx, m.gz))
    )
    for h in range(2):
        resid = (m.tokens[own[h]].astype(F32) + scatter_a[h].result()).astype(BF)
        m.f_gained[h] = (resid.astype(F32) * gain).astype(BF)
        trades[h].start()
        m.f_tokens[(0, *own[h])] = resid
        near[h].start()
    spread_weights(2)
    for h in range(2):
        trades[h].wait_recv()
        away[h].start()
        near[h].onward()
    for h in range(2):
        near[h].end()
        away[h].onward()
    for h in range(2):
        away[h].end()
    for h in range(2):
        near[h].finish()
    squares = Squares(at, m.fs_part, m.fs_near, m.fs_mid, m.fs_far, m.fsy, m.fsz)
    for k in (2, 1, 3):
        scaled(m.f_tokens.at[0], gain, m.f_normed, squares, at.yi(k))
    squares.start()
    scaled(m.f_tokens.at[0], gain, m.f_normed, squares, at.y)
    m.acc[...] = jnp.zeros_like(m.acc)
    for h in range(2):
        away[h].finish()

    fellow = [(0, pl.ds((1 - team) * 2 * ROWS, 2 * ROWS), at.zdev(2))]
    own_rows = pl.ds(team * 2 * ROWS, 2 * ROWS)
    own_lanes = pl.ds(pl.multiple_of(side * HEAD, HEAD), HEAD)
    hs = Reduce(at, m.h_part, m.h_one, m.h_two, m.h_three, (m.h1, m.h2, m.h3), fellow)
    hg = Gather(
        at,
        lambda c: m.hidden.at[c, at.y, own_rows, own_lanes],
        lambda c, yy, rows: m.hidden.at[c, yy, rows],
        (m.hl, m.hr, m.hp),
    )

    def product(c, yy):
        return jnp.dot(m.f_normed[yy], m.wgu[c, side], preferred_element_type=F32) + jnp.dot(
            m.f_tokens[1, yy], m.wgu[c, 1 - side], preferred_element_type=F32
        )

    def first(c):
        for g in range(2):
            kept(c, g).wait()
            given(c, g).wait_recv()
        hs.far(c, product)

    def activate(c):
        both = hs.result(c, own_rows) * m.scale[...]
        gate, up = both[:, :HEAD], both[:, HEAD:]
        m.hidden[c, at.y, own_rows, own_lanes] = (gate / (1.0 + jnp.exp(-gate)) * up).astype(BF)
        hg.line(c)

    def ring(c):
        hg.arrived(c)
        hg.ring(c)

    def add_down(c, k):
        yy = at.yi(k)
        m.acc[k] += jnp.dot(m.hidden[c, yy], m.wd[c], preferred_element_type=F32)

    def down_near(c):
        for n in range(2):
            down(c, n).wait()
        for k in (0, 1, 3):
            add_down(c, k)

    def down_far(c):
        hg.finish(c)
        add_down(c, 2)

    squares.middle()
    m.scale[...] = jnp.broadcast_to(squares.scale(2 * ROWS, team * 2 * ROWS), m.scale.shape)
    stages = (
        (first, 0),
        (lambda c: hs.near(c, product), 2),
        (lambda c: hs.own(c, product), 4),
        (activate, 5),
        (ring, 6),
        (hg.hand_on, 7),
        (down_near, 8),
        (down_far, 9),
    )

    def turn(i, carry):
        for stage, lag in stages:
            c = i - lag

            @pl.when((c >= 0) & (c < chunks))
            def _():
                stage(c)

        return carry

    lax.fori_loop(0, chunks + stages[-1][1], turn, 0)
    for k in range(RING):
        m.f_part[at.yi(k)] = m.acc[k].astype(BF)
    scatter_f = scatters(m.f_part, m.f_pair, m.f_total, m.f_first, m.f_second, m.bx)
    for h in range(2):
        m.out[h] = (m.f_tokens[(0, *own[h])].astype(F32) + scatter_f[h].result()).astype(BF)

    def each(body):
        lax.fori_loop(0, chunks, lambda c, carry: (body(c), carry)[1], 0)

    drain()
    for copy in swaps + trades:
        copy.wait_send()
    for piece in near + away + scatter_a + scatter_f:
        for copy in piece.copies():
            copy.wait_send()
    squares.drain()
    each(hs.drain)
    each(hg.drain)

    def drain_given(c):
        for g in range(2):
            given(c, g).wait_send()

    each(drain_given)


def reduce_scratch(name, chunks, columns, slots, rows):
    return {
        name + "_part": pltpu.VMEM((chunks, RING, GROUP, columns), BF),
        name + "_one": pltpu.VMEM((chunks, 2, GROUP // 2, columns), BF),
        name + "_two": pltpu.VMEM((chunks, 2, GROUP, columns), BF),
        name + "_three": pltpu.VMEM((chunks, slots, rows, columns), BF),
    }


def square_scratch(name):
    return {
        name + "_part": pltpu.VMEM((RING, 8, GROUP), F32),
        name + "_near": pltpu.VMEM((3, 8, GROUP), F32),
        name + "_mid": pltpu.VMEM((8, GROUP), F32),
        name + "_far": pltpu.VMEM((3, 8, GROUP), F32),
    }


def scatter_scratch(name, columns):
    return {
        name + "_part": pltpu.VMEM((RING, GROUP, columns), BF),
        name + "_pair": pltpu.VMEM((2, GROUP, columns), BF),
        name + "_total": pltpu.VMEM((2, GROUP, columns), BF),
        name + "_first": pltpu.VMEM((2, 2, ROWS // 2, columns), BF),
        name + "_second": pltpu.VMEM((2, 2, ROWS, columns), BF),
    }


def scratch(cols, heads, chunks, q_chunks):
    wide = 2 * HEAD
    buffers = {
        "gain_attn": pltpu.VMEM((1, cols), BF),
        "gain_ffn": pltpu.VMEM((1, cols), BF),
        "table": pltpu.VMEM((2, ROWS + RING * RING, HEAD), F32),
        "tokens": pltpu.VMEM((RING, GROUP, cols), BF),
        "normed": pltpu.VMEM((RING, GROUP, cols), BF),
        "wq": pltpu.VMEM((cols, heads), BF),
        "wkv": pltpu.VMEM((cols, HEAD), BF),
        "wo": pltpu.VMEM((heads, cols), BF),
        **reduce_scratch("q", q_chunks, heads // q_chunks, 3, ROWS),
        "k_part": pltpu.VMEM((RING, GROUP, HEAD), BF),
        "k_near": pltpu.VMEM((3, GROUP, HEAD), BF),
        "k_far": pltpu.VMEM((3, ROWS, HEAD), BF),
        **square_scratch("ss"),
        "keys": pltpu.VMEM((2, RING, GROUP, HEAD), BF),
        "mixed": pltpu.VMEM((RING, GROUP, heads), BF),
        "scores": pltpu.VMEM((RING, RING * ROWS, GROUP), F32),
        **scatter_scratch("a", cols),
        "f_gained": pltpu.VMEM((2, ROWS, cols), BF),
        "f_tokens": pltpu.VMEM((2, RING, GROUP, cols), BF),
        "f_normed": pltpu.VMEM((RING, GROUP, cols), BF),
        "wgu": pltpu.VMEM((chunks, 2, cols, wide), BF),
        "wd": pltpu.VMEM((chunks, wide, cols), BF),
        **reduce_scratch("h", chunks, wide, 1, 2 * ROWS),
        **square_scratch("fs"),
        "scale": pltpu.VMEM((2 * ROWS, wide), F32),
        "hidden": pltpu.VMEM((chunks, RING, GROUP, wide), BF),
        "acc": pltpu.VMEM((RING, GROUP, cols), F32),
        **scatter_scratch("f", cols),
    }
    single = {"local": (6,), "keep": (chunks, 2), "down": (chunks, 2)}
    double = {
        "give": (chunks, 2), "swap": (2,), "trade": (2,),
        "gx": (2, 8), "fx": (2, 8), "gz": (2, 8), "ax": (2, 8), "bx": (2, 8),
        "ssy": (3,), "ssz": (3,), "fsy": (3,), "fsz": (3,),
        "q1": (q_chunks, 2), "q2": (q_chunks, 2), "q3": (q_chunks, 3),
        "k1": (3,), "k2": (3,), "kl": (3,), "kr": (3,), "kc": (4,),
        "ml": (RING, 3), "mr": (RING, 2), "mp": (RING, 2),
        "h1": (chunks, 2), "h2": (chunks, 2), "h3": (chunks, 1),
        "hl": (chunks, 3), "hr": (chunks, 2), "hp": (chunks, 2),
    }
    for name, shape in single.items():
        buffers[name] = pltpu.SemaphoreType.DMA(shape)
    for name, shape in double.items():
        buffers[name + "_s"] = pltpu.SemaphoreType.DMA(shape)
        buffers[name + "_r"] = pltpu.SemaphoreType.DMA(shape)
    return buffers


def rotary_table(count):
    freq = np.exp(-(2.0 * np.arange(HEAD // 2) / HEAD) * math.log(THETA))
    position = np.concatenate([np.arange(ROWS), np.arange(count) * ROWS]).astype(np.float64)
    angle = position[:, None] * np.concatenate([freq, freq])[None, :]
    return np.stack([np.cos(angle), np.sin(angle)]).astype(np.float32)


def local_layer(
    section_input, gain_attn, w_query, key_value_weight, w_output, gain_ffn, w_gate_up, w_down
):
    cols = section_input.shape[2]
    heads = w_query.shape[2]
    chunks = w_gate_up.shape[3] // (2 * HEAD)
    anywhere = pl.BlockSpec(memory_space=pl.ANY)
    vmem = pl.BlockSpec(memory_space=pltpu.VMEM)
    inputs = {
        "src": (section_input.reshape(2, ROWS, cols), anywhere),
        "gain_attn_hbm": (gain_attn, anywhere),
        "wq_hbm": (w_query[0], anywhere),
        "wkv_hbm": (key_value_weight[0], anywhere),
        "wo_hbm": (w_output[0], anywhere),
        "gain_ffn_hbm": (gain_ffn, anywhere),
        "wgu_hbm": (w_gate_up[0], anywhere),
        "wd_hbm": (w_down[0], anywhere),
        "table_hbm": (jnp.asarray(rotary_table(RING * RING)), anywhere),
    }
    buffers = scratch(cols, heads, chunks, 2)
    result = pl.pallas_call(
        functools.partial(kernel, (*inputs, "out", *buffers)),
        name="layer",
        out_shape=jax.ShapeDtypeStruct((2, ROWS, cols), BF),
        in_specs=[spec for _, spec in inputs.values()],
        out_specs=vmem,
        scratch_shapes=list(buffers.values()),
        compiler_params=pltpu.CompilerParams(
            collective_id=0, has_side_effects=True, vmem_limit_bytes=60 * 1024 * 1024
        ),
    )(*[array for array, _ in inputs.values()])
    return result.reshape(1, 2 * ROWS, cols)


def solution(mesh):
    placed = (
        P("section", "tensor", "dp"),
        P("section", "dp"),
        P("section", "dp", "tensor"),
        P("section", None, "dp", None),
        P("section", "tensor", "dp"),
        P("section", "dp"),
        P("section", None, "dp", "tensor"),
        P("section", "tensor", "dp"),
    )
    return jax.shard_map(
        local_layer, mesh=mesh, in_specs=placed, out_specs=P("section", "tensor", "dp"), check_vma=False
    )
```

```python
import functools
import math
import types

import jax
import jax.numpy as jnp
import numpy as np
from jax import lax
from jax.experimental import pallas as pl
from jax.experimental.pallas import tpu as pltpu
from jax.sharding import PartitionSpec as P

HEAD = 128
EPS = 1e-05
THETA = 500000.0
RING = 4
ROWS = 64
GROUP = RING * ROWS
WIDTH = 8192
SPLIT = (5, 10)

MESH_ID = pl.DeviceIdType.MESH
BF = jnp.bfloat16
F32 = jnp.float32


class Place:
    def __init__(self):
        self.section = lax.axis_index("section")
        dp = lax.axis_index("dp")
        tensor = lax.axis_index("tensor")
        self.dp = dp
        self.z, self.y = lax.div(dp, RING), lax.rem(dp, RING)
        self.x, self.core = lax.div(tensor, 2), lax.rem(tensor, 2)

    def yi(self, k):
        return lax.rem(self.y + k, RING)

    def zi(self, k):
        return lax.rem(self.z + k, RING)

    def xi(self, k):
        return lax.rem(self.x + k, RING)

    def ydev(self, k):
        return {"dp": self.z * RING + self.yi(k)}

    def zdev(self, k):
        return {"dp": self.zi(k) * RING + self.y}

    def xdev(self, k):
        return {"tensor": self.xi(k) * 2 + self.core}

    def sibling(self):
        return {"tensor": self.x * 2 + 1 - self.core}

    def across(self):
        return {"section": 1 - self.section}


def enter(devices):
    barrier = pltpu.get_barrier_semaphore()
    for device in devices:
        pl.semaphore_signal(barrier, inc=1, device_id=device, device_id_type=MESH_ID)
    pl.semaphore_wait(barrier, len(devices))


def send(src, dst, sems, index, device):
    return pltpu.make_async_remote_copy(
        src_ref=src,
        dst_ref=dst,
        send_sem=sems[0].at[index],
        recv_sem=sems[1].at[index],
        device_id=device,
        device_id_type=MESH_ID,
    )


class Spread:
    def __init__(self, at, tokens, h, sems):
        self.right, self.left, self.far = at.xi(1), at.xi(3), at.xi(2)

        def rows(xx, start, count):
            return tokens.at[2 * at.core + h, pl.ds(xx * ROWS + start, count)]

        def block(xx):
            return rows(xx, 0, ROWS)

        def same(ref, index, device):
            return send(ref, ref, sems, (h, index), device)

        half = ROWS // 2
        self.out = [
            same(block(at.x), 0, at.xdev(1)),
            same(block(at.x), 1, at.xdev(3)),
            same(block(at.x), 2, at.sibling()),
        ]
        self.after_left = [
            same(rows(self.left, 0, half), 3, at.xdev(1)),
            same(block(self.left), 4, at.sibling()),
        ]
        self.after_right = [
            same(rows(self.right, half, half), 5, at.xdev(3)),
            same(block(self.right), 6, at.sibling()),
        ]
        self.last = [same(block(self.far), 7, at.sibling())]

    def start(self):
        for copy in self.out:
            copy.start()

    def onward(self):
        self.out[0].wait_recv()
        for copy in self.after_left:
            copy.start()
        self.out[1].wait_recv()
        for copy in self.after_right:
            copy.start()

    def end(self):
        self.after_left[0].wait_recv()
        self.after_right[0].wait_recv()
        self.last[0].start()

    def finish(self):
        for copy in (self.out[2], self.after_left[1], self.after_right[1], self.last[0]):
            copy.wait_recv()

    def copies(self):
        return [*self.out, *self.after_left, *self.after_right, *self.last]


class Scatter:
    def __init__(self, at, part, pair, total, first, second, h, sems):
        self.at, self.part, self.pair, self.h = at, part, pair, h
        self.total, self.first, self.second = total, first, second
        self.mine, other = 2 * at.core + h, 2 * (1 - at.core) + h
        self.right, self.left, self.far = at.xi(1), at.xi(3), at.xi(2)
        self.half = ROWS // 2

        def to(src, dst, index, device):
            return send(src, dst, sems, (h, index), device)

        self.shares = [
            to(part.at[other, self.rows(xx)], pair.at[h, self.rows(xx)], i, at.sibling())
            for i, xx in enumerate((self.far, self.right, self.left, at.x))
        ]
        self.ones = [
            to(total.at[h, pl.ds(self.far * ROWS, self.half)], first.at[h, 0], 4, at.xdev(1)),
            to(total.at[h, pl.ds(self.far * ROWS + self.half, self.half)], first.at[h, 1], 5, at.xdev(3)),
        ]
        self.twos = [
            to(total.at[h, self.rows(self.right)], second.at[h, 0], 6, at.xdev(1)),
            to(total.at[h, self.rows(self.left)], second.at[h, 1], 7, at.xdev(3)),
        ]

    def rows(self, xx):
        return pl.ds(xx * ROWS, ROWS)

    def summed(self, i, xx):
        self.shares[i].wait_recv()
        return self.part[self.mine, self.rows(xx)].astype(F32) + self.pair[self.h, self.rows(xx)].astype(F32)

    def start(self):
        for copy in self.shares:
            copy.start()

    def step_one(self):
        self.total[self.h, self.rows(self.far)] = self.summed(0, self.far).astype(BF)
        for copy in self.ones:
            copy.start()

    def step_two(self):
        half = self.half
        value = self.summed(1, self.right)
        self.ones[0].wait_recv()
        added = value[:half] + self.first[self.h, 0].astype(F32)
        self.total[self.h, self.rows(self.right)] = jnp.concatenate([added, value[half:]], axis=0).astype(BF)
        self.twos[0].start()
        value = self.summed(2, self.left)
        self.ones[1].wait_recv()
        added = value[half:] + self.first[self.h, 1].astype(F32)
        self.total[self.h, self.rows(self.left)] = jnp.concatenate([value[:half], added], axis=0).astype(BF)
        self.twos[1].start()

    def result(self):
        own = self.summed(3, self.at.x)
        for copy in self.twos:
            copy.wait_recv()
        return own + self.second[self.h, 0].astype(F32) + self.second[self.h, 1].astype(F32)

    def copies(self):
        return [*self.shares, *self.ones, *self.twos]


class Reduce:
    def __init__(self, at, part, first, second, third, sems, hand):
        self.at = at
        self.part, self.first, self.second, self.third = part, first, second, third
        self.sems_one, self.sems_two, self.sems_three = sems
        self.hand = hand

    def ones(self, c):
        far = self.at.yi(2)
        low, high = pl.ds(0, GROUP // 2), pl.ds(GROUP // 2, GROUP // 2)
        return (
            send(self.part.at[c, far, low], self.first.at[c, 0], self.sems_one, (c, 0), self.at.ydev(1)),
            send(self.part.at[c, far, high], self.first.at[c, 1], self.sems_one, (c, 1), self.at.ydev(3)),
        )

    def twos(self, c):
        return (
            send(self.part.at[c, self.at.yi(1)], self.second.at[c, 0], self.sems_two, (c, 0), self.at.ydev(1)),
            send(self.part.at[c, self.at.yi(3)], self.second.at[c, 1], self.sems_two, (c, 1), self.at.ydev(3)),
        )

    def threes(self, c):
        return [
            send(
                self.part.at[c, self.at.y, rows], self.third.at[c, slot], self.sems_three, (c, slot), device
            )
            for slot, rows, device in self.hand
        ]

    def far(self, c, product):
        self.part[c, self.at.yi(2)] = product(c, self.at.yi(2)).astype(BF)
        for copy in self.ones(c):
            copy.start()

    def near(self, c, product):
        half = GROUP // 2
        one, two = self.ones(c), self.twos(c)
        right, left = self.at.yi(1), self.at.yi(3)
        value = product(c, right)
        one[0].wait_recv()
        self.part[c, right, 0:half] = (value[:half] + self.first[c, 0].astype(F32)).astype(BF)
        self.part[c, right, half:GROUP] = value[half:].astype(BF)
        two[0].start()
        value = product(c, left)
        one[1].wait_recv()
        self.part[c, left, 0:half] = value[:half].astype(BF)
        self.part[c, left, half:GROUP] = (value[half:] + self.first[c, 1].astype(F32)).astype(BF)
        two[1].start()

    def own(self, c, product):
        value = product(c, self.at.y)
        for copy in self.twos(c):
            copy.wait_recv()
        self.part[c, self.at.y] = (
            value + self.second[c, 0].astype(F32) + self.second[c, 1].astype(F32)
        ).astype(BF)
        for copy in self.threes(c):
            copy.start()

    def result(self, c, rows):
        for copy in self.threes(c):
            copy.wait_recv()
        total = self.part[c, self.at.y, rows].astype(F32)
        for slot, _, _ in self.hand:
            total = total + self.third[c, slot].astype(F32)
        return total

    def drain(self, c):
        for copy in (*self.ones(c), *self.twos(c), *self.threes(c)):
            copy.wait_send()


class Gather:
    def __init__(self, at, mine, block, sems):
        self.at, self.mine, self.block = at, mine, block
        self.sems_line, self.sems_ring, self.sems_pass = sems

    def lines(self, c):
        return [send(self.mine(c), self.mine(c), self.sems_line, c, self.at.zdev(2))]

    def rings(self, c):
        block = self.block(c, self.at.y, pl.ds(0, GROUP))
        return [
            send(block, block, self.sems_ring, (c, 0), self.at.ydev(1)),
            send(block, block, self.sems_ring, (c, 1), self.at.ydev(3)),
        ]

    def passes(self, c):
        low = self.block(c, self.at.yi(3), pl.ds(0, GROUP // 2))
        high = self.block(c, self.at.yi(1), pl.ds(GROUP // 2, GROUP // 2))
        return [
            send(low, low, self.sems_pass, (c, 0), self.at.ydev(1)),
            send(high, high, self.sems_pass, (c, 1), self.at.ydev(3)),
        ]

    def line(self, c):
        for copy in self.lines(c):
            copy.start()

    def arrived(self, c):
        for copy in self.lines(c):
            copy.wait_recv()

    def ring(self, c):
        for copy in self.rings(c):
            copy.start()

    def hand_on(self, c):
        for ring, onward in zip(self.rings(c), self.passes(c)):
            ring.wait_recv()
            onward.start()

    def finish(self, c):
        for copy in self.passes(c):
            copy.wait_recv()

    def drain(self, c):
        for copy in (*self.lines(c), *self.rings(c), *self.passes(c)):
            copy.wait_send()


class Squares:
    def __init__(self, at, part, near, mid, far, sems_y, sems_z):
        self.at, self.part, self.near, self.mid, self.far = at, part, near, mid, far
        self.sems_y, self.sems_z = sems_y, sems_z

    def fill(self, yy, wide):
        squared = (wide * wide).astype(BF)
        self.part[yy] = lax.dot_general(
            jnp.ones((8, wide.shape[1]), BF),
            squared,
            (((1,), (1,)), ((), ())),
            preferred_element_type=F32,
        )

    def ys(self):
        return [
            send(self.part.at[self.at.yi(k)], self.near.at[k - 1], self.sems_y, k - 1, self.at.ydev(k))
            for k in (1, 2, 3)
        ]

    def zs(self):
        return [
            send(self.mid, self.far.at[k - 1], self.sems_z, k - 1, self.at.zdev(k)) for k in (1, 2, 3)
        ]

    def start(self):
        for copy in self.ys():
            copy.start()

    def middle(self):
        for copy in self.ys():
            copy.wait_recv()
        self.mid[...] = self.part[self.at.y] + self.near[0] + self.near[1] + self.near[2]
        for copy in self.zs():
            copy.start()

    def scale(self, count, start):
        for copy in self.zs():
            copy.wait_recv()
        total = self.mid[...] + self.far[0] + self.far[1] + self.far[2]
        line = lax.rsqrt(total / WIDTH + EPS)[0:1]
        row = lax.broadcasted_iota(jnp.int32, (count, GROUP), 0)
        lane = lax.broadcasted_iota(jnp.int32, (count, GROUP), 1)
        picked = jnp.where(lane == row + start, jnp.broadcast_to(line, (count, GROUP)), 0.0)
        return jnp.sum(picked, axis=1, keepdims=True)

    def drain(self):
        for copy in (*self.ys(), *self.zs()):
            copy.wait_send()


def scaled(tokens, gain, out, squares, yy):
    wide = tokens[yy].astype(F32)
    squares.fill(yy, wide)
    out[yy] = (wide * gain).astype(BF)


def attention(at, m, spread, gain, spread_weights):
    half = HEAD // 2
    lane = lax.broadcasted_iota(jnp.int32, (1, HEAD), 1)
    base = [m.table[i, pl.ds(ROWS + at.dp, 1), :] for i in range(2)]
    step = [m.table[i, 0:ROWS, :] for i in range(2)]
    cosine = base[0] * step[0] - base[1] * step[1]
    sine = (base[1] * step[0] + base[0] * step[1]) * jnp.where(lane < half, -1.0, 1.0)
    for piece in spread:
        piece.onward()
    for piece in spread:
        piece.end()
    for piece in spread:
        piece.finish()
    pending = [copy for piece in spread for copy in piece.copies()]

    squares = Squares(at, m.ss_part, m.ss_near, m.ss_mid, m.ss_far, m.ssy, m.ssz)
    along = [(k - 1, pl.ds(at.zi(k) * ROWS, ROWS), at.zdev(k)) for k in (2, 1, 3)]
    own_rows = pl.ds(at.z * ROWS, ROWS)
    qs = Reduce(at, m.q_part, m.q_one, m.q_two, m.q_three, (m.q1, m.q2, m.q3), along)
    q_chunks = m.q_part.shape[0]
    q_cols = m.q_part.shape[3]

    def product_q(c, yy):
        columns = m.wq[:, c * q_cols : (c + 1) * q_cols]
        return jnp.dot(m.normed[yy], columns, preferred_element_type=F32)

    def product_k(yy):
        return jnp.dot(m.normed[yy], m.wkv[...], preferred_element_type=F32)

    key_y = [
        send(m.k_part.at[at.yi(k)], m.k_near.at[k - 1], m.k1, k - 1, at.ydev(k)) for k in (2, 1, 3)
    ]
    for k, copy in zip((2, 1, 3), key_y):
        scaled(m.tokens, gain, m.normed, squares, at.yi(k))
        m.k_part[at.yi(k)] = product_k(at.yi(k)).astype(BF)
        copy.start()
    squares.start()
    for c in range(q_chunks):
        qs.far(c, product_q)
    scaled(m.tokens, gain, m.normed, squares, at.y)
    total = product_k(at.y)
    for k, copy in zip((2, 1, 3), key_y):
        copy.wait_recv()
        total = total + m.k_near[k - 1].astype(F32)
    m.k_part[at.y] = total.astype(BF)
    key_z = [
        send(m.k_part.at[at.y, rows], m.k_far.at[slot], m.k2, slot, device)
        for slot, rows, device in along
    ]
    for copy in key_z:
        copy.start()
    squares.middle()
    for c in range(q_chunks):
        qs.near(c, product_q)
    scale = squares.scale(ROWS, at.z * ROWS)

    def rotated(value, cos, sin):
        return value * cos + pltpu.roll(value, half, 1) * sin

    is_key = at.core == 0
    core = at.core
    value = m.k_part[at.y, own_rows].astype(F32)
    for slot, copy in zip((1, 0, 2), key_z):
        copy.wait_recv()
        value = value + m.k_far[slot].astype(F32)
    m.keys[core, at.y, own_rows] = rotated(
        value * scale, jnp.where(is_key, cosine, 1.0), jnp.where(is_key, sine, 0.0)
    ).astype(BF)
    mine = m.keys.at[core, at.y, own_rows]
    lines = [send(mine, mine, m.kl, k - 1, at.zdev(k)) for k in (2, 1, 3)]
    for copy in lines:
        copy.start()
    qs.own(0, product_q)
    for copy in lines:
        copy.wait_recv()
    block = m.keys.at[core, at.y]
    rings = [send(block, block, m.kr, k - 1, at.ydev(k)) for k in (2, 1, 3)]
    shares = [send(block, block, m.kc, 0, at.sibling())]
    for copy in rings + shares:
        copy.start()
    for c in range(1, q_chunks):
        qs.own(c, product_q)
    for k, ring in zip((2, 1, 3), rings):
        ring.wait_recv()
        came = m.keys.at[core, at.yi(RING - k)]
        shares.append(send(came, came, m.kc, k, at.sibling()))
        shares[-1].start()
    pending += key_y + key_z + lines + rings + shares

    per = q_cols // HEAD
    pieces = []
    for c in range(q_chunks):
        queries = qs.result(c, own_rows) * scale
        pieces += [rotated(queries[:, h * HEAD : (h + 1) * HEAD], cosine, sine) for h in range(per)]
    stacked = jnp.concatenate(pieces, axis=0).astype(BF)
    for copy in shares:
        copy.wait_recv()
    row = lax.broadcasted_iota(jnp.int32, (RING * ROWS, GROUP), 0)
    col = lax.broadcasted_iota(jnp.int32, (RING * ROWS, GROUP), 1)
    query_at = lax.rem(row, ROWS) + at.dp * ROWS
    key_at = lax.div(col, ROWS) * GROUP + lax.rem(col, ROWS)
    weight = jnp.zeros((RING * ROWS, 1), F32)
    for yy in range(RING):
        raw = lax.dot_general(
            stacked, m.keys[0, yy], (((1,), (1,)), ((), ())), preferred_element_type=F32
        ) * HEAD ** (-0.5)
        kept = jnp.where(key_at + yy * ROWS <= query_at, jnp.exp(raw), 0.0)
        m.scores[yy] = kept
        weight = weight + jnp.sum(kept, axis=1, keepdims=True)
    mix = jnp.zeros((RING * ROWS, HEAD), F32)
    for yy in range(RING):
        mix = mix + jnp.dot(
            (m.scores[yy] / weight).astype(BF), m.keys[1, yy], preferred_element_type=F32
        )

    def rows_of(yy, k, start=0, count=ROWS):
        return m.mixed.at[yy, pl.ds(at.zi(k) * ROWS + start, count)]

    def rings_of(k):
        block = rows_of(at.y, k)
        return [send(block, block, m.mr, (k, i), at.ydev(way)) for i, way in enumerate((1, 3))]

    def passes_of(k):
        low, high = rows_of(at.yi(3), k, 0, ROWS // 2), rows_of(at.yi(1), k, ROWS // 2, ROWS // 2)
        return [send(low, low, m.mp, (k, 0), at.ydev(1)), send(high, high, m.mp, (k, 1), at.ydev(3))]

    def ring(k):
        for copy in rings_of(k):
            copy.start()

    def hand_on(k):
        for came, onward in zip(rings_of(k), passes_of(k)):
            came.wait_recv()
            onward.start()

    for h in range(RING):
        m.mixed[at.y, own_rows, h * HEAD : (h + 1) * HEAD] = mix[h * ROWS : (h + 1) * ROWS].astype(BF)
    lines_m = {k: send(rows_of(at.y, 0), rows_of(at.y, 0), m.ml, k - 1, at.zdev(k)) for k in (1, 3, 2)}
    for copy in lines_m.values():
        copy.start()
    ring(0)
    before = 0
    for k in (1, 3, 2):
        lines_m[RING - k].wait_recv()
        ring(k)
        hand_on(before)
        before = k
    spread_weights(1)
    hand_on(before)

    def project(yy):
        m.a_part[yy] = jnp.dot(m.mixed[yy], m.wo[...], preferred_element_type=F32).astype(BF)

    project(at.y)
    project(at.yi(1))
    project(at.yi(3))
    for k in range(RING):
        for copy in passes_of(k):
            copy.wait_recv()
    project(at.yi(2))

    def drain():
        for copy in pending + list(lines_m.values()):
            copy.wait_send()
        squares.drain()
        for c in range(q_chunks):
            qs.drain(c)
        for k in range(RING):
            for copy in (*rings_of(k), *passes_of(k)):
                copy.wait_send()

    return drain


def kernel(names, *refs):
    m = types.SimpleNamespace()
    for name, ref in zip(names, refs):
        if name.endswith("_s"):
            setattr(m, name[:-2], [ref])
        elif name.endswith("_r"):
            getattr(m, name[:-2]).append(ref)
        else:
            setattr(m, name, ref)
    at = Place()
    chunks = m.wgu.shape[0]
    side, team = lax.rem(at.z, 2), lax.div(at.z, 2)
    partner = {"dp": (at.z + 1 - 2 * side) * RING + at.y}
    span = chunks * HEAD

    enter(
        [at.ydev(k) for k in (1, 2, 3)]
        + [at.zdev(k) for k in (1, 2, 3)]
        + [at.xdev(1), at.xdev(3), at.sibling(), at.across()]
    )
    own = [(2 * at.core + h, pl.ds(at.x * ROWS, ROWS)) for h in range(2)]
    swaps = [send(m.src.at[h], m.tokens.at[own[h]], m.swap, h, at.across()) for h in range(2)]
    for swap in swaps:
        swap.start()
    loads = [
        pltpu.make_async_copy(*pair, m.local.at[i])
        for i, pair in enumerate(
            (
                (m.gain_attn_hbm, m.gain_attn),
                (m.wkv_hbm.at[at.core, :, pl.ds(at.x * HEAD, HEAD)], m.wkv),
                (m.wq_hbm, m.wq),
                (m.table_hbm, m.table),
                (m.wo_hbm, m.wo),
                (m.gain_ffn_hbm, m.gain_ffn),
            )
        )
    ]
    for load in loads:
        load.start()

    def columns(n, c):
        return pl.ds(pl.multiple_of(n * span + c * HEAD, HEAD), HEAD)

    def kept(c, g):
        return pltpu.make_async_copy(
            m.wgu_hbm.at[g, :, columns(side, c)],
            m.wgu.at[c, side, :, pl.ds(g * HEAD, HEAD)],
            m.keep.at[c, g],
        )

    def given(c, g):
        return send(
            m.wgu_hbm.at[g, :, columns(1 - side, c)],
            m.wgu.at[c, side, :, pl.ds(g * HEAD, HEAD)],
            m.give,
            (c, g),
            partner,
        )

    def down(c):
        return pltpu.make_async_copy(
            m.wd_hbm.at[pl.ds(side * span + c * HEAD, HEAD)], m.wd.at[c, side], m.down.at[c]
        )

    def lent(c):
        return send(
            m.wd_hbm.at[pl.ds((1 - side) * span + c * HEAD, HEAD)], m.wd.at[c, side], m.lend, c, partner
        )

    every = [(c, g) for c in range(chunks) for g in range(2)]
    shares = (every[:SPLIT[0]], every[SPLIT[0]:SPLIT[1]], every[SPLIT[1]:])

    def spread_weights(stage):
        for c, g in shares[stage]:
            given(c, g).start()

    for c, g in every:
        kept(c, g).start()
    for c in range(chunks):
        down(c).start()
    for load in loads:
        load.wait()
    spread = [Spread(at, m.tokens, h, m.gx) for h in range(2)]
    for swap, piece in zip(swaps, spread):
        swap.wait_recv()
        piece.start()
    spread_weights(0)
    drain = attention(at, m, spread, m.gain_attn[...].astype(F32), spread_weights)

    def scatters(part, pair, total, first, second, sems):
        pieces = [Scatter(at, part, pair, total, first, second, h, sems) for h in range(2)]
        for piece in pieces:
            piece.start()
        for piece in pieces:
            piece.step_one()
        for piece in pieces:
            piece.step_two()
        return pieces

    gain = m.gain_ffn[...].astype(F32)
    scatter_a = scatters(m.a_part, m.a_pair, m.a_total, m.a_first, m.a_second, m.ax)
    trades = [
        send(m.f_gained.at[h], m.f_tokens.at[(1, *own[h])], m.trade, h, partner) for h in range(2)
    ]
    near, away = (
        [Spread(at, m.f_tokens.at[i], h, sems) for h in range(2)] for i, sems in enumerate((m.fx, m.gz))
    )
    for h in range(2):
        resid = (m.tokens[own[h]].astype(F32) + scatter_a[h].result()).astype(BF)
        m.f_gained[h] = (resid.astype(F32) * gain).astype(BF)
        trades[h].start()
        m.f_tokens[(0, *own[h])] = resid
        near[h].start()
    spread_weights(2)
    for h in range(2):
        trades[h].wait_recv()
        away[h].start()
        near[h].onward()
    for h in range(2):
        near[h].end()
        away[h].onward()
    for h in range(2):
        away[h].end()
    for h in range(2):
        near[h].finish()
    squares = Squares(at, m.fs_part, m.fs_near, m.fs_mid, m.fs_far, m.fsy, m.fsz)
    for k in (2, 1, 3):
        scaled(m.f_tokens.at[0], gain, m.f_normed, squares, at.yi(k))
    squares.start()
    scaled(m.f_tokens.at[0], gain, m.f_normed, squares, at.y)
    m.acc[...] = jnp.zeros_like(m.acc)
    for h in range(2):
        away[h].finish()

    fellow = [(0, pl.ds((1 - team) * 2 * ROWS, 2 * ROWS), at.zdev(2))]
    own_rows = pl.ds(team * 2 * ROWS, 2 * ROWS)
    hs = Reduce(at, m.h_part, m.h_one, m.h_two, m.h_three, (m.h1, m.h2, m.h3), fellow)
    hg = Gather(
        at,
        lambda c: m.hidden.at[c, at.y, own_rows],
        lambda c, yy, rows: m.hidden.at[c, yy, rows],
        (m.hl, m.hr, m.hp),
    )

    def product(c, yy):
        return jnp.dot(m.f_normed[yy], m.wgu[c, side], preferred_element_type=F32) + jnp.dot(
            m.f_tokens[1, yy], m.wgu[c, 1 - side], preferred_element_type=F32
        )

    def first(c):
        for g in range(2):
            kept(c, g).wait()
            given(c, g).wait_recv()
        hs.far(c, product)
        lent(c).start()

    def activate(c):
        both = hs.result(c, own_rows) * m.scale[...]
        gate, up = both[:, :HEAD], both[:, HEAD:]
        m.hidden[c, at.y, own_rows] = (gate / (1.0 + jnp.exp(-gate)) * up).astype(BF)
        hg.line(c)

    def ring(c):
        hg.arrived(c)
        hg.ring(c)

    def add_down(c, k):
        yy = at.yi(k)
        m.acc[0, k] += jnp.dot(m.hidden[c, yy], m.wd[c, side], preferred_element_type=F32)
        m.acc[1, k] += jnp.dot(m.hidden[c, yy], m.wd[c, 1 - side], preferred_element_type=F32)

    def down_near(c):
        down(c).wait()
        lent(c).wait_recv()
        for k in (0, 1, 3):
            add_down(c, k)

    def down_far(c):
        hg.finish(c)
        add_down(c, 2)


    def row_scale():
        m.scale[...] = jnp.broadcast_to(squares.scale(2 * ROWS, team * 2 * ROWS), m.scale.shape)

    once = ((squares.middle, 2), (row_scale, 4))
    stages = (
        (first, 0),
        (lambda c: hs.near(c, product), 2),
        (lambda c: hs.own(c, product), 4),
        (activate, 5),
        (ring, 6),
        (hg.hand_on, 7),
        (down_near, 8),
        (down_far, 9),
    )

    def turn(i, carry):
        for step, when in once:
            pl.when(i == when)(step)
        for stage, lag in stages:
            c = i - lag

            @pl.when((c >= 0) & (c < chunks))
            def _():
                stage(c)

        return carry

    lax.fori_loop(0, chunks + stages[-1][1], turn, 0)
    others = [
        Scatter(at, m.g_part, m.g_pair, m.g_total, m.g_first, m.g_second, h, m.cx) for h in range(2)
    ]
    owns = [
        Scatter(at, m.f_part, m.f_pair, m.f_total, m.f_first, m.f_second, h, m.bx) for h in range(2)
    ]
    for j, part, pieces in ((1, m.g_part, others), (0, m.f_part, owns)):
        for yy, piece in zip((2 * (1 - at.core), 2 * (1 - at.core) + 1), pieces):
            part[yy] = m.acc[j, lax.rem(yy - at.y + RING, RING)].astype(BF)
            piece.start()
        for yy in (2 * at.core, 2 * at.core + 1):
            part[yy] = m.acc[j, lax.rem(yy - at.y + RING, RING)].astype(BF)
    for piece in others:
        piece.step_one()
    for piece in owns:
        piece.step_one()
    for piece in others:
        piece.step_two()
    for piece in owns:
        piece.step_two()
    backs = [send(m.back_out.at[h], m.back_in.at[h], m.back, h, partner) for h in range(2)]
    for h in range(2):
        m.back_out[h] = others[h].result().astype(BF)
        backs[h].start()
    for h in range(2):
        value = m.f_tokens[(0, *own[h])].astype(F32) + owns[h].result()
        backs[h].wait_recv()
        m.out[h] = (value + m.back_in[h].astype(F32)).astype(BF)

    def each(body):
        lax.fori_loop(0, chunks, lambda c, carry: (body(c), carry)[1], 0)

    drain()
    for copy in swaps + trades + backs:
        copy.wait_send()
    for piece in near + away + scatter_a + others + owns:
        for copy in piece.copies():
            copy.wait_send()
    squares.drain()
    each(hs.drain)
    each(hg.drain)

    def drain_given(c):
        for g in range(2):
            given(c, g).wait_send()
        lent(c).wait_send()

    each(drain_given)


def reduce_scratch(name, chunks, columns, slots, rows):
    return {
        name + "_part": pltpu.VMEM((chunks, RING, GROUP, columns), BF),
        name + "_one": pltpu.VMEM((chunks, 2, GROUP // 2, columns), BF),
        name + "_two": pltpu.VMEM((chunks, 2, GROUP, columns), BF),
        name + "_three": pltpu.VMEM((chunks, slots, rows, columns), BF),
    }


def square_scratch(name):
    return {
        name + "_part": pltpu.VMEM((RING, 8, GROUP), F32),
        name + "_near": pltpu.VMEM((3, 8, GROUP), F32),
        name + "_mid": pltpu.VMEM((8, GROUP), F32),
        name + "_far": pltpu.VMEM((3, 8, GROUP), F32),
    }


def scatter_scratch(name, columns):
    return {
        name + "_part": pltpu.VMEM((RING, GROUP, columns), BF),
        name + "_pair": pltpu.VMEM((2, GROUP, columns), BF),
        name + "_total": pltpu.VMEM((2, GROUP, columns), BF),
        name + "_first": pltpu.VMEM((2, 2, ROWS // 2, columns), BF),
        name + "_second": pltpu.VMEM((2, 2, ROWS, columns), BF),
    }


def scratch(cols, heads, chunks, q_chunks):
    wide = 2 * HEAD
    buffers = {
        "gain_attn": pltpu.VMEM((1, cols), BF),
        "gain_ffn": pltpu.VMEM((1, cols), BF),
        "table": pltpu.VMEM((2, ROWS + RING * RING, HEAD), F32),
        "tokens": pltpu.VMEM((RING, GROUP, cols), BF),
        "normed": pltpu.VMEM((RING, GROUP, cols), BF),
        "wq": pltpu.VMEM((cols, heads), BF),
        "wkv": pltpu.VMEM((cols, HEAD), BF),
        "wo": pltpu.VMEM((heads, cols), BF),
        **reduce_scratch("q", q_chunks, heads // q_chunks, 3, ROWS),
        "k_part": pltpu.VMEM((RING, GROUP, HEAD), BF),
        "k_near": pltpu.VMEM((3, GROUP, HEAD), BF),
        "k_far": pltpu.VMEM((3, ROWS, HEAD), BF),
        **square_scratch("ss"),
        "keys": pltpu.VMEM((2, RING, GROUP, HEAD), BF),
        "mixed": pltpu.VMEM((RING, GROUP, heads), BF),
        "scores": pltpu.VMEM((RING, RING * ROWS, GROUP), F32),
        **scatter_scratch("a", cols),
        "f_gained": pltpu.VMEM((2, ROWS, cols), BF),
        "f_tokens": pltpu.VMEM((2, RING, GROUP, cols), BF),
        "f_normed": pltpu.VMEM((RING, GROUP, cols), BF),
        "wgu": pltpu.VMEM((chunks, 2, cols, wide), BF),
        "wd": pltpu.VMEM((chunks, 2, HEAD, cols), BF),
        **reduce_scratch("h", chunks, wide, 1, 2 * ROWS),
        **square_scratch("fs"),
        "scale": pltpu.VMEM((2 * ROWS, wide), F32),
        "hidden": pltpu.VMEM((chunks, RING, GROUP, HEAD), BF),
        "acc": pltpu.VMEM((2, RING, GROUP, cols), F32),
        **scatter_scratch("f", cols),
        **scatter_scratch("g", cols),
        "back_out": pltpu.VMEM((2, ROWS, cols), BF),
        "back_in": pltpu.VMEM((2, ROWS, cols), BF),
    }
    single = {"local": (6,), "keep": (chunks, 2), "down": (chunks,)}
    double = {
        "give": (chunks, 2), "lend": (chunks,), "back": (2,), "cx": (2, 8), "swap": (2,), "trade": (2,),
        "gx": (2, 8), "fx": (2, 8), "gz": (2, 8), "ax": (2, 8), "bx": (2, 8),
        "ssy": (3,), "ssz": (3,), "fsy": (3,), "fsz": (3,),
        "q1": (q_chunks, 2), "q2": (q_chunks, 2), "q3": (q_chunks, 3),
        "k1": (3,), "k2": (3,), "kl": (3,), "kr": (3,), "kc": (4,),
        "ml": (3,), "mr": (RING, 2), "mp": (RING, 2),
        "h1": (chunks, 2), "h2": (chunks, 2), "h3": (chunks, 1),
        "hl": (chunks,), "hr": (chunks, 2), "hp": (chunks, 2),
    }
    for name, shape in single.items():
        buffers[name] = pltpu.SemaphoreType.DMA(shape)
    for name, shape in double.items():
        buffers[name + "_s"] = pltpu.SemaphoreType.DMA(shape)
        buffers[name + "_r"] = pltpu.SemaphoreType.DMA(shape)
    return buffers


def rotary_table(count):
    freq = np.exp(-(2.0 * np.arange(HEAD // 2) / HEAD) * math.log(THETA))
    position = np.concatenate([np.arange(ROWS), np.arange(count) * ROWS]).astype(np.float64)
    angle = position[:, None] * np.concatenate([freq, freq])[None, :]
    return np.stack([np.cos(angle), np.sin(angle)]).astype(np.float32)


def local_layer(
    section_input, gain_attn, w_query, key_value_weight, w_output, gain_ffn, w_gate_up, w_down
):
    cols = section_input.shape[2]
    heads = w_query.shape[2]
    chunks = w_gate_up.shape[3] // (2 * HEAD)
    anywhere = pl.BlockSpec(memory_space=pl.ANY)
    vmem = pl.BlockSpec(memory_space=pltpu.VMEM)
    inputs = {
        "src": (section_input.reshape(2, ROWS, cols), anywhere),
        "gain_attn_hbm": (gain_attn, anywhere),
        "wq_hbm": (w_query[0], anywhere),
        "wkv_hbm": (key_value_weight[0], anywhere),
        "wo_hbm": (w_output[0], anywhere),
        "gain_ffn_hbm": (gain_ffn, anywhere),
        "wgu_hbm": (w_gate_up[0], anywhere),
        "wd_hbm": (w_down[0], anywhere),
        "table_hbm": (jnp.asarray(rotary_table(RING * RING)), anywhere),
    }
    buffers = scratch(cols, heads, chunks, 2)
    result = pl.pallas_call(
        functools.partial(kernel, (*inputs, "out", *buffers)),
        name="layer",
        out_shape=jax.ShapeDtypeStruct((2, ROWS, cols), BF),
        in_specs=[spec for _, spec in inputs.values()],
        out_specs=vmem,
        scratch_shapes=list(buffers.values()),
        compiler_params=pltpu.CompilerParams(
            collective_id=0, has_side_effects=True, vmem_limit_bytes=60 * 1024 * 1024
        ),
    )(*[array for array, _ in inputs.values()])
    return result.reshape(1, 2 * ROWS, cols)


def solution(mesh):
    placed = (
        P("section", "tensor", "dp"),
        P("section", "dp"),
        P("section", "dp", "tensor"),
        P("section", None, "dp", None),
        P("section", "tensor", "dp"),
        P("section", "dp"),
        P("section", None, "dp", "tensor"),
        P("section", "tensor", "dp"),
    )
    return jax.shard_map(
        local_layer, mesh=mesh, in_specs=placed, out_specs=P("section", "tensor", "dp"), check_vma=False
    )
```

```python
import functools
import math
import types

import jax
import jax.numpy as jnp
import numpy as np
from jax import lax
from jax.experimental import pallas as pl
from jax.experimental.pallas import tpu as pltpu
from jax.sharding import PartitionSpec as P

HEAD = 128
EPS = 1e-05
THETA = 500000.0
RING = 4
ROWS = 64
GROUP = RING * ROWS
WIDTH = 8192
SPLIT = (5, 10)

MESH_ID = pl.DeviceIdType.MESH
BF = jnp.bfloat16
F32 = jnp.float32


class Place:
    def __init__(self):
        self.section = lax.axis_index("section")
        dp = lax.axis_index("dp")
        tensor = lax.axis_index("tensor")
        self.dp = dp
        self.z, self.y = lax.div(dp, RING), lax.rem(dp, RING)
        self.x, self.core = lax.div(tensor, 2), lax.rem(tensor, 2)

    def yi(self, k):
        return lax.rem(self.y + k, RING)

    def zi(self, k):
        return lax.rem(self.z + k, RING)

    def xi(self, k):
        return lax.rem(self.x + k, RING)

    def ydev(self, k):
        return {"dp": self.z * RING + self.yi(k)}

    def zdev(self, k):
        return {"dp": self.zi(k) * RING + self.y}

    def xdev(self, k):
        return {"tensor": self.xi(k) * 2 + self.core}

    def sibling(self):
        return {"tensor": self.x * 2 + 1 - self.core}

    def across(self):
        return {"section": 1 - self.section}


def enter(devices):
    barrier = pltpu.get_barrier_semaphore()
    for device in devices:
        pl.semaphore_signal(barrier, inc=1, device_id=device, device_id_type=MESH_ID)
    pl.semaphore_wait(barrier, len(devices))


def send(src, dst, sems, index, device):
    return pltpu.make_async_remote_copy(
        src_ref=src,
        dst_ref=dst,
        send_sem=sems[0].at[index],
        recv_sem=sems[1].at[index],
        device_id=device,
        device_id_type=MESH_ID,
    )


class Spread:
    def __init__(self, at, tokens, h, sems):
        self.right, self.left, self.far = at.xi(1), at.xi(3), at.xi(2)

        def rows(xx, start, count):
            return tokens.at[2 * at.core + h, pl.ds(xx * ROWS + start, count)]

        def block(xx):
            return rows(xx, 0, ROWS)

        def same(ref, index, device):
            return send(ref, ref, sems, (h, index), device)

        half = ROWS // 2
        self.out = [
            same(block(at.x), 0, at.xdev(1)),
            same(block(at.x), 1, at.xdev(3)),
            same(block(at.x), 2, at.sibling()),
        ]
        self.after_left = [
            same(rows(self.left, 0, half), 3, at.xdev(1)),
            same(block(self.left), 4, at.sibling()),
        ]
        self.after_right = [
            same(rows(self.right, half, half), 5, at.xdev(3)),
            same(block(self.right), 6, at.sibling()),
        ]
        self.last = [same(block(self.far), 7, at.sibling())]

    def start(self):
        for copy in self.out:
            copy.start()

    def onward(self):
        self.out[0].wait_recv()
        for copy in self.after_left:
            copy.start()
        self.out[1].wait_recv()
        for copy in self.after_right:
            copy.start()

    def end(self):
        self.after_left[0].wait_recv()
        self.after_right[0].wait_recv()
        self.last[0].start()

    def finish(self):
        for copy in (self.out[2], self.after_left[1], self.after_right[1], self.last[0]):
            copy.wait_recv()

    def copies(self):
        return [*self.out, *self.after_left, *self.after_right, *self.last]


class Scatter:
    def __init__(self, at, part, pair, total, first, second, h, sems):
        self.at, self.part, self.pair, self.h = at, part, pair, h
        self.total, self.first, self.second = total, first, second
        self.mine, other = 2 * at.core + h, 2 * (1 - at.core) + h
        self.right, self.left, self.far = at.xi(1), at.xi(3), at.xi(2)
        self.half = ROWS // 2

        def to(src, dst, index, device):
            return send(src, dst, sems, (h, index), device)

        self.shares = [
            to(part.at[other, self.rows(xx)], pair.at[h, self.rows(xx)], i, at.sibling())
            for i, xx in enumerate((self.far, self.right, self.left, at.x))
        ]
        self.ones = [
            to(total.at[h, pl.ds(self.far * ROWS, self.half)], first.at[h, 0], 4, at.xdev(1)),
            to(total.at[h, pl.ds(self.far * ROWS + self.half, self.half)], first.at[h, 1], 5, at.xdev(3)),
        ]
        self.twos = [
            to(total.at[h, self.rows(self.right)], second.at[h, 0], 6, at.xdev(1)),
            to(total.at[h, self.rows(self.left)], second.at[h, 1], 7, at.xdev(3)),
        ]

    def rows(self, xx):
        return pl.ds(xx * ROWS, ROWS)

    def summed(self, i, xx):
        self.shares[i].wait_recv()
        return self.part[self.mine, self.rows(xx)].astype(F32) + self.pair[self.h, self.rows(xx)].astype(F32)

    def start(self):
        for copy in self.shares:
            copy.start()

    def step_one(self):
        self.total[self.h, self.rows(self.far)] = self.summed(0, self.far).astype(BF)
        for copy in self.ones:
            copy.start()

    def step_two(self):
        half = self.half
        value = self.summed(1, self.right)
        self.ones[0].wait_recv()
        added = value[:half] + self.first[self.h, 0].astype(F32)
        self.total[self.h, self.rows(self.right)] = jnp.concatenate([added, value[half:]], axis=0).astype(BF)
        self.twos[0].start()
        value = self.summed(2, self.left)
        self.ones[1].wait_recv()
        added = value[half:] + self.first[self.h, 1].astype(F32)
        self.total[self.h, self.rows(self.left)] = jnp.concatenate([value[:half], added], axis=0).astype(BF)
        self.twos[1].start()

    def result(self):
        own = self.summed(3, self.at.x)
        for copy in self.twos:
            copy.wait_recv()
        return own + self.second[self.h, 0].astype(F32) + self.second[self.h, 1].astype(F32)

    def copies(self):
        return [*self.shares, *self.ones, *self.twos]


class Reduce:
    def __init__(self, at, part, first, second, third, sems, hand):
        self.at = at
        self.part, self.first, self.second, self.third = part, first, second, third
        self.sems_one, self.sems_two, self.sems_three = sems
        self.hand = hand

    def ones(self, c):
        far = self.at.yi(2)
        low, high = pl.ds(0, GROUP // 2), pl.ds(GROUP // 2, GROUP // 2)
        return (
            send(self.part.at[c, far, low], self.first.at[c, 0], self.sems_one, (c, 0), self.at.ydev(1)),
            send(self.part.at[c, far, high], self.first.at[c, 1], self.sems_one, (c, 1), self.at.ydev(3)),
        )

    def twos(self, c):
        return (
            send(self.part.at[c, self.at.yi(1)], self.second.at[c, 0], self.sems_two, (c, 0), self.at.ydev(1)),
            send(self.part.at[c, self.at.yi(3)], self.second.at[c, 1], self.sems_two, (c, 1), self.at.ydev(3)),
        )

    def threes(self, c):
        return [
            send(
                self.part.at[c, self.at.y, rows], self.third.at[c, slot], self.sems_three, (c, slot), device
            )
            for slot, rows, device in self.hand
        ]

    def far(self, c, product):
        self.part[c, self.at.yi(2)] = product(c, self.at.yi(2)).astype(BF)
        for copy in self.ones(c):
            copy.start()

    def near(self, c, product):
        half = GROUP // 2
        one, two = self.ones(c), self.twos(c)
        right, left = self.at.yi(1), self.at.yi(3)
        value = product(c, right)
        one[0].wait_recv()
        self.part[c, right, 0:half] = (value[:half] + self.first[c, 0].astype(F32)).astype(BF)
        self.part[c, right, half:GROUP] = value[half:].astype(BF)
        two[0].start()
        value = product(c, left)
        one[1].wait_recv()
        self.part[c, left, 0:half] = value[:half].astype(BF)
        self.part[c, left, half:GROUP] = (value[half:] + self.first[c, 1].astype(F32)).astype(BF)
        two[1].start()

    def own(self, c, product):
        value = product(c, self.at.y)
        for copy in self.twos(c):
            copy.wait_recv()
        self.part[c, self.at.y] = (
            value + self.second[c, 0].astype(F32) + self.second[c, 1].astype(F32)
        ).astype(BF)
        for copy in self.threes(c):
            copy.start()

    def result(self, c, rows):
        for copy in self.threes(c):
            copy.wait_recv()
        total = self.part[c, self.at.y, rows].astype(F32)
        for slot, _, _ in self.hand:
            total = total + self.third[c, slot].astype(F32)
        return total

    def drain(self, c):
        for copy in (*self.ones(c), *self.twos(c), *self.threes(c)):
            copy.wait_send()


class Gather:
    def __init__(self, at, mine, block, sems):
        self.at, self.mine, self.block = at, mine, block
        self.sems_line, self.sems_ring, self.sems_pass = sems

    def lines(self, c):
        return [send(self.mine(c), self.mine(c), self.sems_line, c, self.at.zdev(2))]

    def rings(self, c):
        block = self.block(c, self.at.y, pl.ds(0, GROUP))
        return [
            send(block, block, self.sems_ring, (c, 0), self.at.ydev(1)),
            send(block, block, self.sems_ring, (c, 1), self.at.ydev(3)),
        ]

    def passes(self, c):
        low = self.block(c, self.at.yi(3), pl.ds(0, GROUP // 2))
        high = self.block(c, self.at.yi(1), pl.ds(GROUP // 2, GROUP // 2))
        return [
            send(low, low, self.sems_pass, (c, 0), self.at.ydev(1)),
            send(high, high, self.sems_pass, (c, 1), self.at.ydev(3)),
        ]

    def line(self, c):
        for copy in self.lines(c):
            copy.start()

    def arrived(self, c):
        for copy in self.lines(c):
            copy.wait_recv()

    def ring(self, c):
        for copy in self.rings(c):
            copy.start()

    def hand_on(self, c):
        for ring, onward in zip(self.rings(c), self.passes(c)):
            ring.wait_recv()
            onward.start()

    def finish(self, c):
        for copy in self.passes(c):
            copy.wait_recv()

    def drain(self, c):
        for copy in (*self.lines(c), *self.rings(c), *self.passes(c)):
            copy.wait_send()


class Squares:
    def __init__(self, at, part, near, mid, far, sems_y, sems_z):
        self.at, self.part, self.near, self.mid, self.far = at, part, near, mid, far
        self.sems_y, self.sems_z = sems_y, sems_z

    def fill(self, yy, wide):
        squared = (wide * wide).astype(BF)
        self.part[yy] = lax.dot_general(
            jnp.ones((8, wide.shape[1]), BF),
            squared,
            (((1,), (1,)), ((), ())),
            preferred_element_type=F32,
        )

    def ys(self):
        return [
            send(self.part.at[self.at.yi(k)], self.near.at[k - 1], self.sems_y, k - 1, self.at.ydev(k))
            for k in (1, 2, 3)
        ]

    def zs(self):
        return [
            send(self.mid, self.far.at[k - 1], self.sems_z, k - 1, self.at.zdev(k)) for k in (1, 2, 3)
        ]

    def start(self):
        for copy in self.ys():
            copy.start()

    def middle(self):
        for copy in self.ys():
            copy.wait_recv()
        self.mid[...] = self.part[self.at.y] + self.near[0] + self.near[1] + self.near[2]
        for copy in self.zs():
            copy.start()

    def scale(self, count, start):
        for copy in self.zs():
            copy.wait_recv()
        total = self.mid[...] + self.far[0] + self.far[1] + self.far[2]
        line = lax.rsqrt(total / WIDTH + EPS)[0:1]
        row = lax.broadcasted_iota(jnp.int32, (count, GROUP), 0)
        lane = lax.broadcasted_iota(jnp.int32, (count, GROUP), 1)
        picked = jnp.where(lane == row + start, jnp.broadcast_to(line, (count, GROUP)), 0.0)
        return jnp.sum(picked, axis=1, keepdims=True)

    def drain(self):
        for copy in (*self.ys(), *self.zs()):
            copy.wait_send()


def scaled(tokens, gain, out, squares, yy):
    wide = tokens[yy].astype(F32)
    squares.fill(yy, wide)
    out[yy] = (wide * gain).astype(BF)


def attention(at, m, spread, gain, spread_weights):
    half = HEAD // 2
    lane = lax.broadcasted_iota(jnp.int32, (1, HEAD), 1)
    base = [m.table[i, pl.ds(ROWS + at.dp, 1), :] for i in range(2)]
    step = [m.table[i, 0:ROWS, :] for i in range(2)]
    cosine = base[0] * step[0] - base[1] * step[1]
    sine = (base[1] * step[0] + base[0] * step[1]) * jnp.where(lane < half, -1.0, 1.0)
    for piece in spread:
        piece.onward()
    for piece in spread:
        piece.end()
    for piece in spread:
        piece.finish()
    pending = [copy for piece in spread for copy in piece.copies()]

    squares = Squares(at, m.ss_part, m.ss_near, m.ss_mid, m.ss_far, m.ssy, m.ssz)
    along = [(k - 1, pl.ds(at.zi(k) * ROWS, ROWS), at.zdev(k)) for k in (2, 1, 3)]
    own_rows = pl.ds(at.z * ROWS, ROWS)
    qs = Reduce(at, m.q_part, m.q_one, m.q_two, m.q_three, (m.q1, m.q2, m.q3), along)
    q_chunks = m.q_part.shape[0]
    q_cols = m.q_part.shape[3]

    def product_q(c, yy):
        columns = m.wq[:, c * q_cols : (c + 1) * q_cols]
        return jnp.dot(m.normed[yy], columns, preferred_element_type=F32)

    def product_k(yy):
        return jnp.dot(m.normed[yy], m.wkv[...], preferred_element_type=F32)

    key_y = [
        send(m.k_part.at[at.yi(k)], m.k_near.at[k - 1], m.k1, k - 1, at.ydev(k)) for k in (2, 1, 3)
    ]
    for k, copy in zip((2, 1, 3), key_y):
        scaled(m.tokens, gain, m.normed, squares, at.yi(k))
        m.k_part[at.yi(k)] = product_k(at.yi(k)).astype(BF)
        copy.start()
    squares.start()
    for c in range(q_chunks):
        qs.far(c, product_q)
    scaled(m.tokens, gain, m.normed, squares, at.y)
    total = product_k(at.y)
    for k, copy in zip((2, 1, 3), key_y):
        copy.wait_recv()
        total = total + m.k_near[k - 1].astype(F32)
    m.k_part[at.y] = total.astype(BF)
    key_z = [
        send(m.k_part.at[at.y, rows], m.k_far.at[slot], m.k2, slot, device)
        for slot, rows, device in along
    ]
    for copy in key_z:
        copy.start()
    squares.middle()
    for c in range(q_chunks):
        qs.near(c, product_q)
    scale = squares.scale(ROWS, at.z * ROWS)

    def rotated(value, cos, sin):
        return value * cos + pltpu.roll(value, half, 1) * sin

    is_key = at.core == 0
    core = at.core
    value = m.k_part[at.y, own_rows].astype(F32)
    for slot, copy in zip((1, 0, 2), key_z):
        copy.wait_recv()
        value = value + m.k_far[slot].astype(F32)
    m.keys[core, at.y, own_rows] = rotated(
        value * scale, jnp.where(is_key, cosine, 1.0), jnp.where(is_key, sine, 0.0)
    ).astype(BF)
    mine = m.keys.at[core, at.y, own_rows]
    lines = [send(mine, mine, m.kl, k - 1, at.zdev(k)) for k in (2, 1, 3)]
    for copy in lines:
        copy.start()
    qs.own(0, product_q)
    for copy in lines:
        copy.wait_recv()
    block = m.keys.at[core, at.y]
    rings = [send(block, block, m.kr, k - 1, at.ydev(k)) for k in (2, 1, 3)]
    shares = [send(block, block, m.kc, 0, at.sibling())]
    for copy in rings + shares:
        copy.start()
    for c in range(1, q_chunks):
        qs.own(c, product_q)
    for k, ring in zip((2, 1, 3), rings):
        ring.wait_recv()
        came = m.keys.at[core, at.yi(RING - k)]
        shares.append(send(came, came, m.kc, k, at.sibling()))
        shares[-1].start()
    pending += key_y + key_z + lines + rings + shares

    per = q_cols // HEAD
    pieces = []
    for c in range(q_chunks):
        queries = qs.result(c, own_rows) * scale
        pieces += [rotated(queries[:, h * HEAD : (h + 1) * HEAD], cosine, sine) for h in range(per)]
    stacked = jnp.concatenate(pieces, axis=0).astype(BF)
    for copy in shares:
        copy.wait_recv()
    row = lax.broadcasted_iota(jnp.int32, (RING * ROWS, GROUP), 0)
    col = lax.broadcasted_iota(jnp.int32, (RING * ROWS, GROUP), 1)
    query_at = lax.rem(row, ROWS) + at.dp * ROWS
    key_at = lax.div(col, ROWS) * GROUP + lax.rem(col, ROWS)
    weight = jnp.zeros((RING * ROWS, 1), F32)
    for yy in range(RING):
        raw = lax.dot_general(
            stacked, m.keys[0, yy], (((1,), (1,)), ((), ())), preferred_element_type=F32
        ) * HEAD ** (-0.5)
        kept = jnp.where(key_at + yy * ROWS <= query_at, jnp.exp(raw), 0.0)
        m.scores[yy] = kept
        weight = weight + jnp.sum(kept, axis=1, keepdims=True)
    mix = jnp.zeros((RING * ROWS, HEAD), F32)
    for yy in range(RING):
        mix = mix + jnp.dot(
            (m.scores[yy] / weight).astype(BF), m.keys[1, yy], preferred_element_type=F32
        )

    def rows_of(yy, k, start=0, count=ROWS):
        return m.mixed.at[yy, pl.ds(at.zi(k) * ROWS + start, count)]

    def rings_of(k):
        block = rows_of(at.y, k)
        return [send(block, block, m.mr, (k, i), at.ydev(way)) for i, way in enumerate((1, 3))]

    def passes_of(k):
        low, high = rows_of(at.yi(3), k, 0, ROWS // 2), rows_of(at.yi(1), k, ROWS // 2, ROWS // 2)
        return [send(low, low, m.mp, (k, 0), at.ydev(1)), send(high, high, m.mp, (k, 1), at.ydev(3))]

    def ring(k):
        for copy in rings_of(k):
            copy.start()

    def hand_on(k):
        for came, onward in zip(rings_of(k), passes_of(k)):
            came.wait_recv()
            onward.start()

    for h in range(RING):
        m.mixed[at.y, own_rows, h * HEAD : (h + 1) * HEAD] = mix[h * ROWS : (h + 1) * ROWS].astype(BF)
    lines_m = {k: send(rows_of(at.y, 0), rows_of(at.y, 0), m.ml, k - 1, at.zdev(k)) for k in (1, 3, 2)}
    for copy in lines_m.values():
        copy.start()
    ring(0)
    before = 0
    for k in (1, 3, 2):
        lines_m[RING - k].wait_recv()
        ring(k)
        hand_on(before)
        before = k
    spread_weights(1)
    hand_on(before)

    def project(yy):
        m.a_part[yy] = jnp.dot(m.mixed[yy], m.wo[...], preferred_element_type=F32).astype(BF)

    project(at.y)
    project(at.yi(1))
    project(at.yi(3))
    for k in range(RING):
        for copy in passes_of(k):
            copy.wait_recv()
    project(at.yi(2))

    def drain():
        for copy in pending + list(lines_m.values()):
            copy.wait_send()
        squares.drain()
        for c in range(q_chunks):
            qs.drain(c)
        for k in range(RING):
            for copy in (*rings_of(k), *passes_of(k)):
                copy.wait_send()

    return drain


def kernel(names, *refs):
    m = types.SimpleNamespace()
    for name, ref in zip(names, refs):
        if name.endswith("_s"):
            setattr(m, name[:-2], [ref])
        elif name.endswith("_r"):
            getattr(m, name[:-2]).append(ref)
        else:
            setattr(m, name, ref)
    at = Place()
    chunks = m.wgu.shape[0]
    side, team = lax.rem(at.z, 2), lax.div(at.z, 2)
    partner = {"dp": (at.z + 1 - 2 * side) * RING + at.y}
    span = chunks * HEAD

    enter(
        [at.ydev(k) for k in (1, 2, 3)]
        + [at.zdev(k) for k in (1, 2, 3)]
        + [at.xdev(1), at.xdev(3), at.sibling(), at.across()]
    )
    own = [(2 * at.core + h, pl.ds(at.x * ROWS, ROWS)) for h in range(2)]
    swaps = [send(m.src.at[h], m.tokens.at[own[h]], m.swap, h, at.across()) for h in range(2)]
    for swap in swaps:
        swap.start()
    loads = [
        pltpu.make_async_copy(*pair, m.local.at[i])
        for i, pair in enumerate(
            (
                (m.gain_attn_hbm, m.gain_attn),
                (m.wkv_hbm.at[at.core, :, pl.ds(at.x * HEAD, HEAD)], m.wkv),
                (m.wq_hbm, m.wq),
                (m.table_hbm, m.table),
                (m.wo_hbm, m.wo),
                (m.gain_ffn_hbm, m.gain_ffn),
            )
        )
    ]
    for load in loads:
        load.start()

    def columns(n, c):
        return pl.ds(pl.multiple_of(n * span + c * HEAD, HEAD), HEAD)

    def kept(c, g):
        return pltpu.make_async_copy(
            m.wgu_hbm.at[g, :, columns(side, c)],
            m.wgu.at[c, side, :, pl.ds(g * HEAD, HEAD)],
            m.keep.at[c, g],
        )

    def given(c, g):
        return send(
            m.wgu_hbm.at[g, :, columns(1 - side, c)],
            m.wgu.at[c, side, :, pl.ds(g * HEAD, HEAD)],
            m.give,
            (c, g),
            partner,
        )

    def down(c):
        return pltpu.make_async_copy(
            m.wd_hbm.at[pl.ds(side * span + c * HEAD, HEAD)], m.wd.at[c, side], m.down.at[c]
        )

    def lent(c):
        return send(
            m.wd_hbm.at[pl.ds((1 - side) * span + c * HEAD, HEAD)], m.wd.at[c, side], m.lend, c, partner
        )

    every = [(c, g) for c in range(chunks) for g in range(2)]
    shares = (every[:SPLIT[0]], every[SPLIT[0]:SPLIT[1]], every[SPLIT[1]:])

    def spread_weights(stage):
        for c, g in shares[stage]:
            given(c, g).start()

    for c, g in every:
        kept(c, g).start()
    for c in range(chunks):
        down(c).start()
    for load in loads:
        load.wait()
    spread = [Spread(at, m.tokens, h, m.gx) for h in range(2)]
    for swap, piece in zip(swaps, spread):
        swap.wait_recv()
        piece.start()
    spread_weights(0)
    drain = attention(at, m, spread, m.gain_attn[...].astype(F32), spread_weights)

    def scatters(part, pair, total, first, second, sems):
        pieces = [Scatter(at, part, pair, total, first, second, h, sems) for h in range(2)]
        for piece in pieces:
            piece.start()
        for piece in pieces:
            piece.step_one()
        for piece in pieces:
            piece.step_two()
        return pieces

    gain = m.gain_ffn[...].astype(F32)
    scatter_a = scatters(m.a_part, m.a_pair, m.a_total, m.a_first, m.a_second, m.ax)
    trades = [
        send(m.f_gained.at[h], m.f_tokens.at[(1, *own[h])], m.trade, h, partner) for h in range(2)
    ]
    near, away = (
        [Spread(at, m.f_tokens.at[i], h, sems) for h in range(2)] for i, sems in enumerate((m.fx, m.gz))
    )
    for h in range(2):
        resid = (m.tokens[own[h]].astype(F32) + scatter_a[h].result()).astype(BF)
        m.f_gained[h] = (resid.astype(F32) * gain).astype(BF)
        trades[h].start()
        m.f_tokens[(0, *own[h])] = resid
        near[h].start()
    spread_weights(2)
    for h in range(2):
        trades[h].wait_recv()
        away[h].start()
        near[h].onward()
    for h in range(2):
        near[h].end()
        away[h].onward()
    for h in range(2):
        away[h].end()
    for h in range(2):
        near[h].finish()
    squares = Squares(at, m.fs_part, m.fs_near, m.fs_mid, m.fs_far, m.fsy, m.fsz)
    for k in (2, 1, 3):
        scaled(m.f_tokens.at[0], gain, m.f_normed, squares, at.yi(k))
    squares.start()
    scaled(m.f_tokens.at[0], gain, m.f_normed, squares, at.y)
    m.acc[...] = jnp.zeros_like(m.acc)
    for h in range(2):
        away[h].finish()

    fellow = [(0, pl.ds((1 - team) * 2 * ROWS, 2 * ROWS), at.zdev(2))]
    own_rows = pl.ds(team * 2 * ROWS, 2 * ROWS)
    hs = Reduce(at, m.h_part, m.h_one, m.h_two, m.h_three, (m.h1, m.h2, m.h3), fellow)
    hg = Gather(
        at,
        lambda c: m.hidden.at[c, at.y, own_rows],
        lambda c, yy, rows: m.hidden.at[c, yy, rows],
        (m.hl, m.hr, m.hp),
    )

    def product(c, yy):
        return jnp.dot(m.f_normed[yy], m.wgu[c, side], preferred_element_type=F32) + jnp.dot(
            m.f_tokens[1, yy], m.wgu[c, 1 - side], preferred_element_type=F32
        )

    def first(c):
        for g in range(2):
            kept(c, g).wait()
            given(c, g).wait_recv()
        hs.far(c, product)
        lent(c).start()

    def activate(c):
        both = hs.result(c, own_rows) * m.scale[...]
        gate, up = both[:, :HEAD], both[:, HEAD:]
        m.hidden[c, at.y, own_rows] = (gate / (1.0 + jnp.exp(-gate)) * up).astype(BF)
        hg.line(c)

    def ring(c):
        hg.arrived(c)
        hg.ring(c)

    def add_down(held, k):
        yy = at.yi(k)
        left = jnp.concatenate([m.hidden[c, yy] for c in held], axis=1)
        for j, half in enumerate((side, 1 - side)):
            right = jnp.concatenate([m.wd[c, half] for c in held], axis=0)
            m.acc[j, k] += jnp.dot(left, right, preferred_element_type=F32)

    def by_pairs(c, blocks):
        @pl.when(lax.rem(c, 2) == 1)
        def _():
            for k in blocks:
                add_down((c - 1, c), k)

        if chunks % 2:

            @pl.when(c == chunks - 1)
            def _():
                for k in blocks:
                    add_down((c,), k)

    def down_near(c):
        down(c).wait()
        lent(c).wait_recv()
        by_pairs(c, (0, 1, 3))

    def down_far(c):
        hg.finish(c)
        by_pairs(c, (2,))

    def row_scale():
        m.scale[...] = jnp.broadcast_to(squares.scale(2 * ROWS, team * 2 * ROWS), m.scale.shape)

    once = ((squares.middle, 2), (row_scale, 4))
    stages = (
        (first, 0),
        (lambda c: hs.near(c, product), 2),
        (lambda c: hs.own(c, product), 3),
        (activate, 4),
        (ring, 5),
        (hg.hand_on, 6),
        (down_near, 7),
        (down_far, 8),
    )

    def turn(i, carry):
        for step, when in once:
            pl.when(i == when)(step)
        for stage, lag in stages:
            c = i - lag

            @pl.when((c >= 0) & (c < chunks))
            def _():
                stage(c)

        return carry

    lax.fori_loop(0, chunks + stages[-1][1], turn, 0)
    others = [
        Scatter(at, m.g_part, m.g_pair, m.g_total, m.g_first, m.g_second, h, m.cx) for h in range(2)
    ]
    owns = [
        Scatter(at, m.f_part, m.f_pair, m.f_total, m.f_first, m.f_second, h, m.bx) for h in range(2)
    ]
    for j, part, pieces in ((1, m.g_part, others), (0, m.f_part, owns)):
        for yy, piece in zip((2 * (1 - at.core), 2 * (1 - at.core) + 1), pieces):
            part[yy] = m.acc[j, lax.rem(yy - at.y + RING, RING)].astype(BF)
            piece.start()
        for yy in (2 * at.core, 2 * at.core + 1):
            part[yy] = m.acc[j, lax.rem(yy - at.y + RING, RING)].astype(BF)
    for piece in others:
        piece.step_one()
    for piece in owns:
        piece.step_one()

    def drain_chunk(c, carry):
        hs.drain(c)
        hg.drain(c)
        for g in range(2):
            given(c, g).wait_send()
        lent(c).wait_send()
        return carry

    drain()
    for copy in swaps + trades:
        copy.wait_send()
    for piece in near + away + scatter_a:
        for copy in piece.copies():
            copy.wait_send()
    squares.drain()
    lax.fori_loop(0, chunks, drain_chunk, 0)
    for piece in others:
        piece.step_two()
    for piece in owns:
        piece.step_two()
    backs = [send(m.back_out.at[h], m.back_in.at[h], m.back, h, partner) for h in range(2)]
    for h in range(2):
        m.back_out[h] = others[h].result().astype(BF)
        backs[h].start()
    for h in range(2):
        value = m.f_tokens[(0, *own[h])].astype(F32) + owns[h].result()
        backs[h].wait_recv()
        m.out[h] = (value + m.back_in[h].astype(F32)).astype(BF)

    for copy in backs:
        copy.wait_send()
    for piece in others + owns:
        for copy in piece.copies():
            copy.wait_send()


def reduce_scratch(name, chunks, columns, slots, rows):
    return {
        name + "_part": pltpu.VMEM((chunks, RING, GROUP, columns), BF),
        name + "_one": pltpu.VMEM((chunks, 2, GROUP // 2, columns), BF),
        name + "_two": pltpu.VMEM((chunks, 2, GROUP, columns), BF),
        name + "_three": pltpu.VMEM((chunks, slots, rows, columns), BF),
    }


def square_scratch(name):
    return {
        name + "_part": pltpu.VMEM((RING, 8, GROUP), F32),
        name + "_near": pltpu.VMEM((3, 8, GROUP), F32),
        name + "_mid": pltpu.VMEM((8, GROUP), F32),
        name + "_far": pltpu.VMEM((3, 8, GROUP), F32),
    }


def scatter_scratch(name, columns):
    return {
        name + "_part": pltpu.VMEM((RING, GROUP, columns), BF),
        name + "_pair": pltpu.VMEM((2, GROUP, columns), BF),
        name + "_total": pltpu.VMEM((2, GROUP, columns), BF),
        name + "_first": pltpu.VMEM((2, 2, ROWS // 2, columns), BF),
        name + "_second": pltpu.VMEM((2, 2, ROWS, columns), BF),
    }


def scratch(cols, heads, chunks, q_chunks):
    wide = 2 * HEAD
    buffers = {
        "gain_attn": pltpu.VMEM((1, cols), BF),
        "gain_ffn": pltpu.VMEM((1, cols), BF),
        "table": pltpu.VMEM((2, ROWS + RING * RING, HEAD), F32),
        "tokens": pltpu.VMEM((RING, GROUP, cols), BF),
        "normed": pltpu.VMEM((RING, GROUP, cols), BF),
        "wq": pltpu.VMEM((cols, heads), BF),
        "wkv": pltpu.VMEM((cols, HEAD), BF),
        "wo": pltpu.VMEM((heads, cols), BF),
        **reduce_scratch("q", q_chunks, heads // q_chunks, 3, ROWS),
        "k_part": pltpu.VMEM((RING, GROUP, HEAD), BF),
        "k_near": pltpu.VMEM((3, GROUP, HEAD), BF),
        "k_far": pltpu.VMEM((3, ROWS, HEAD), BF),
        **square_scratch("ss"),
        "keys": pltpu.VMEM((2, RING, GROUP, HEAD), BF),
        "mixed": pltpu.VMEM((RING, GROUP, heads), BF),
        "scores": pltpu.VMEM((RING, RING * ROWS, GROUP), F32),
        **scatter_scratch("a", cols),
        "f_gained": pltpu.VMEM((2, ROWS, cols), BF),
        "f_tokens": pltpu.VMEM((2, RING, GROUP, cols), BF),
        "f_normed": pltpu.VMEM((RING, GROUP, cols), BF),
        "wgu": pltpu.VMEM((chunks, 2, cols, wide), BF),
        "wd": pltpu.VMEM((chunks, 2, HEAD, cols), BF),
        **reduce_scratch("h", chunks, wide, 1, 2 * ROWS),
        **square_scratch("fs"),
        "scale": pltpu.VMEM((2 * ROWS, wide), F32),
        "hidden": pltpu.VMEM((chunks, RING, GROUP, HEAD), BF),
        "acc": pltpu.VMEM((2, RING, GROUP, cols), F32),
        **scatter_scratch("f", cols),
        **scatter_scratch("g", cols),
        "back_out": pltpu.VMEM((2, ROWS, cols), BF),
        "back_in": pltpu.VMEM((2, ROWS, cols), BF),
    }
    single = {"local": (6,), "keep": (chunks, 2), "down": (chunks,)}
    double = {
        "give": (chunks, 2), "lend": (chunks,), "back": (2,), "cx": (2, 8), "swap": (2,), "trade": (2,),
        "gx": (2, 8), "fx": (2, 8), "gz": (2, 8), "ax": (2, 8), "bx": (2, 8),
        "ssy": (3,), "ssz": (3,), "fsy": (3,), "fsz": (3,),
        "q1": (q_chunks, 2), "q2": (q_chunks, 2), "q3": (q_chunks, 3),
        "k1": (3,), "k2": (3,), "kl": (3,), "kr": (3,), "kc": (4,),
        "ml": (3,), "mr": (RING, 2), "mp": (RING, 2),
        "h1": (chunks, 2), "h2": (chunks, 2), "h3": (chunks, 1),
        "hl": (chunks,), "hr": (chunks, 2), "hp": (chunks, 2),
    }
    for name, shape in single.items():
        buffers[name] = pltpu.SemaphoreType.DMA(shape)
    for name, shape in double.items():
        buffers[name + "_s"] = pltpu.SemaphoreType.DMA(shape)
        buffers[name + "_r"] = pltpu.SemaphoreType.DMA(shape)
    return buffers


def rotary_table(count):
    freq = np.exp(-(2.0 * np.arange(HEAD // 2) / HEAD) * math.log(THETA))
    position = np.concatenate([np.arange(ROWS), np.arange(count) * ROWS]).astype(np.float64)
    angle = position[:, None] * np.concatenate([freq, freq])[None, :]
    return np.stack([np.cos(angle), np.sin(angle)]).astype(np.float32)


def local_layer(
    section_input, gain_attn, w_query, key_value_weight, w_output, gain_ffn, w_gate_up, w_down
):
    cols = section_input.shape[2]
    heads = w_query.shape[2]
    chunks = w_gate_up.shape[3] // (2 * HEAD)
    anywhere = pl.BlockSpec(memory_space=pl.ANY)
    vmem = pl.BlockSpec(memory_space=pltpu.VMEM)
    inputs = {
        "src": (section_input.reshape(2, ROWS, cols), anywhere),
        "gain_attn_hbm": (gain_attn, anywhere),
        "wq_hbm": (w_query[0], anywhere),
        "wkv_hbm": (key_value_weight[0], anywhere),
        "wo_hbm": (w_output[0], anywhere),
        "gain_ffn_hbm": (gain_ffn, anywhere),
        "wgu_hbm": (w_gate_up[0], anywhere),
        "wd_hbm": (w_down[0], anywhere),
        "table_hbm": (jnp.asarray(rotary_table(RING * RING)), anywhere),
    }
    buffers = scratch(cols, heads, chunks, 2)
    result = pl.pallas_call(
        functools.partial(kernel, (*inputs, "out", *buffers)),
        name="layer",
        out_shape=jax.ShapeDtypeStruct((2, ROWS, cols), BF),
        in_specs=[spec for _, spec in inputs.values()],
        out_specs=vmem,
        scratch_shapes=list(buffers.values()),
        compiler_params=pltpu.CompilerParams(
            collective_id=0, has_side_effects=True, vmem_limit_bytes=60 * 1024 * 1024
        ),
    )(*[array for array, _ in inputs.values()])
    return result.reshape(1, 2 * ROWS, cols)


def solution(mesh):
    placed = (
        P("section", "tensor", "dp"),
        P("section", "dp"),
        P("section", "dp", "tensor"),
        P("section", None, "dp", None),
        P("section", "tensor", "dp"),
        P("section", "dp"),
        P("section", None, "dp", "tensor"),
        P("section", "tensor", "dp"),
    )
    return jax.shard_map(
        local_layer, mesh=mesh, in_specs=placed, out_specs=P("section", "tensor", "dp"), check_vma=False
    )
```

```python
import functools
import math
import types

import jax
import jax.numpy as jnp
import numpy as np
from jax import lax
from jax.experimental import pallas as pl
from jax.experimental.pallas import tpu as pltpu
from jax.sharding import PartitionSpec as P

HEAD = 128
EPS = 1e-05
THETA = 500000.0
RING = 4
ROWS = 64
GROUP = RING * ROWS
WIDTH = 8192
SPLIT = (5, 10)

MESH_ID = pl.DeviceIdType.MESH
BF = jnp.bfloat16
F32 = jnp.float32


class Place:
    def __init__(self):
        self.section = lax.axis_index("section")
        dp = lax.axis_index("dp")
        tensor = lax.axis_index("tensor")
        self.dp = dp
        self.z, self.y = lax.div(dp, RING), lax.rem(dp, RING)
        self.x, self.core = lax.div(tensor, 2), lax.rem(tensor, 2)

    def yi(self, k):
        return lax.rem(self.y + k, RING)

    def zi(self, k):
        return lax.rem(self.z + k, RING)

    def xi(self, k):
        return lax.rem(self.x + k, RING)

    def ydev(self, k):
        return {"dp": self.z * RING + self.yi(k)}

    def zdev(self, k):
        return {"dp": self.zi(k) * RING + self.y}

    def xdev(self, k):
        return {"tensor": self.xi(k) * 2 + self.core}

    def sibling(self):
        return {"tensor": self.x * 2 + 1 - self.core}

    def across(self):
        return {"section": 1 - self.section}


def enter(devices):
    barrier = pltpu.get_barrier_semaphore()
    for device in devices:
        pl.semaphore_signal(barrier, inc=1, device_id=device, device_id_type=MESH_ID)
    pl.semaphore_wait(barrier, len(devices))


def send(src, dst, sems, index, device):
    return pltpu.make_async_remote_copy(
        src_ref=src,
        dst_ref=dst,
        send_sem=sems[0].at[index],
        recv_sem=sems[1].at[index],
        device_id=device,
        device_id_type=MESH_ID,
    )


class Spread:
    def __init__(self, at, tokens, h, sems):
        self.right, self.left, self.far = at.xi(1), at.xi(3), at.xi(2)

        def rows(xx, start, count):
            return tokens.at[2 * at.core + h, pl.ds(xx * ROWS + start, count)]

        def block(xx):
            return rows(xx, 0, ROWS)

        def same(ref, index, device):
            return send(ref, ref, sems, (h, index), device)

        half = ROWS // 2
        self.out = [
            same(block(at.x), 0, at.xdev(1)),
            same(block(at.x), 1, at.xdev(3)),
            same(block(at.x), 2, at.sibling()),
        ]
        self.after_left = [
            same(rows(self.left, 0, half), 3, at.xdev(1)),
            same(block(self.left), 4, at.sibling()),
        ]
        self.after_right = [
            same(rows(self.right, half, half), 5, at.xdev(3)),
            same(block(self.right), 6, at.sibling()),
        ]
        self.last = [same(block(self.far), 7, at.sibling())]

    def start(self):
        for copy in self.out:
            copy.start()

    def onward(self):
        self.out[0].wait_recv()
        for copy in self.after_left:
            copy.start()
        self.out[1].wait_recv()
        for copy in self.after_right:
            copy.start()

    def end(self):
        self.after_left[0].wait_recv()
        self.after_right[0].wait_recv()
        self.last[0].start()

    def finish(self):
        for copy in (self.out[2], self.after_left[1], self.after_right[1], self.last[0]):
            copy.wait_recv()

    def copies(self):
        return [*self.out, *self.after_left, *self.after_right, *self.last]


class Scatter:
    def __init__(self, at, part, pair, total, first, second, h, sems):
        self.at, self.part, self.pair, self.h = at, part, pair, h
        self.total, self.first, self.second = total, first, second
        self.mine, other = 2 * at.core + h, 2 * (1 - at.core) + h
        self.other = other
        self.right, self.left, self.far = at.xi(1), at.xi(3), at.xi(2)
        self.half = ROWS // 2

        def to(src, dst, index, device):
            return send(src, dst, sems, (h, index), device)

        self.shares = [
            to(part.at[other, self.rows(xx)], pair.at[h, self.rows(xx)], i, at.sibling())
            for i, xx in enumerate((self.far, self.right, self.left, at.x))
        ]
        self.ones = [
            to(total.at[h, pl.ds(self.far * ROWS, self.half)], first.at[h, 0], 4, at.xdev(1)),
            to(total.at[h, pl.ds(self.far * ROWS + self.half, self.half)], first.at[h, 1], 5, at.xdev(3)),
        ]
        self.twos = [
            to(total.at[h, self.rows(self.right)], second.at[h, 0], 6, at.xdev(1)),
            to(total.at[h, self.rows(self.left)], second.at[h, 1], 7, at.xdev(3)),
        ]

    def rows(self, xx):
        return pl.ds(xx * ROWS, ROWS)

    def summed(self, i, xx):
        self.shares[i].wait_recv()
        return self.part[self.mine, self.rows(xx)].astype(F32) + self.pair[self.h, self.rows(xx)].astype(F32)

    def start(self, late):
        is_far = self.other == self.at.yi(2)

        @pl.when(is_far if late else jnp.logical_not(is_far))
        def _():
            for copy in self.shares:
                copy.start()

    def step_one(self):
        self.total[self.h, self.rows(self.far)] = self.summed(0, self.far).astype(BF)
        for copy in self.ones:
            copy.start()

    def step_two(self):
        half = self.half
        value = self.summed(1, self.right)
        self.ones[0].wait_recv()
        added = value[:half] + self.first[self.h, 0].astype(F32)
        self.total[self.h, self.rows(self.right)] = jnp.concatenate([added, value[half:]], axis=0).astype(BF)
        self.twos[0].start()
        value = self.summed(2, self.left)
        self.ones[1].wait_recv()
        added = value[half:] + self.first[self.h, 1].astype(F32)
        self.total[self.h, self.rows(self.left)] = jnp.concatenate([value[:half], added], axis=0).astype(BF)
        self.twos[1].start()

    def result(self):
        own = self.summed(3, self.at.x)
        for copy in self.twos:
            copy.wait_recv()
        return own + self.second[self.h, 0].astype(F32) + self.second[self.h, 1].astype(F32)

    def copies(self):
        return [*self.shares, *self.ones, *self.twos]


class Reduce:
    def __init__(self, at, part, first, second, third, sems, hand):
        self.at = at
        self.part, self.first, self.second, self.third = part, first, second, third
        self.sems_one, self.sems_two, self.sems_three = sems
        self.hand = hand

    def ones(self, c):
        far = self.at.yi(2)
        low, high = pl.ds(0, GROUP // 2), pl.ds(GROUP // 2, GROUP // 2)
        return (
            send(self.part.at[c, far, low], self.first.at[c, 0], self.sems_one, (c, 0), self.at.ydev(1)),
            send(self.part.at[c, far, high], self.first.at[c, 1], self.sems_one, (c, 1), self.at.ydev(3)),
        )

    def twos(self, c):
        return (
            send(self.part.at[c, self.at.yi(1)], self.second.at[c, 0], self.sems_two, (c, 0), self.at.ydev(1)),
            send(self.part.at[c, self.at.yi(3)], self.second.at[c, 1], self.sems_two, (c, 1), self.at.ydev(3)),
        )

    def threes(self, c):
        return [
            send(
                self.part.at[c, self.at.y, rows], self.third.at[c, slot], self.sems_three, (c, slot), device
            )
            for slot, rows, device in self.hand
        ]

    def far(self, c, product):
        self.part[c, self.at.yi(2)] = product(c, self.at.yi(2)).astype(BF)
        for copy in self.ones(c):
            copy.start()

    def near(self, c, product):
        half = GROUP // 2
        one, two = self.ones(c), self.twos(c)
        right, left = self.at.yi(1), self.at.yi(3)
        value = product(c, right)
        one[0].wait_recv()
        self.part[c, right, 0:half] = (value[:half] + self.first[c, 0].astype(F32)).astype(BF)
        self.part[c, right, half:GROUP] = value[half:].astype(BF)
        two[0].start()
        value = product(c, left)
        one[1].wait_recv()
        self.part[c, left, 0:half] = value[:half].astype(BF)
        self.part[c, left, half:GROUP] = (value[half:] + self.first[c, 1].astype(F32)).astype(BF)
        two[1].start()

    def own(self, c, product):
        value = product(c, self.at.y)
        for copy in self.twos(c):
            copy.wait_recv()
        self.part[c, self.at.y] = (
            value + self.second[c, 0].astype(F32) + self.second[c, 1].astype(F32)
        ).astype(BF)
        for copy in self.threes(c):
            copy.start()

    def result(self, c, rows):
        for copy in self.threes(c):
            copy.wait_recv()
        total = self.part[c, self.at.y, rows].astype(F32)
        for slot, _, _ in self.hand:
            total = total + self.third[c, slot].astype(F32)
        return total

    def drain(self, c):
        for copy in (*self.ones(c), *self.twos(c), *self.threes(c)):
            copy.wait_send()


class Gather:
    def __init__(self, at, mine, block, sems):
        self.at, self.mine, self.block = at, mine, block
        self.sems_line, self.sems_ring, self.sems_pass = sems

    def lines(self, c):
        return [send(self.mine(c), self.mine(c), self.sems_line, c, self.at.zdev(2))]

    def rings(self, c):
        block = self.block(c, self.at.y, pl.ds(0, GROUP))
        return [
            send(block, block, self.sems_ring, (c, 0), self.at.ydev(1)),
            send(block, block, self.sems_ring, (c, 1), self.at.ydev(3)),
        ]

    def passes(self, c):
        low = self.block(c, self.at.yi(3), pl.ds(0, GROUP // 2))
        high = self.block(c, self.at.yi(1), pl.ds(GROUP // 2, GROUP // 2))
        return [
            send(low, low, self.sems_pass, (c, 0), self.at.ydev(1)),
            send(high, high, self.sems_pass, (c, 1), self.at.ydev(3)),
        ]

    def line(self, c):
        for copy in self.lines(c):
            copy.start()

    def arrived(self, c):
        for copy in self.lines(c):
            copy.wait_recv()

    def ring(self, c):
        for copy in self.rings(c):
            copy.start()

    def hand_on(self, c):
        for ring, onward in zip(self.rings(c), self.passes(c)):
            ring.wait_recv()
            onward.start()

    def finish(self, c):
        for copy in self.passes(c):
            copy.wait_recv()

    def drain(self, c):
        for copy in (*self.lines(c), *self.rings(c), *self.passes(c)):
            copy.wait_send()


class Squares:
    def __init__(self, at, part, near, mid, far, sems_y, sems_z):
        self.at, self.part, self.near, self.mid, self.far = at, part, near, mid, far
        self.sems_y, self.sems_z = sems_y, sems_z

    def fill(self, yy, wide):
        squared = (wide * wide).astype(BF)
        self.part[yy] = lax.dot_general(
            jnp.ones((8, wide.shape[1]), BF),
            squared,
            (((1,), (1,)), ((), ())),
            preferred_element_type=F32,
        )

    def ys(self):
        return [
            send(self.part.at[self.at.yi(k)], self.near.at[k - 1], self.sems_y, k - 1, self.at.ydev(k))
            for k in (1, 2, 3)
        ]

    def zs(self):
        return [
            send(self.mid, self.far.at[k - 1], self.sems_z, k - 1, self.at.zdev(k)) for k in (1, 2, 3)
        ]

    def start(self):
        for copy in self.ys():
            copy.start()

    def middle(self):
        for copy in self.ys():
            copy.wait_recv()
        self.mid[...] = self.part[self.at.y] + self.near[0] + self.near[1] + self.near[2]
        for copy in self.zs():
            copy.start()

    def scale(self, count, start):
        for copy in self.zs():
            copy.wait_recv()
        total = self.mid[...] + self.far[0] + self.far[1] + self.far[2]
        line = lax.rsqrt(total / WIDTH + EPS)[0:1]
        row = lax.broadcasted_iota(jnp.int32, (count, GROUP), 0)
        lane = lax.broadcasted_iota(jnp.int32, (count, GROUP), 1)
        picked = jnp.where(lane == row + start, jnp.broadcast_to(line, (count, GROUP)), 0.0)
        return jnp.sum(picked, axis=1, keepdims=True)

    def drain(self):
        for copy in (*self.ys(), *self.zs()):
            copy.wait_send()


def scaled(tokens, gain, out, squares, yy):
    wide = tokens[yy].astype(F32)
    squares.fill(yy, wide)
    out[yy] = (wide * gain).astype(BF)


def attention(at, m, spread, scatter, gain, spread_weights):
    half = HEAD // 2
    lane = lax.broadcasted_iota(jnp.int32, (1, HEAD), 1)
    base = [m.table[i, pl.ds(ROWS + at.dp, 1), :] for i in range(2)]
    step = [m.table[i, 0:ROWS, :] for i in range(2)]
    cosine = base[0] * step[0] - base[1] * step[1]
    sine = (base[1] * step[0] + base[0] * step[1]) * jnp.where(lane < half, -1.0, 1.0)
    for piece in spread:
        piece.onward()
    for piece in spread:
        piece.end()
    for piece in spread:
        piece.finish()
    pending = [copy for piece in spread for copy in piece.copies()]

    squares = Squares(at, m.ss_part, m.ss_near, m.ss_mid, m.ss_far, m.ssy, m.ssz)
    along = [(k - 1, pl.ds(at.zi(k) * ROWS, ROWS), at.zdev(k)) for k in (2, 1, 3)]
    own_rows = pl.ds(at.z * ROWS, ROWS)
    qs = Reduce(at, m.q_part, m.q_one, m.q_two, m.q_three, (m.q1, m.q2, m.q3), along)
    q_chunks = m.q_part.shape[0]
    q_cols = m.q_part.shape[3]

    def product_q(c, yy):
        columns = m.wq[:, c * q_cols : (c + 1) * q_cols]
        return jnp.dot(m.normed[yy], columns, preferred_element_type=F32)

    def product_k(yy):
        return jnp.dot(m.normed[yy], m.wkv[...], preferred_element_type=F32)

    key_y = [
        send(m.k_part.at[at.yi(k)], m.k_near.at[k - 1], m.k1, k - 1, at.ydev(k)) for k in (2, 1, 3)
    ]
    for k, copy in zip((2, 1, 3), key_y):
        scaled(m.tokens, gain, m.normed, squares, at.yi(k))
        m.k_part[at.yi(k)] = product_k(at.yi(k)).astype(BF)
        copy.start()
    squares.start()
    for c in range(q_chunks):
        qs.far(c, product_q)
    scaled(m.tokens, gain, m.normed, squares, at.y)
    total = product_k(at.y)
    for k, copy in zip((2, 1, 3), key_y):
        copy.wait_recv()
        total = total + m.k_near[k - 1].astype(F32)
    m.k_part[at.y] = total.astype(BF)
    key_z = [
        send(m.k_part.at[at.y, rows], m.k_far.at[slot], m.k2, slot, device)
        for slot, rows, device in along
    ]
    for copy in key_z:
        copy.start()
    squares.middle()
    for c in range(q_chunks):
        qs.near(c, product_q)
    scale = squares.scale(ROWS, at.z * ROWS)

    def rotated(value, cos, sin):
        return value * cos + pltpu.roll(value, half, 1) * sin

    is_key = at.core == 0
    core = at.core
    value = m.k_part[at.y, own_rows].astype(F32)
    for slot, copy in zip((1, 0, 2), key_z):
        copy.wait_recv()
        value = value + m.k_far[slot].astype(F32)
    m.keys[core, at.y, own_rows] = rotated(
        value * scale, jnp.where(is_key, cosine, 1.0), jnp.where(is_key, sine, 0.0)
    ).astype(BF)
    mine = m.keys.at[core, at.y, own_rows]
    lines = [send(mine, mine, m.kl, k - 1, at.zdev(k)) for k in (2, 1, 3)]
    for copy in lines:
        copy.start()
    qs.own(0, product_q)
    for copy in lines:
        copy.wait_recv()
    block = m.keys.at[core, at.y]
    rings = [send(block, block, m.kr, k - 1, at.ydev(k)) for k in (2, 1, 3)]
    shares = [send(block, block, m.kc, 0, at.sibling())]
    for copy in rings + shares:
        copy.start()
    for c in range(1, q_chunks):
        qs.own(c, product_q)
    for k, ring in zip((2, 1, 3), rings):
        ring.wait_recv()
        came = m.keys.at[core, at.yi(RING - k)]
        shares.append(send(came, came, m.kc, k, at.sibling()))
        shares[-1].start()
    pending += key_y + key_z + lines + rings + shares

    per = q_cols // HEAD
    pieces = []
    for c in range(q_chunks):
        queries = qs.result(c, own_rows) * scale
        pieces += [rotated(queries[:, h * HEAD : (h + 1) * HEAD], cosine, sine) for h in range(per)]
    stacked = jnp.concatenate(pieces, axis=0).astype(BF)
    for copy in shares:
        copy.wait_recv()
    row = lax.broadcasted_iota(jnp.int32, (RING * ROWS, GROUP), 0)
    col = lax.broadcasted_iota(jnp.int32, (RING * ROWS, GROUP), 1)
    query_at = lax.rem(row, ROWS) + at.dp * ROWS
    key_at = lax.div(col, ROWS) * GROUP + lax.rem(col, ROWS)
    weight = jnp.zeros((RING * ROWS, 1), F32)
    for yy in range(RING):
        raw = lax.dot_general(
            stacked, m.keys[0, yy], (((1,), (1,)), ((), ())), preferred_element_type=F32
        ) * HEAD ** (-0.5)
        kept = jnp.where(key_at + yy * ROWS <= query_at, jnp.exp(raw), 0.0)
        m.scores[yy] = kept
        weight = weight + jnp.sum(kept, axis=1, keepdims=True)
    mix = jnp.zeros((RING * ROWS, HEAD), F32)
    for yy in range(RING):
        mix = mix + jnp.dot(
            (m.scores[yy] / weight).astype(BF), m.keys[1, yy], preferred_element_type=F32
        )

    def rows_of(yy, k, start=0, count=ROWS):
        return m.mixed.at[yy, pl.ds(at.zi(k) * ROWS + start, count)]

    def rings_of(k):
        block = rows_of(at.y, k)
        return [send(block, block, m.mr, (k, i), at.ydev(way)) for i, way in enumerate((1, 3))]

    def passes_of(k):
        low, high = rows_of(at.yi(3), k, 0, ROWS // 2), rows_of(at.yi(1), k, ROWS // 2, ROWS // 2)
        return [send(low, low, m.mp, (k, 0), at.ydev(1)), send(high, high, m.mp, (k, 1), at.ydev(3))]

    def ring(k):
        for copy in rings_of(k):
            copy.start()

    def hand_on(k):
        for came, onward in zip(rings_of(k), passes_of(k)):
            came.wait_recv()
            onward.start()

    for h in range(RING):
        m.mixed[at.y, own_rows, h * HEAD : (h + 1) * HEAD] = mix[h * ROWS : (h + 1) * ROWS].astype(BF)
    lines_m = {k: send(rows_of(at.y, 0), rows_of(at.y, 0), m.ml, k - 1, at.zdev(k)) for k in (1, 3, 2)}
    for copy in lines_m.values():
        copy.start()
    ring(0)
    before = 0
    for k in (1, 3, 2):
        lines_m[RING - k].wait_recv()
        ring(k)
        hand_on(before)
        before = k
    spread_weights(1)
    hand_on(before)

    def project(yy):
        m.a_part[yy] = jnp.dot(m.mixed[yy], m.wo[...], preferred_element_type=F32).astype(BF)

    project(at.y)
    project(at.yi(1))
    project(at.yi(3))
    for piece in scatter:
        piece.start(False)
    for k in range(RING):
        for copy in passes_of(k):
            copy.wait_recv()
    project(at.yi(2))
    for piece in scatter:
        piece.start(True)

    def drain():
        for copy in pending + list(lines_m.values()):
            copy.wait_send()
        squares.drain()
        for c in range(q_chunks):
            qs.drain(c)
        for k in range(RING):
            for copy in (*rings_of(k), *passes_of(k)):
                copy.wait_send()

    return drain


def kernel(names, *refs):
    m = types.SimpleNamespace()
    for name, ref in zip(names, refs):
        if name.endswith("_s"):
            setattr(m, name[:-2], [ref])
        elif name.endswith("_r"):
            getattr(m, name[:-2]).append(ref)
        else:
            setattr(m, name, ref)
    at = Place()
    chunks = m.wgu.shape[0]
    side, team = lax.rem(at.z, 2), lax.div(at.z, 2)
    partner = {"dp": (at.z + 1 - 2 * side) * RING + at.y}
    span = chunks * HEAD

    enter(
        [at.ydev(k) for k in (1, 2, 3)]
        + [at.zdev(k) for k in (1, 2, 3)]
        + [at.xdev(1), at.xdev(3), at.sibling(), at.across()]
    )
    own = [(2 * at.core + h, pl.ds(at.x * ROWS, ROWS)) for h in range(2)]
    swaps = [send(m.src.at[h], m.tokens.at[own[h]], m.swap, h, at.across()) for h in range(2)]
    for swap in swaps:
        swap.start()
    loads = [
        pltpu.make_async_copy(*pair, m.local.at[i])
        for i, pair in enumerate(
            (
                (m.gain_attn_hbm, m.gain_attn),
                (m.wkv_hbm.at[at.core, :, pl.ds(at.x * HEAD, HEAD)], m.wkv),
                (m.wq_hbm, m.wq),
                (m.table_hbm, m.table),
                (m.wo_hbm, m.wo),
                (m.gain_ffn_hbm, m.gain_ffn),
            )
        )
    ]
    for load in loads:
        load.start()

    def columns(n, c):
        return pl.ds(pl.multiple_of(n * span + c * HEAD, HEAD), HEAD)

    def kept(c, g):
        return pltpu.make_async_copy(
            m.wgu_hbm.at[g, :, columns(side, c)],
            m.wgu.at[c, side, :, pl.ds(g * HEAD, HEAD)],
            m.keep.at[c, g],
        )

    def given(c, g):
        return send(
            m.wgu_hbm.at[g, :, columns(1 - side, c)],
            m.wgu.at[c, side, :, pl.ds(g * HEAD, HEAD)],
            m.give,
            (c, g),
            partner,
        )

    def down(c):
        return pltpu.make_async_copy(
            m.wd_hbm.at[pl.ds(side * span + c * HEAD, HEAD)], m.wd.at[c, side], m.down.at[c]
        )

    def lent(c):
        return send(
            m.wd_hbm.at[pl.ds((1 - side) * span + c * HEAD, HEAD)], m.wd.at[c, side], m.lend, c, partner
        )

    every = [(c, g) for c in range(chunks) for g in range(2)]
    shares = (every[:SPLIT[0]], every[SPLIT[0]:SPLIT[1]], every[SPLIT[1]:])

    def spread_weights(stage):
        for c, g in shares[stage]:
            given(c, g).start()

    for c, g in every:
        kept(c, g).start()
    for c in range(chunks):
        down(c).start()
    for load in loads:
        load.wait()
    spread = [Spread(at, m.tokens, h, m.gx) for h in range(2)]
    for swap, piece in zip(swaps, spread):
        swap.wait_recv()
        piece.start()
    spread_weights(0)
    scatter_a = [
        Scatter(at, m.a_part, m.a_pair, m.a_total, m.a_first, m.a_second, h, m.ax) for h in range(2)
    ]
    drain = attention(at, m, spread, scatter_a, m.gain_attn[...].astype(F32), spread_weights)

    gain = m.gain_ffn[...].astype(F32)
    for piece in scatter_a:
        piece.step_one()
    for piece in scatter_a:
        piece.step_two()
    trades = [
        send(m.f_gained.at[h], m.f_tokens.at[(1, *own[h])], m.trade, h, partner) for h in range(2)
    ]
    near, away = (
        [Spread(at, m.f_tokens.at[i], h, sems) for h in range(2)] for i, sems in enumerate((m.fx, m.gz))
    )
    for h in range(2):
        resid = (m.tokens[own[h]].astype(F32) + scatter_a[h].result()).astype(BF)
        m.f_gained[h] = (resid.astype(F32) * gain).astype(BF)
        trades[h].start()
        m.f_tokens[(0, *own[h])] = resid
        near[h].start()
    spread_weights(2)
    for h in range(2):
        trades[h].wait_recv()
        away[h].start()
        near[h].onward()
    for h in range(2):
        near[h].end()
        away[h].onward()
    for h in range(2):
        away[h].end()
    for h in range(2):
        near[h].finish()
    squares = Squares(at, m.fs_part, m.fs_near, m.fs_mid, m.fs_far, m.fsy, m.fsz)
    for k in (2, 1, 3):
        scaled(m.f_tokens.at[0], gain, m.f_normed, squares, at.yi(k))
    squares.start()
    scaled(m.f_tokens.at[0], gain, m.f_normed, squares, at.y)
    m.acc[...] = jnp.zeros_like(m.acc)
    for h in range(2):
        away[h].finish()

    fellow = [(0, pl.ds((1 - team) * 2 * ROWS, 2 * ROWS), at.zdev(2))]
    own_rows = pl.ds(team * 2 * ROWS, 2 * ROWS)
    hs = Reduce(at, m.h_part, m.h_one, m.h_two, m.h_three, (m.h1, m.h2, m.h3), fellow)
    hg = Gather(
        at,
        lambda c: m.hidden.at[c, at.y, own_rows],
        lambda c, yy, rows: m.hidden.at[c, yy, rows],
        (m.hl, m.hr, m.hp),
    )

    def product(c, yy):
        return jnp.dot(m.f_normed[yy], m.wgu[c, side], preferred_element_type=F32) + jnp.dot(
            m.f_tokens[1, yy], m.wgu[c, 1 - side], preferred_element_type=F32
        )

    def first(c):
        for g in range(2):
            kept(c, g).wait()
            given(c, g).wait_recv()
        hs.far(c, product)
        lent(c).start()

    def activate(c):
        both = hs.result(c, own_rows) * m.scale[...]
        gate, up = both[:, :HEAD], both[:, HEAD:]
        m.hidden[c, at.y, own_rows] = (gate / (1.0 + jnp.exp(-gate)) * up).astype(BF)
        hg.line(c)

    def ring(c):
        hg.arrived(c)
        hg.ring(c)

    def add_down(held, k):
        yy = at.yi(k)
        left = jnp.concatenate([m.hidden[c, yy] for c in held], axis=1)
        for j, half in enumerate((side, 1 - side)):
            right = jnp.concatenate([m.wd[c, half] for c in held], axis=0)
            m.acc[j, k] += jnp.dot(left, right, preferred_element_type=F32)

    def by_pairs(c, blocks):
        @pl.when(lax.rem(c, 2) == 1)
        def _():
            for k in blocks:
                add_down((c - 1, c), k)

        if chunks % 2:

            @pl.when(c == chunks - 1)
            def _():
                for k in blocks:
                    add_down((c,), k)

    def down_near(c):
        down(c).wait()
        lent(c).wait_recv()
        by_pairs(c, (0, 1, 3))

    def down_far(c):
        hg.finish(c)
        by_pairs(c, (2,))

    def row_scale():
        m.scale[...] = jnp.broadcast_to(squares.scale(2 * ROWS, team * 2 * ROWS), m.scale.shape)

    def both_sums():
        sets = (
            (m.g_part, m.g_pair, m.g_total, m.g_first, m.g_second, m.cx),
            (m.f_part, m.f_pair, m.f_total, m.f_first, m.f_second, m.bx),
        )
        return [[Scatter(at, *refs[:5], h, refs[5]) for h in range(2)] for refs in sets]

    def hand_over(blocks, late):
        for j, part, pieces in zip((1, 0), (m.g_part, m.f_part), both_sums()):
            for k in blocks:
                part[at.yi(k)] = m.acc[j, k].astype(BF)
            for piece in pieces:
                piece.start(late)

    once = (
        (squares.middle, 2),
        (row_scale, 4),
        (lambda: hand_over((0, 1, 3), False), chunks + 7),
    )
    stages = (
        (first, 0),
        (lambda c: hs.near(c, product), 2),
        (lambda c: hs.own(c, product), 3),
        (activate, 4),
        (ring, 5),
        (hg.hand_on, 6),
        (down_near, 7),
        (down_far, 8),
    )

    def turn(i, carry):
        for step, when in once:
            pl.when(i == when)(step)
        for stage, lag in stages:
            c = i - lag

            @pl.when((c >= 0) & (c < chunks))
            def _():
                stage(c)

        return carry

    lax.fori_loop(0, chunks + stages[-1][1], turn, 0)
    others, owns = both_sums()
    hand_over((2,), True)
    for piece in others:
        piece.step_one()
    for piece in owns:
        piece.step_one()

    def drain_chunk(c, carry):
        hs.drain(c)
        hg.drain(c)
        for g in range(2):
            given(c, g).wait_send()
        lent(c).wait_send()
        return carry

    drain()
    for copy in swaps + trades:
        copy.wait_send()
    for piece in near + away + scatter_a:
        for copy in piece.copies():
            copy.wait_send()
    squares.drain()
    lax.fori_loop(0, chunks, drain_chunk, 0)
    for piece in others:
        piece.step_two()
    for piece in owns:
        piece.step_two()
    backs = [send(m.back_out.at[h], m.back_in.at[h], m.back, h, partner) for h in range(2)]
    for h in range(2):
        m.back_out[h] = others[h].result().astype(BF)
        backs[h].start()
    for h in range(2):
        value = m.f_tokens[(0, *own[h])].astype(F32) + owns[h].result()
        backs[h].wait_recv()
        m.out[h] = (value + m.back_in[h].astype(F32)).astype(BF)

    for copy in backs:
        copy.wait_send()
    for piece in others + owns:
        for copy in piece.copies():
            copy.wait_send()


def reduce_scratch(name, chunks, columns, slots, rows):
    return {
        name + "_part": pltpu.VMEM((chunks, RING, GROUP, columns), BF),
        name + "_one": pltpu.VMEM((chunks, 2, GROUP // 2, columns), BF),
        name + "_two": pltpu.VMEM((chunks, 2, GROUP, columns), BF),
        name + "_three": pltpu.VMEM((chunks, slots, rows, columns), BF),
    }


def square_scratch(name):
    return {
        name + "_part": pltpu.VMEM((RING, 8, GROUP), F32),
        name + "_near": pltpu.VMEM((3, 8, GROUP), F32),
        name + "_mid": pltpu.VMEM((8, GROUP), F32),
        name + "_far": pltpu.VMEM((3, 8, GROUP), F32),
    }


def scatter_scratch(name, columns):
    return {
        name + "_part": pltpu.VMEM((RING, GROUP, columns), BF),
        name + "_pair": pltpu.VMEM((2, GROUP, columns), BF),
        name + "_total": pltpu.VMEM((2, GROUP, columns), BF),
        name + "_first": pltpu.VMEM((2, 2, ROWS // 2, columns), BF),
        name + "_second": pltpu.VMEM((2, 2, ROWS, columns), BF),
    }


def scratch(cols, heads, chunks, q_chunks):
    wide = 2 * HEAD
    buffers = {
        "gain_attn": pltpu.VMEM((1, cols), BF),
        "gain_ffn": pltpu.VMEM((1, cols), BF),
        "table": pltpu.VMEM((2, ROWS + RING * RING, HEAD), F32),
        "tokens": pltpu.VMEM((RING, GROUP, cols), BF),
        "normed": pltpu.VMEM((RING, GROUP, cols), BF),
        "wq": pltpu.VMEM((cols, heads), BF),
        "wkv": pltpu.VMEM((cols, HEAD), BF),
        "wo": pltpu.VMEM((heads, cols), BF),
        **reduce_scratch("q", q_chunks, heads // q_chunks, 3, ROWS),
        "k_part": pltpu.VMEM((RING, GROUP, HEAD), BF),
        "k_near": pltpu.VMEM((3, GROUP, HEAD), BF),
        "k_far": pltpu.VMEM((3, ROWS, HEAD), BF),
        **square_scratch("ss"),
        "keys": pltpu.VMEM((2, RING, GROUP, HEAD), BF),
        "mixed": pltpu.VMEM((RING, GROUP, heads), BF),
        "scores": pltpu.VMEM((RING, RING * ROWS, GROUP), F32),
        **scatter_scratch("a", cols),
        "f_gained": pltpu.VMEM((2, ROWS, cols), BF),
        "f_tokens": pltpu.VMEM((2, RING, GROUP, cols), BF),
        "f_normed": pltpu.VMEM((RING, GROUP, cols), BF),
        "wgu": pltpu.VMEM((chunks, 2, cols, wide), BF),
        "wd": pltpu.VMEM((chunks, 2, HEAD, cols), BF),
        **reduce_scratch("h", chunks, wide, 1, 2 * ROWS),
        **square_scratch("fs"),
        "scale": pltpu.VMEM((2 * ROWS, wide), F32),
        "hidden": pltpu.VMEM((chunks, RING, GROUP, HEAD), BF),
        "acc": pltpu.VMEM((2, RING, GROUP, cols), F32),
        **scatter_scratch("f", cols),
        **scatter_scratch("g", cols),
        "back_out": pltpu.VMEM((2, ROWS, cols), BF),
        "back_in": pltpu.VMEM((2, ROWS, cols), BF),
    }
    single = {"local": (6,), "keep": (chunks, 2), "down": (chunks,)}
    double = {
        "give": (chunks, 2), "lend": (chunks,), "back": (2,), "cx": (2, 8), "swap": (2,), "trade": (2,),
        "gx": (2, 8), "fx": (2, 8), "gz": (2, 8), "ax": (2, 8), "bx": (2, 8),
        "ssy": (3,), "ssz": (3,), "fsy": (3,), "fsz": (3,),
        "q1": (q_chunks, 2), "q2": (q_chunks, 2), "q3": (q_chunks, 3),
        "k1": (3,), "k2": (3,), "kl": (3,), "kr": (3,), "kc": (4,),
        "ml": (3,), "mr": (RING, 2), "mp": (RING, 2),
        "h1": (chunks, 2), "h2": (chunks, 2), "h3": (chunks, 1),
        "hl": (chunks,), "hr": (chunks, 2), "hp": (chunks, 2),
    }
    for name, shape in single.items():
        buffers[name] = pltpu.SemaphoreType.DMA(shape)
    for name, shape in double.items():
        buffers[name + "_s"] = pltpu.SemaphoreType.DMA(shape)
        buffers[name + "_r"] = pltpu.SemaphoreType.DMA(shape)
    return buffers


def rotary_table(count):
    freq = np.exp(-(2.0 * np.arange(HEAD // 2) / HEAD) * math.log(THETA))
    position = np.concatenate([np.arange(ROWS), np.arange(count) * ROWS]).astype(np.float64)
    angle = position[:, None] * np.concatenate([freq, freq])[None, :]
    return np.stack([np.cos(angle), np.sin(angle)]).astype(np.float32)


def local_layer(
    section_input, gain_attn, w_query, key_value_weight, w_output, gain_ffn, w_gate_up, w_down
):
    cols = section_input.shape[2]
    heads = w_query.shape[2]
    chunks = w_gate_up.shape[3] // (2 * HEAD)
    anywhere = pl.BlockSpec(memory_space=pl.ANY)
    vmem = pl.BlockSpec(memory_space=pltpu.VMEM)
    inputs = {
        "src": (section_input.reshape(2, ROWS, cols), anywhere),
        "gain_attn_hbm": (gain_attn, anywhere),
        "wq_hbm": (w_query[0], anywhere),
        "wkv_hbm": (key_value_weight[0], anywhere),
        "wo_hbm": (w_output[0], anywhere),
        "gain_ffn_hbm": (gain_ffn, anywhere),
        "wgu_hbm": (w_gate_up[0], anywhere),
        "wd_hbm": (w_down[0], anywhere),
        "table_hbm": (jnp.asarray(rotary_table(RING * RING)), anywhere),
    }
    buffers = scratch(cols, heads, chunks, 2)
    result = pl.pallas_call(
        functools.partial(kernel, (*inputs, "out", *buffers)),
        name="layer",
        out_shape=jax.ShapeDtypeStruct((2, ROWS, cols), BF),
        in_specs=[spec for _, spec in inputs.values()],
        out_specs=vmem,
        scratch_shapes=list(buffers.values()),
        compiler_params=pltpu.CompilerParams(
            collective_id=0, has_side_effects=True, vmem_limit_bytes=60 * 1024 * 1024
        ),
    )(*[array for array, _ in inputs.values()])
    return result.reshape(1, 2 * ROWS, cols)


def solution(mesh):
    placed = (
        P("section", "tensor", "dp"),
        P("section", "dp"),
        P("section", "dp", "tensor"),
        P("section", None, "dp", None),
        P("section", "tensor", "dp"),
        P("section", "dp"),
        P("section", None, "dp", "tensor"),
        P("section", "tensor", "dp"),
    )
    return jax.shard_map(
        local_layer, mesh=mesh, in_specs=placed, out_specs=P("section", "tensor", "dp"), check_vma=False
    )
```

```python
import functools
import math
import types

import jax
import jax.numpy as jnp
import numpy as np
from jax import lax
from jax.experimental import pallas as pl
from jax.experimental.pallas import tpu as pltpu
from jax.sharding import PartitionSpec as P

HEAD = 128
EPS = 1e-05
THETA = 500000.0
RING = 4
ROWS = 64
GROUP = RING * ROWS
WIDTH = 8192
SPLIT = (5, 10)

MESH_ID = pl.DeviceIdType.MESH
BF = jnp.bfloat16
F32 = jnp.float32


class Place:
    def __init__(self):
        self.section = lax.axis_index("section")
        dp = lax.axis_index("dp")
        tensor = lax.axis_index("tensor")
        self.dp = dp
        self.z, self.y = lax.div(dp, RING), lax.rem(dp, RING)
        self.x, self.core = lax.div(tensor, 2), lax.rem(tensor, 2)

    def yi(self, k):
        return lax.rem(self.y + k, RING)

    def zi(self, k):
        return lax.rem(self.z + k, RING)

    def xi(self, k):
        return lax.rem(self.x + k, RING)

    def ydev(self, k):
        return {"dp": self.z * RING + self.yi(k)}

    def zdev(self, k):
        return {"dp": self.zi(k) * RING + self.y}

    def xdev(self, k):
        return {"tensor": self.xi(k) * 2 + self.core}

    def sibling(self):
        return {"tensor": self.x * 2 + 1 - self.core}

    def across(self):
        return {"section": 1 - self.section}


def enter(devices):
    barrier = pltpu.get_barrier_semaphore()
    for device in devices:
        pl.semaphore_signal(barrier, inc=1, device_id=device, device_id_type=MESH_ID)
    pl.semaphore_wait(barrier, len(devices))


def send(src, dst, sems, index, device):
    return pltpu.make_async_remote_copy(
        src_ref=src,
        dst_ref=dst,
        send_sem=sems[0].at[index],
        recv_sem=sems[1].at[index],
        device_id=device,
        device_id_type=MESH_ID,
    )


class Spread:
    def __init__(self, at, tokens, h, sems):
        self.right, self.left, self.far = at.xi(1), at.xi(3), at.xi(2)

        def rows(xx, start, count):
            return tokens.at[2 * at.core + h, pl.ds(xx * ROWS + start, count)]

        def block(xx):
            return rows(xx, 0, ROWS)

        def same(ref, index, device):
            return send(ref, ref, sems, (h, index), device)

        half = ROWS // 2
        self.out = [
            same(block(at.x), 0, at.xdev(1)),
            same(block(at.x), 1, at.xdev(3)),
            same(block(at.x), 2, at.sibling()),
        ]
        self.after_left = [
            same(rows(self.left, 0, half), 3, at.xdev(1)),
            same(block(self.left), 4, at.sibling()),
        ]
        self.after_right = [
            same(rows(self.right, half, half), 5, at.xdev(3)),
            same(block(self.right), 6, at.sibling()),
        ]
        self.last = [same(block(self.far), 7, at.sibling())]

    def start(self):
        for copy in self.out:
            copy.start()

    def onward(self):
        self.out[0].wait_recv()
        for copy in self.after_left:
            copy.start()
        self.out[1].wait_recv()
        for copy in self.after_right:
            copy.start()

    def end(self):
        self.after_left[0].wait_recv()
        self.after_right[0].wait_recv()
        self.last[0].start()

    def finish(self):
        for copy in (self.out[2], self.after_left[1], self.after_right[1], self.last[0]):
            copy.wait_recv()

    def copies(self):
        return [*self.out, *self.after_left, *self.after_right, *self.last]


class Scatter:
    def __init__(self, at, part, pair, total, first, second, h, sems):
        self.at, self.part, self.pair, self.h = at, part, pair, h
        self.total, self.first, self.second = total, first, second
        self.mine, other = 2 * at.core + h, 2 * (1 - at.core) + h
        self.other = other
        self.right, self.left, self.far = at.xi(1), at.xi(3), at.xi(2)
        self.half = ROWS // 2

        def to(src, dst, index, device):
            return send(src, dst, sems, (h, index), device)

        self.shares = [
            to(part.at[other, self.rows(xx)], pair.at[h, self.rows(xx)], i, at.sibling())
            for i, xx in enumerate((self.far, self.right, self.left, at.x))
        ]
        self.ones = [
            to(total.at[h, pl.ds(self.far * ROWS, self.half)], first.at[h, 0], 4, at.xdev(1)),
            to(total.at[h, pl.ds(self.far * ROWS + self.half, self.half)], first.at[h, 1], 5, at.xdev(3)),
        ]
        self.twos = [
            to(total.at[h, self.rows(self.right)], second.at[h, 0], 6, at.xdev(1)),
            to(total.at[h, self.rows(self.left)], second.at[h, 1], 7, at.xdev(3)),
        ]

    def rows(self, xx):
        return pl.ds(xx * ROWS, ROWS)

    def summed(self, i, xx):
        self.shares[i].wait_recv()
        return self.part[self.mine, self.rows(xx)].astype(F32) + self.pair[self.h, self.rows(xx)].astype(F32)

    def start(self, late):
        is_far = self.other == self.at.yi(2)

        @pl.when(is_far if late else jnp.logical_not(is_far))
        def _():
            for copy in self.shares:
                copy.start()

    def step_one(self):
        self.total[self.h, self.rows(self.far)] = self.summed(0, self.far).astype(BF)
        for copy in self.ones:
            copy.start()

    def step_two(self):
        half = self.half
        value = self.summed(1, self.right)
        self.ones[0].wait_recv()
        added = value[:half] + self.first[self.h, 0].astype(F32)
        self.total[self.h, self.rows(self.right)] = jnp.concatenate([added, value[half:]], axis=0).astype(BF)
        self.twos[0].start()
        value = self.summed(2, self.left)
        self.ones[1].wait_recv()
        added = value[half:] + self.first[self.h, 1].astype(F32)
        self.total[self.h, self.rows(self.left)] = jnp.concatenate([value[:half], added], axis=0).astype(BF)
        self.twos[1].start()

    def result(self):
        own = self.summed(3, self.at.x)
        for copy in self.twos:
            copy.wait_recv()
        return own + self.second[self.h, 0].astype(F32) + self.second[self.h, 1].astype(F32)

    def copies(self):
        return [*self.shares, *self.ones, *self.twos]


class Reduce:
    def __init__(self, at, part, first, second, third, sems, hand):
        self.at = at
        self.part, self.first, self.second, self.third = part, first, second, third
        self.sems_one, self.sems_two, self.sems_three = sems
        self.hand = hand

    def ones(self, c):
        far = self.at.yi(2)
        low, high = pl.ds(0, GROUP // 2), pl.ds(GROUP // 2, GROUP // 2)
        return (
            send(self.part.at[c, far, low], self.first.at[c, 0], self.sems_one, (c, 0), self.at.ydev(1)),
            send(self.part.at[c, far, high], self.first.at[c, 1], self.sems_one, (c, 1), self.at.ydev(3)),
        )

    def twos(self, c):
        return (
            send(self.part.at[c, self.at.yi(1)], self.second.at[c, 0], self.sems_two, (c, 0), self.at.ydev(1)),
            send(self.part.at[c, self.at.yi(3)], self.second.at[c, 1], self.sems_two, (c, 1), self.at.ydev(3)),
        )

    def threes(self, c):
        return [
            send(
                self.part.at[c, self.at.y, rows], self.third.at[c, slot], self.sems_three, (c, slot), device
            )
            for slot, rows, device in self.hand
        ]

    def far(self, c, product):
        self.part[c, self.at.yi(2)] = product(c, self.at.yi(2)).astype(BF)
        for copy in self.ones(c):
            copy.start()

    def near(self, c, product):
        half = GROUP // 2
        one, two = self.ones(c), self.twos(c)
        right, left = self.at.yi(1), self.at.yi(3)
        value = product(c, right)
        one[0].wait_recv()
        self.part[c, right, 0:half] = (value[:half] + self.first[c, 0].astype(F32)).astype(BF)
        self.part[c, right, half:GROUP] = value[half:].astype(BF)
        two[0].start()
        value = product(c, left)
        one[1].wait_recv()
        self.part[c, left, 0:half] = value[:half].astype(BF)
        self.part[c, left, half:GROUP] = (value[half:] + self.first[c, 1].astype(F32)).astype(BF)
        two[1].start()

    def own(self, c, product):
        value = product(c, self.at.y)
        for copy in self.twos(c):
            copy.wait_recv()
        self.part[c, self.at.y] = (
            value + self.second[c, 0].astype(F32) + self.second[c, 1].astype(F32)
        ).astype(BF)
        for copy in self.threes(c):
            copy.start()

    def result(self, c, rows):
        for copy in self.threes(c):
            copy.wait_recv()
        total = self.part[c, self.at.y, rows].astype(F32)
        for slot, _, _ in self.hand:
            total = total + self.third[c, slot].astype(F32)
        return total

    def drain(self, c):
        for copy in (*self.ones(c), *self.twos(c), *self.threes(c)):
            copy.wait_send()


class Gather:
    def __init__(self, at, mine, block, sems):
        self.at, self.mine, self.block = at, mine, block
        self.sems_line, self.sems_ring, self.sems_pass = sems

    def lines(self, c):
        return [send(self.mine(c), self.mine(c), self.sems_line, c, self.at.zdev(2))]

    def rings(self, c):
        block = self.block(c, self.at.y, pl.ds(0, GROUP))
        return [
            send(block, block, self.sems_ring, (c, 0), self.at.ydev(1)),
            send(block, block, self.sems_ring, (c, 1), self.at.ydev(3)),
        ]

    def passes(self, c):
        low = self.block(c, self.at.yi(3), pl.ds(0, GROUP // 2))
        high = self.block(c, self.at.yi(1), pl.ds(GROUP // 2, GROUP // 2))
        return [
            send(low, low, self.sems_pass, (c, 0), self.at.ydev(1)),
            send(high, high, self.sems_pass, (c, 1), self.at.ydev(3)),
        ]

    def line(self, c):
        for copy in self.lines(c):
            copy.start()

    def arrived(self, c):
        for copy in self.lines(c):
            copy.wait_recv()

    def ring(self, c):
        for copy in self.rings(c):
            copy.start()

    def hand_on(self, c):
        for ring, onward in zip(self.rings(c), self.passes(c)):
            ring.wait_recv()
            onward.start()

    def finish(self, c):
        for copy in self.passes(c):
            copy.wait_recv()

    def drain(self, c):
        for copy in (*self.lines(c), *self.rings(c), *self.passes(c)):
            copy.wait_send()


class Squares:
    def __init__(self, at, part, near, mid, far, sems_y, sems_z):
        self.at, self.part, self.near, self.mid, self.far = at, part, near, mid, far
        self.sems_y, self.sems_z = sems_y, sems_z

    def fill(self, yy, wide):
        squared = (wide * wide).astype(BF)
        self.part[yy] = lax.dot_general(
            jnp.ones((8, wide.shape[1]), BF),
            squared,
            (((1,), (1,)), ((), ())),
            preferred_element_type=F32,
        )

    def ys(self):
        return [
            send(self.part.at[self.at.yi(k)], self.near.at[k - 1], self.sems_y, k - 1, self.at.ydev(k))
            for k in (1, 2, 3)
        ]

    def zs(self):
        return [
            send(self.mid, self.far.at[k - 1], self.sems_z, k - 1, self.at.zdev(k)) for k in (1, 2, 3)
        ]

    def start(self):
        for copy in self.ys():
            copy.start()

    def middle(self):
        for copy in self.ys():
            copy.wait_recv()
        self.mid[...] = self.part[self.at.y] + self.near[0] + self.near[1] + self.near[2]
        for copy in self.zs():
            copy.start()

    def scale(self, count, start):
        for copy in self.zs():
            copy.wait_recv()
        total = self.mid[...] + self.far[0] + self.far[1] + self.far[2]
        line = lax.rsqrt(total / WIDTH + EPS)[0:1]
        row = lax.broadcasted_iota(jnp.int32, (count, GROUP), 0)
        lane = lax.broadcasted_iota(jnp.int32, (count, GROUP), 1)
        picked = jnp.where(lane == row + start, jnp.broadcast_to(line, (count, GROUP)), 0.0)
        return jnp.sum(picked, axis=1, keepdims=True)

    def drain(self):
        for copy in (*self.ys(), *self.zs()):
            copy.wait_send()


def scaled(tokens, gain, out, squares, yy):
    wide = tokens[yy].astype(F32)
    squares.fill(yy, wide)
    out[yy] = (wide * gain).astype(BF)


def attention(at, m, spread, scatter, gain, spread_weights):
    half = HEAD // 2
    lane = lax.broadcasted_iota(jnp.int32, (1, HEAD), 1)
    base = [m.table[i, pl.ds(ROWS + at.dp, 1), :] for i in range(2)]
    step = [m.table[i, 0:ROWS, :] for i in range(2)]
    cosine = base[0] * step[0] - base[1] * step[1]
    sine = (base[1] * step[0] + base[0] * step[1]) * jnp.where(lane < half, -1.0, 1.0)
    for piece in spread:
        piece.onward()
    for piece in spread:
        piece.end()
    for piece in spread:
        piece.finish()
    pending = [copy for piece in spread for copy in piece.copies()]

    squares = Squares(at, m.ss_part, m.ss_near, m.ss_mid, m.ss_far, m.ssy, m.ssz)
    along = [(k - 1, pl.ds(at.zi(k) * ROWS, ROWS), at.zdev(k)) for k in (2, 1, 3)]
    own_rows = pl.ds(at.z * ROWS, ROWS)
    qs = Reduce(at, m.q_part, m.q_one, m.q_two, m.q_three, (m.q1, m.q2, m.q3), along)
    q_chunks = m.q_part.shape[0]
    q_cols = m.q_part.shape[3]

    def product_q(c, yy):
        columns = m.wq[:, c * q_cols : (c + 1) * q_cols]
        return jnp.dot(m.normed[yy], columns, preferred_element_type=F32)

    def product_k(yy):
        return jnp.dot(m.normed[yy], m.wkv[...], preferred_element_type=F32)

    key_y = [
        send(m.k_part.at[at.yi(k)], m.k_near.at[k - 1], m.k1, k - 1, at.ydev(k)) for k in (2, 1, 3)
    ]
    for k, copy in zip((2, 1, 3), key_y):
        scaled(m.tokens, gain, m.normed, squares, at.yi(k))
        m.k_part[at.yi(k)] = product_k(at.yi(k)).astype(BF)
        copy.start()
    squares.start()
    for c in range(q_chunks):
        qs.far(c, product_q)
    scaled(m.tokens, gain, m.normed, squares, at.y)
    total = product_k(at.y)
    for k, copy in zip((2, 1, 3), key_y):
        copy.wait_recv()
        total = total + m.k_near[k - 1].astype(F32)
    m.k_part[at.y] = total.astype(BF)
    key_z = [
        send(m.k_part.at[at.y, rows], m.k_far.at[slot], m.k2, slot, device)
        for slot, rows, device in along
    ]
    for copy in key_z:
        copy.start()
    squares.middle()
    for c in range(q_chunks):
        qs.near(c, product_q)
    scale = squares.scale(ROWS, at.z * ROWS)

    def rotated(value, cos, sin):
        return value * cos + pltpu.roll(value, half, 1) * sin

    is_key = at.core == 0
    core = at.core
    value = m.k_part[at.y, own_rows].astype(F32)
    for slot, copy in zip((1, 0, 2), key_z):
        copy.wait_recv()
        value = value + m.k_far[slot].astype(F32)
    m.keys[core, at.y, own_rows] = rotated(
        value * scale, jnp.where(is_key, cosine, 1.0), jnp.where(is_key, sine, 0.0)
    ).astype(BF)
    mine = m.keys.at[core, at.y, own_rows]
    lines = [send(mine, mine, m.kl, k - 1, at.zdev(k)) for k in (2, 1, 3)]
    for copy in lines:
        copy.start()
    qs.own(0, product_q)
    for copy in lines:
        copy.wait_recv()
    block = m.keys.at[core, at.y]
    rings = [send(block, block, m.kr, k - 1, at.ydev(k)) for k in (2, 1, 3)]
    shares = [send(block, block, m.kc, 0, at.sibling())]
    for copy in rings + shares:
        copy.start()
    for c in range(1, q_chunks):
        qs.own(c, product_q)
    for k, ring in zip((2, 1, 3), rings):
        ring.wait_recv()
        came = m.keys.at[core, at.yi(RING - k)]
        shares.append(send(came, came, m.kc, k, at.sibling()))
        shares[-1].start()
    pending += key_y + key_z + lines + rings + shares

    per = q_cols // HEAD
    pieces = []
    for c in range(q_chunks):
        queries = qs.result(c, own_rows) * scale
        pieces += [rotated(queries[:, h * HEAD : (h + 1) * HEAD], cosine, sine) for h in range(per)]
    stacked = jnp.concatenate(pieces, axis=0).astype(BF)
    row = lax.broadcasted_iota(jnp.int32, (RING * ROWS, GROUP), 0)
    col = lax.broadcasted_iota(jnp.int32, (RING * ROWS, GROUP), 1)
    query_at = lax.rem(row, ROWS) + at.dp * ROWS
    key_at = lax.div(col, ROWS) * GROUP + lax.rem(col, ROWS)
    weight = jnp.zeros((RING * ROWS, 1), F32)
    arrivals = [at.yi(k) for k in (0, 2, 3, 1)]
    for i, yy in enumerate(arrivals):
        shares[i].wait_recv()
        raw = lax.dot_general(
            stacked, m.keys[0, yy], (((1,), (1,)), ((), ())), preferred_element_type=F32
        ) * HEAD ** (-0.5)
        kept = jnp.where(key_at + yy * ROWS <= query_at, jnp.exp(raw), 0.0)
        m.scores[i] = kept
        weight = weight + jnp.sum(kept, axis=1, keepdims=True)
    mix = jnp.zeros((RING * ROWS, HEAD), F32)
    for i, yy in enumerate(arrivals):
        mix = mix + jnp.dot(
            (m.scores[i] / weight).astype(BF), m.keys[1, yy], preferred_element_type=F32
        )

    def rows_of(yy, k, start=0, count=ROWS):
        return m.mixed.at[yy, pl.ds(at.zi(k) * ROWS + start, count)]

    def rings_of(k):
        block = rows_of(at.y, k)
        return [send(block, block, m.mr, (k, i), at.ydev(way)) for i, way in enumerate((1, 3))]

    def passes_of(k):
        low, high = rows_of(at.yi(3), k, 0, ROWS // 2), rows_of(at.yi(1), k, ROWS // 2, ROWS // 2)
        return [send(low, low, m.mp, (k, 0), at.ydev(1)), send(high, high, m.mp, (k, 1), at.ydev(3))]

    def ring(k):
        for copy in rings_of(k):
            copy.start()

    def hand_on(k):
        for came, onward in zip(rings_of(k), passes_of(k)):
            came.wait_recv()
            onward.start()

    for h in range(RING):
        m.mixed[at.y, own_rows, h * HEAD : (h + 1) * HEAD] = mix[h * ROWS : (h + 1) * ROWS].astype(BF)
    lines_m = {k: send(rows_of(at.y, 0), rows_of(at.y, 0), m.ml, k - 1, at.zdev(k)) for k in (1, 3, 2)}
    for copy in lines_m.values():
        copy.start()
    ring(0)
    before = 0
    for k in (1, 3, 2):
        lines_m[RING - k].wait_recv()
        ring(k)
        hand_on(before)
        before = k
    spread_weights(1)
    hand_on(before)

    def project(yy):
        m.a_part[yy] = jnp.dot(m.mixed[yy], m.wo[...], preferred_element_type=F32).astype(BF)

    project(at.y)
    project(at.yi(1))
    project(at.yi(3))
    for piece in scatter:
        piece.start(False)
    for k in range(RING):
        for copy in passes_of(k):
            copy.wait_recv()
    project(at.yi(2))
    for piece in scatter:
        piece.start(True)

    def drain():
        for copy in pending + list(lines_m.values()):
            copy.wait_send()
        squares.drain()
        for c in range(q_chunks):
            qs.drain(c)
        for k in range(RING):
            for copy in (*rings_of(k), *passes_of(k)):
                copy.wait_send()

    return drain


def kernel(names, *refs):
    m = types.SimpleNamespace()
    for name, ref in zip(names, refs):
        if name.endswith("_s"):
            setattr(m, name[:-2], [ref])
        elif name.endswith("_r"):
            getattr(m, name[:-2]).append(ref)
        else:
            setattr(m, name, ref)
    at = Place()
    chunks = m.wgu.shape[0]
    side, team = lax.rem(at.z, 2), lax.div(at.z, 2)
    partner = {"dp": (at.z + 1 - 2 * side) * RING + at.y}
    span = chunks * HEAD

    enter(
        [at.ydev(k) for k in (1, 2, 3)]
        + [at.zdev(k) for k in (1, 2, 3)]
        + [at.xdev(1), at.xdev(3), at.sibling(), at.across()]
    )
    own = [(2 * at.core + h, pl.ds(at.x * ROWS, ROWS)) for h in range(2)]
    swaps = [send(m.src.at[h], m.tokens.at[own[h]], m.swap, h, at.across()) for h in range(2)]
    for swap in swaps:
        swap.start()
    loads = [
        pltpu.make_async_copy(*pair, m.local.at[i])
        for i, pair in enumerate(
            (
                (m.gain_attn_hbm, m.gain_attn),
                (m.wkv_hbm.at[at.core, :, pl.ds(at.x * HEAD, HEAD)], m.wkv),
                (m.wq_hbm, m.wq),
                (m.table_hbm, m.table),
                (m.wo_hbm, m.wo),
                (m.gain_ffn_hbm, m.gain_ffn),
            )
        )
    ]
    for load in loads:
        load.start()

    def columns(n, c):
        return pl.ds(pl.multiple_of(n * span + c * HEAD, HEAD), HEAD)

    def kept(c, g):
        return pltpu.make_async_copy(
            m.wgu_hbm.at[g, :, columns(side, c)],
            m.wgu.at[c, side, :, pl.ds(g * HEAD, HEAD)],
            m.keep.at[c, g],
        )

    def given(c, g):
        return send(
            m.wgu_hbm.at[g, :, columns(1 - side, c)],
            m.wgu.at[c, side, :, pl.ds(g * HEAD, HEAD)],
            m.give,
            (c, g),
            partner,
        )

    def down(c):
        return pltpu.make_async_copy(
            m.wd_hbm.at[pl.ds(side * span + c * HEAD, HEAD)], m.wd.at[c, side], m.down.at[c]
        )

    def lent(c):
        return send(
            m.wd_hbm.at[pl.ds((1 - side) * span + c * HEAD, HEAD)], m.wd.at[c, side], m.lend, c, partner
        )

    every = [(c, g) for c in range(chunks) for g in range(2)]
    shares = (every[:SPLIT[0]], every[SPLIT[0]:SPLIT[1]], every[SPLIT[1]:])

    def spread_weights(stage):
        for c, g in shares[stage]:
            given(c, g).start()

    for c, g in every:
        kept(c, g).start()
    for c in range(chunks):
        down(c).start()
    for load in loads:
        load.wait()
    spread = [Spread(at, m.tokens, h, m.gx) for h in range(2)]
    for swap, piece in zip(swaps, spread):
        swap.wait_recv()
        piece.start()
    spread_weights(0)
    scatter_a = [
        Scatter(at, m.a_part, m.a_pair, m.a_total, m.a_first, m.a_second, h, m.ax) for h in range(2)
    ]
    drain = attention(at, m, spread, scatter_a, m.gain_attn[...].astype(F32), spread_weights)

    gain = m.gain_ffn[...].astype(F32)
    for piece in scatter_a:
        piece.step_one()
    for piece in scatter_a:
        piece.step_two()
    trades = [
        send(m.f_gained.at[h], m.f_tokens.at[(1, *own[h])], m.trade, h, partner) for h in range(2)
    ]
    near, away = (
        [Spread(at, m.f_tokens.at[i], h, sems) for h in range(2)] for i, sems in enumerate((m.fx, m.gz))
    )
    for h in range(2):
        resid = (m.tokens[own[h]].astype(F32) + scatter_a[h].result()).astype(BF)
        m.f_gained[h] = (resid.astype(F32) * gain).astype(BF)
        trades[h].start()
        m.f_tokens[(0, *own[h])] = resid
        near[h].start()
    spread_weights(2)
    for h in range(2):
        trades[h].wait_recv()
        away[h].start()
        near[h].onward()
    for h in range(2):
        near[h].end()
        away[h].onward()
    for h in range(2):
        away[h].end()
    for h in range(2):
        near[h].finish()
    squares = Squares(at, m.fs_part, m.fs_near, m.fs_mid, m.fs_far, m.fsy, m.fsz)
    for k in (2, 1, 3):
        scaled(m.f_tokens.at[0], gain, m.f_normed, squares, at.yi(k))
    squares.start()
    scaled(m.f_tokens.at[0], gain, m.f_normed, squares, at.y)
    m.acc[...] = jnp.zeros_like(m.acc)
    for h in range(2):
        away[h].finish()

    fellow = [(0, pl.ds((1 - team) * 2 * ROWS, 2 * ROWS), at.zdev(2))]
    own_rows = pl.ds(team * 2 * ROWS, 2 * ROWS)
    hs = Reduce(at, m.h_part, m.h_one, m.h_two, m.h_three, (m.h1, m.h2, m.h3), fellow)
    hg = Gather(
        at,
        lambda c: m.hidden.at[c, at.y, own_rows],
        lambda c, yy, rows: m.hidden.at[c, yy, rows],
        (m.hl, m.hr, m.hp),
    )

    def product(c, yy):
        return jnp.dot(m.f_normed[yy], m.wgu[c, side], preferred_element_type=F32) + jnp.dot(
            m.f_tokens[1, yy], m.wgu[c, 1 - side], preferred_element_type=F32
        )

    def first(c):
        for g in range(2):
            kept(c, g).wait()
            given(c, g).wait_recv()
        hs.far(c, product)
        lent(c).start()

    def activate(c):
        both = hs.result(c, own_rows) * m.scale[...]
        gate, up = both[:, :HEAD], both[:, HEAD:]
        m.hidden[c, at.y, own_rows] = (gate / (1.0 + jnp.exp(-gate)) * up).astype(BF)
        hg.line(c)

    def ring(c):
        hg.arrived(c)
        hg.ring(c)

    def add_down(held, k):
        yy = at.yi(k)
        left = jnp.concatenate([m.hidden[c, yy] for c in held], axis=1)
        for j, half in enumerate((side, 1 - side)):
            right = jnp.concatenate([m.wd[c, half] for c in held], axis=0)
            m.acc[j, k] += jnp.dot(left, right, preferred_element_type=F32)

    def by_pairs(c, blocks):
        @pl.when(lax.rem(c, 2) == 1)
        def _():
            for k in blocks:
                add_down((c - 1, c), k)

        if chunks % 2:

            @pl.when(c == chunks - 1)
            def _():
                for k in blocks:
                    add_down((c,), k)

    def down_near(c):
        down(c).wait()
        lent(c).wait_recv()
        by_pairs(c, (0, 1, 3))

    def down_far(c):
        hg.finish(c)
        by_pairs(c, (2,))

    def row_scale():
        m.scale[...] = jnp.broadcast_to(squares.scale(2 * ROWS, team * 2 * ROWS), m.scale.shape)

    def both_sums():
        sets = (
            (m.g_part, m.g_pair, m.g_total, m.g_first, m.g_second, m.cx),
            (m.f_part, m.f_pair, m.f_total, m.f_first, m.f_second, m.bx),
        )
        return [[Scatter(at, *refs[:5], h, refs[5]) for h in range(2)] for refs in sets]

    def hand_over(blocks, late):
        for j, part, pieces in zip((1, 0), (m.g_part, m.f_part), both_sums()):
            for k in blocks:
                part[at.yi(k)] = m.acc[j, k].astype(BF)
            for piece in pieces:
                piece.start(late)

    once = (
        (squares.middle, 2),
        (row_scale, 4),
        (lambda: hand_over((0, 1, 3), False), chunks + 7),
    )
    stages = (
        (first, 0),
        (lambda c: hs.near(c, product), 2),
        (lambda c: hs.own(c, product), 3),
        (activate, 4),
        (ring, 5),
        (hg.hand_on, 6),
        (down_near, 7),
        (down_far, 8),
    )

    def turn(i, carry):
        for step, when in once:
            pl.when(i == when)(step)
        for stage, lag in stages:
            c = i - lag

            @pl.when((c >= 0) & (c < chunks))
            def _():
                stage(c)

        return carry

    lax.fori_loop(0, chunks + stages[-1][1], turn, 0)
    others, owns = both_sums()
    hand_over((2,), True)
    for piece in others:
        piece.step_one()
    for piece in owns:
        piece.step_one()

    def drain_chunk(c, carry):
        hs.drain(c)
        hg.drain(c)
        for g in range(2):
            given(c, g).wait_send()
        lent(c).wait_send()
        return carry

    drain()
    for copy in swaps + trades:
        copy.wait_send()
    for piece in near + away + scatter_a:
        for copy in piece.copies():
            copy.wait_send()
    squares.drain()
    lax.fori_loop(0, chunks, drain_chunk, 0)
    for piece in others:
        piece.step_two()
    for piece in owns:
        piece.step_two()
    backs = [send(m.back_out.at[h], m.back_in.at[h], m.back, h, partner) for h in range(2)]
    for h in range(2):
        m.back_out[h] = others[h].result().astype(BF)
        backs[h].start()
    for h in range(2):
        value = m.f_tokens[(0, *own[h])].astype(F32) + owns[h].result()
        backs[h].wait_recv()
        m.out[h] = (value + m.back_in[h].astype(F32)).astype(BF)

    for copy in backs:
        copy.wait_send()
    for piece in others + owns:
        for copy in piece.copies():
            copy.wait_send()


def reduce_scratch(name, chunks, columns, slots, rows):
    return {
        name + "_part": pltpu.VMEM((chunks, RING, GROUP, columns), BF),
        name + "_one": pltpu.VMEM((chunks, 2, GROUP // 2, columns), BF),
        name + "_two": pltpu.VMEM((chunks, 2, GROUP, columns), BF),
        name + "_three": pltpu.VMEM((chunks, slots, rows, columns), BF),
    }


def square_scratch(name):
    return {
        name + "_part": pltpu.VMEM((RING, 8, GROUP), F32),
        name + "_near": pltpu.VMEM((3, 8, GROUP), F32),
        name + "_mid": pltpu.VMEM((8, GROUP), F32),
        name + "_far": pltpu.VMEM((3, 8, GROUP), F32),
    }


def scatter_scratch(name, columns):
    return {
        name + "_part": pltpu.VMEM((RING, GROUP, columns), BF),
        name + "_pair": pltpu.VMEM((2, GROUP, columns), BF),
        name + "_total": pltpu.VMEM((2, GROUP, columns), BF),
        name + "_first": pltpu.VMEM((2, 2, ROWS // 2, columns), BF),
        name + "_second": pltpu.VMEM((2, 2, ROWS, columns), BF),
    }


def scratch(cols, heads, chunks, q_chunks):
    wide = 2 * HEAD
    buffers = {
        "gain_attn": pltpu.VMEM((1, cols), BF),
        "gain_ffn": pltpu.VMEM((1, cols), BF),
        "table": pltpu.VMEM((2, ROWS + RING * RING, HEAD), F32),
        "tokens": pltpu.VMEM((RING, GROUP, cols), BF),
        "normed": pltpu.VMEM((RING, GROUP, cols), BF),
        "wq": pltpu.VMEM((cols, heads), BF),
        "wkv": pltpu.VMEM((cols, HEAD), BF),
        "wo": pltpu.VMEM((heads, cols), BF),
        **reduce_scratch("q", q_chunks, heads // q_chunks, 3, ROWS),
        "k_part": pltpu.VMEM((RING, GROUP, HEAD), BF),
        "k_near": pltpu.VMEM((3, GROUP, HEAD), BF),
        "k_far": pltpu.VMEM((3, ROWS, HEAD), BF),
        **square_scratch("ss"),
        "keys": pltpu.VMEM((2, RING, GROUP, HEAD), BF),
        "mixed": pltpu.VMEM((RING, GROUP, heads), BF),
        "scores": pltpu.VMEM((RING, RING * ROWS, GROUP), F32),
        **scatter_scratch("a", cols),
        "f_gained": pltpu.VMEM((2, ROWS, cols), BF),
        "f_tokens": pltpu.VMEM((2, RING, GROUP, cols), BF),
        "f_normed": pltpu.VMEM((RING, GROUP, cols), BF),
        "wgu": pltpu.VMEM((chunks, 2, cols, wide), BF),
        "wd": pltpu.VMEM((chunks, 2, HEAD, cols), BF),
        **reduce_scratch("h", chunks, wide, 1, 2 * ROWS),
        **square_scratch("fs"),
        "scale": pltpu.VMEM((2 * ROWS, wide), F32),
        "hidden": pltpu.VMEM((chunks, RING, GROUP, HEAD), BF),
        "acc": pltpu.VMEM((2, RING, GROUP, cols), F32),
        **scatter_scratch("f", cols),
        **scatter_scratch("g", cols),
        "back_out": pltpu.VMEM((2, ROWS, cols), BF),
        "back_in": pltpu.VMEM((2, ROWS, cols), BF),
    }
    single = {"local": (6,), "keep": (chunks, 2), "down": (chunks,)}
    double = {
        "give": (chunks, 2), "lend": (chunks,), "back": (2,), "cx": (2, 8), "swap": (2,), "trade": (2,),
        "gx": (2, 8), "fx": (2, 8), "gz": (2, 8), "ax": (2, 8), "bx": (2, 8),
        "ssy": (3,), "ssz": (3,), "fsy": (3,), "fsz": (3,),
        "q1": (q_chunks, 2), "q2": (q_chunks, 2), "q3": (q_chunks, 3),
        "k1": (3,), "k2": (3,), "kl": (3,), "kr": (3,), "kc": (4,),
        "ml": (3,), "mr": (RING, 2), "mp": (RING, 2),
        "h1": (chunks, 2), "h2": (chunks, 2), "h3": (chunks, 1),
        "hl": (chunks,), "hr": (chunks, 2), "hp": (chunks, 2),
    }
    for name, shape in single.items():
        buffers[name] = pltpu.SemaphoreType.DMA(shape)
    for name, shape in double.items():
        buffers[name + "_s"] = pltpu.SemaphoreType.DMA(shape)
        buffers[name + "_r"] = pltpu.SemaphoreType.DMA(shape)
    return buffers


def rotary_table(count):
    freq = np.exp(-(2.0 * np.arange(HEAD // 2) / HEAD) * math.log(THETA))
    position = np.concatenate([np.arange(ROWS), np.arange(count) * ROWS]).astype(np.float64)
    angle = position[:, None] * np.concatenate([freq, freq])[None, :]
    return np.stack([np.cos(angle), np.sin(angle)]).astype(np.float32)


def local_layer(
    section_input, gain_attn, w_query, key_value_weight, w_output, gain_ffn, w_gate_up, w_down
):
    cols = section_input.shape[2]
    heads = w_query.shape[2]
    chunks = w_gate_up.shape[3] // (2 * HEAD)
    anywhere = pl.BlockSpec(memory_space=pl.ANY)
    vmem = pl.BlockSpec(memory_space=pltpu.VMEM)
    inputs = {
        "src": (section_input.reshape(2, ROWS, cols), anywhere),
        "gain_attn_hbm": (gain_attn, anywhere),
        "wq_hbm": (w_query[0], anywhere),
        "wkv_hbm": (key_value_weight[0], anywhere),
        "wo_hbm": (w_output[0], anywhere),
        "gain_ffn_hbm": (gain_ffn, anywhere),
        "wgu_hbm": (w_gate_up[0], anywhere),
        "wd_hbm": (w_down[0], anywhere),
        "table_hbm": (jnp.asarray(rotary_table(RING * RING)), anywhere),
    }
    buffers = scratch(cols, heads, chunks, 2)
    result = pl.pallas_call(
        functools.partial(kernel, (*inputs, "out", *buffers)),
        name="layer",
        out_shape=jax.ShapeDtypeStruct((2, ROWS, cols), BF),
        in_specs=[spec for _, spec in inputs.values()],
        out_specs=vmem,
        scratch_shapes=list(buffers.values()),
        compiler_params=pltpu.CompilerParams(
            collective_id=0, has_side_effects=True, vmem_limit_bytes=60 * 1024 * 1024
        ),
    )(*[array for array, _ in inputs.values()])
    return result.reshape(1, 2 * ROWS, cols)


def solution(mesh):
    placed = (
        P("section", "tensor", "dp"),
        P("section", "dp"),
        P("section", "dp", "tensor"),
        P("section", None, "dp", None),
        P("section", "tensor", "dp"),
        P("section", "dp"),
        P("section", None, "dp", "tensor"),
        P("section", "tensor", "dp"),
    )
    return jax.shard_map(
        local_layer, mesh=mesh, in_specs=placed, out_specs=P("section", "tensor", "dp"), check_vma=False
    )
```
